32 devices in a mesh: dp: 8 (over y, x, core), tensor: 4 (over z).
Axes of the slice: x: 2, y: 2, z: 4, core: 2. Of those that a mesh axis runs over, the one named last changes fastest.
Arguments:
- x_prompt: bfloat16 [8192, 768], P('dp'), may hold values from -6 to 6
- x_cont: bfloat16 [4096, 768], P('dp'), may hold values from -6 to 6
- enc_out: bfloat16 [4096, 768], P('dp'), may hold values from -6 to 6
- cot_prompt: bfloat16 [8192, 768], P(('dp', 'tensor')), may hold values from -6 to 6
- cot_cont: bfloat16 [4096, 768], P(('dp', 'tensor')), may hold values from -6 to 6
- teacher: bfloat16 [4096, 768], P(('dp', 'tensor')), may hold values from -6 to 6
- valid: int32 [4096], P('dp'), may hold values from 0 to 1, as said below
- prompt_of: int32 [32], P('dp'), may hold values from 0 to 7, as said below
- buckets: int32 [1152], replicated, may hold values from 0 to 31
- gain_self: float32 [768], replicated, may hold values from 0.5 to 1.5
- gain_cross: float32 [768], replicated, may hold values from 0.5 to 1.5
- gain_ffn: float32 [768], replicated, may hold values from 0.5 to 1.5
- rel_table: float32 [32, 12], P(None, 'tensor'), may hold values from -6 to 6
- w_q: bfloat16 [768, 768], P(None, 'tensor'), may hold values from -0.21875 to 0.21875
- w_k: bfloat16 [768, 768], P(None, 'tensor'), may hold values from -0.21875 to 0.21875
- w_v: bfloat16 [768, 768], P(None, 'tensor'), may hold values from -0.21875 to 0.21875
- w_o: bfloat16 [768, 768], P('tensor'), may hold values from -0.875 to 0.875
- c_q: bfloat16 [768, 768], P(None, 'tensor'), may hold values from -0.21875 to 0.21875
- c_k: bfloat16 [768, 768], P(None, 'tensor'), may hold values from -0.21875 to 0.21875
- c_v: bfloat16 [768, 768], P(None, 'tensor'), may hold values from -0.21875 to 0.21875
- c_o: bfloat16 [768, 768], P('tensor'), may hold values from -0.875 to 0.875
- w_gate: bfloat16 [768, 2048], P(None, 'tensor'), may hold values from -0.21875 to 0.21875
- w_up: bfloat16 [768, 2048], P(None, 'tensor'), may hold values from -0.21875 to 0.21875
- w_down: bfloat16 [2048, 768], P('tensor'), may hold values from -0.125 to 0.125
Outputs:
- y_prompt: bfloat16 [8192, 768], P(('dp', 'tensor'))
- y_cont: bfloat16 [4096, 768], P(('dp', 'tensor'))
- grad_x_prompt: float32 [8192, 768], P(('dp', 'tensor'))
- grad_x_cont: float32 [4096, 768], P(('dp', 'tensor'))
- grad_enc: float32 [4096, 768], P('dp')
- grad_gain_self: float32 [768], replicated
- grad_gain_cross: float32 [768], replicated
- grad_gain_ffn: float32 [768], replicated
- grad_rel_table: float32 [32, 12], P(None, 'tensor')
- grad_w_q: float32 [768, 768], P(None, 'tensor')
- grad_w_k: float32 [768, 768], P(None, 'tensor')
- grad_w_v: float32 [768, 768], P(None, 'tensor')
- grad_w_o: float32 [768, 768], P('tensor')
- grad_c_q: float32 [768, 768], P(None, 'tensor')
- grad_c_k: float32 [768, 768], P(None, 'tensor')
- grad_c_v: float32 [768, 768], P(None, 'tensor')
- grad_c_o: float32 [768, 768], P('tensor')
- grad_w_gate: float32 [768, 2048], P(None, 'tensor')
- grad_w_up: float32 [768, 2048], P(None, 'tensor')
- grad_w_down: float32 [2048, 768], P('tensor')
- loss: float32 [], replicated
The draws below stay inside these ranges and needn't reach their ends.
Inputs may be any that keep to these rules, and one draw needn't show every extreme that they name: The valid tokens of each continuation are a prefix of it, of 1 to 128 tokens. `prompt_of`: in the k-th aligned block of 4 entries (the continuations of group k), two entries name group k and two name group k xor 1.
All inputs are finite; a program needn't handle non-finite values.
Results may differ from the reference program's by a relative error of at most 0.023.
Values may be sent and summed in bfloat16 or wider, within the bound.
A program may use at most 192 MiB of HBM per device.

```python
import jax
import jax.numpy as jnp
from jax import lax

D = 768
HEADS = 12
HEAD = 64
FF = 2048
NB = 32
PROMPT = 1024
CONTS = 4
CONT_LEN = 128
ENC_LEN = 512
GRP_DEV = 1
GROUPS = 8
DIST = 1152


def draw_prompt_of(key, part):
    blocks = GROUPS // GRP_DEV
    per_block = GRP_DEV * CONTS
    slot_ids = jnp.arange(per_block, dtype=jnp.int32)
    far_side = (slot_ids < per_block // 2).astype(jnp.int32)
    inside = slot_ids % GRP_DEV
    subkeys = jax.random.split(key, blocks)
    shuffles = jax.vmap(lambda subkey: jax.random.permutation(subkey, per_block))(subkeys)
    block_ids = jnp.arange(blocks, dtype=jnp.int32)[:, None]
    target_block = jnp.bitwise_xor(block_ids, far_side[shuffles])
    return (target_block * GRP_DEV + inside[shuffles]).reshape(-1).astype(jnp.int32)


def draw_valid(key, part):
    conts_all = GROUPS * CONTS
    group_ids = jnp.arange(conts_all, dtype=jnp.int32) // CONTS
    spread = max(GROUPS - 1, 1)
    lowest = CONT_LEN // 4 + 3 * CONT_LEN // 4 * group_ids // spread
    jitter = jax.random.randint(key, (conts_all,), 0, CONT_LEN // 8 + 1, dtype=jnp.int32)
    lengths = jnp.minimum(lowest + jitter, CONT_LEN)
    position = jnp.arange(CONT_LEN, dtype=jnp.int32)
    return (position[None, :] < lengths[:, None]).astype(jnp.int32).reshape(-1)


def set_ends(result, key, low, high):
    longest = result.shape.index(max(result.shape))
    spots = []
    for shift in (0, 1):
        where = [jax.random.randint(jax.random.fold_in(key, axis), (), 0, length) for axis, length in enumerate(result.shape)]
        where[longest] = (where[longest] + shift) % result.shape[longest]
        spots.append(tuple(where))
    return result.at[spots[0]].set(low).at[spots[1]].set(high)


def block_scale(own_key, shape, shards, low, largest):
    gain, own = 1.0, jax.random.fold_in(own_key, 6)
    for dim, blocks in shards:
        steps = jnp.exp(jax.random.uniform(jax.random.fold_in(own, dim), (blocks,), jnp.float32, low / len(shards), largest / len(shards)))
        gain = gain * jnp.repeat(steps, shape[dim] // blocks).reshape([-1 if axis == dim else 1 for axis in range(len(shape))])
    return gain


def centred(rng, shape, width, bound, pieces=(), kind=jnp.bfloat16):
    result = jax.random.normal(rng, shape, jnp.float32) * width
    if len(pieces) > 0:
        result = block_scale(rng, shape, pieces, -0.22, 0.18) * result
    return jnp.clip(result, min=-bound, max=bound).astype(kind)


def setup_inputs(seed: int = 0) -> dict:
    key_list = jax.random.split(jax.random.key(seed), 25)
    return {
        "x_prompt": centred(key_list[0], (GROUPS * PROMPT, D), 1.0, 6.0, ((0, 8),)),
        "x_cont": centred(key_list[1], (GROUPS * CONTS * CONT_LEN, D), 1.0, 6.0, ((0, 8),)),
        "enc_out": centred(key_list[2], (GROUPS * ENC_LEN, D), 1.0, 6.0, ((0, 8),)),
        "cot_prompt": centred(key_list[3], (GROUPS * PROMPT, D), 1.0, 6.0, ((0, 32),)),
        "cot_cont": centred(key_list[4], (GROUPS * CONTS * CONT_LEN, D), 1.0, 6.0, ((0, 32),)),
        "teacher": centred(key_list[5], (GROUPS * CONTS * CONT_LEN, D), 1.0, 6.0, ((0, 32),)),
        "valid": draw_valid(jax.random.fold_in(key_list[24], 71), 0),
        "prompt_of": draw_prompt_of(jax.random.fold_in(key_list[24], 71), 0),
        "buckets": set_ends(jax.random.randint(key_list[8], (DIST,), 0, NB), jax.random.fold_in(key_list[8], 1), 0, NB - 1).astype(jnp.int32),
        "gain_self": jnp.clip(1.0 + 0.1 * jax.random.normal(key_list[9], (D,), jnp.float32), 0.5, 1.5),
        "gain_cross": jnp.clip(1.0 + 0.1 * jax.random.normal(key_list[10], (D,), jnp.float32), 0.5, 1.5),
        "gain_ffn": jnp.clip(1.0 + 0.1 * jax.random.normal(key_list[11], (D,), jnp.float32), 0.5, 1.5),
        "rel_table": centred(key_list[12], (NB, HEADS), 1.0, 6.0, ((1, 4),), jnp.float32),
        "w_q": centred(key_list[13], (D, HEADS * HEAD), D ** -0.5, 0.21875, ((1, 4),)),
        "w_k": centred(key_list[14], (D, HEADS * HEAD), D ** -0.5, 0.21875, ((1, 4),)),
        "w_v": centred(key_list[15], (D, HEADS * HEAD), D ** -0.5, 0.21875, ((1, 4),)),
        "w_o": centred(key_list[16], (HEADS * HEAD, D), (HEADS * HEAD // 16) ** -0.5, 0.875, ((0, 4),)),
        "c_q": centred(key_list[17], (D, HEADS * HEAD), D ** -0.5, 0.21875, ((1, 4),)),
        "c_k": centred(key_list[18], (D, HEADS * HEAD), D ** -0.5, 0.21875, ((1, 4),)),
        "c_v": centred(key_list[19], (D, HEADS * HEAD), D ** -0.5, 0.21875, ((1, 4),)),
        "c_o": centred(key_list[20], (HEADS * HEAD, D), (HEADS * HEAD // 16) ** -0.5, 0.875, ((0, 4),)),
        "w_gate": centred(key_list[21], (D, FF), D ** -0.5, 0.21875, ((1, 4),)),
        "w_up": centred(key_list[22], (D, FF), D ** -0.5, 0.21875, ((1, 4),)),
        "w_down": centred(key_list[23], (FF, D), FF ** -0.5, 0.125, ((0, 4),)),
    }


@jax.custom_vjp
def low(v):
    return lax.optimization_barrier(v.astype(jnp.bfloat16)).astype(jnp.float32)

@jax.custom_vjp
def low_back(v):
    return v

def low_keep(v):
    return (low(v), None)

def low_pass(kept, grad):
    return (grad,)

def back_keep(v):
    return (v, None)

def back_low(kept, grad):
    return (low(grad),)
low.defvjp(low_keep, low_pass)
low_back.defvjp(back_keep, back_low)
norm_eps = 1e-06
masked_value = -1e+30

def matmul(left_in, right_in):
    return jnp.dot(left_in, right_in, precision=lax.Precision.HIGHEST)

def rounded(values):
    return low(low_back(values))

def rms_norm(values, weight):
    return values * lax.rsqrt(lax.optimization_barrier(jnp.mean(values * values, axis=-1, keepdims=True)) + norm_eps) * weight

def attention(queries, keys_in, values_in, pos_bias, allowed):
    scores = jnp.einsum('rhe,khe->hrk', queries, keys_in, precision=lax.Precision.HIGHEST) * HEAD ** (-0.5)
    if pos_bias is not None:
        scores = scores + pos_bias
    if allowed is not None:
        scores = jnp.where(allowed[None], scores, masked_value)
    scores = low_back(scores)
    topmost = lax.optimization_barrier(jnp.max(scores, axis=-1, keepdims=True))
    expsum = jnp.exp(scores - topmost)
    probabilities = low(expsum / lax.optimization_barrier(jnp.sum(expsum, axis=-1, keepdims=True)))
    return jnp.einsum('hrk,khe->rhe', probabilities, values_in, precision=lax.Precision.HIGHEST)

def reference(x_prompt, x_cont, enc_out, cot_prompt, cot_cont, teacher, valid, prompt_of, buckets, gain_self, gain_cross, gain_ffn, rel_table, w_q, w_k, w_v, w_o, c_q, c_k, c_v, c_o, w_gate, w_up, w_down):
    prompt_rows = GROUPS * PROMPT
    cont_count = GROUPS * CONTS
    dist_count = PROMPT + CONT_LEN
    valid_f = valid.astype(jnp.float32)
    token_count = jnp.sum(valid_f)
    teacher_f = teacher.astype(jnp.float32)
    prompt_dist = jnp.arange(PROMPT)[:, None] - jnp.arange(PROMPT)[None, :]
    prompt_ok = prompt_dist >= 0
    cont_dist = PROMPT + jnp.arange(CONT_LEN)[:, None] - jnp.arange(dist_count)[None, :]
    cont_base = cont_dist >= 0
    valid_rows = valid.reshape(cont_count, CONT_LEN) > 0
    key_ok = jnp.concatenate([jnp.ones((cont_count, PROMPT), jnp.bool_), valid_rows], axis=1)

    def to_prompt(values):
        return values[:prompt_rows].reshape(GROUPS, PROMPT, HEADS, HEAD)

    def to_cont(values):
        return values[prompt_rows:].reshape(cont_count, CONT_LEN, HEADS, HEAD)

    def forward(prompt_in, cont_in, encoded, norm_self, norm_cross, norm_ffn, bias_in, w_query, w_key, w_value, w_out, x_query, x_key, x_value, x_out, w_gate_in, w_up_in, w_down_in):
        stream = jnp.concatenate([prompt_in, cont_in])
        bias_dist = jnp.take(bias_in, buckets, axis=0).T
        prompt_bias = jnp.take(bias_dist, jnp.clip(prompt_dist, 0, dist_count - 1), axis=1)
        cont_bias = jnp.take(bias_dist, jnp.clip(cont_dist, 0, dist_count - 1), axis=1)
        normed_one = low(rms_norm(stream, norm_self))
        queries = rounded(matmul(normed_one, w_query))
        keys_all = rounded(matmul(normed_one, w_key))
        values_all = rounded(matmul(normed_one, w_value))
        prompt_keys = to_prompt(keys_all)
        prompt_values = to_prompt(values_all)

        def prompt_block(operands):
            return attention(operands[0], operands[1], operands[2], prompt_bias, prompt_ok)

        def cont_block(operands):
            cont_q, own_k, own_v, index, ok_keys = operands
            keys_in = jnp.concatenate([prompt_keys[index], own_k])
            values_in = jnp.concatenate([prompt_values[index], own_v])
            return attention(cont_q, keys_in, values_in, cont_bias, cont_base & ok_keys[None, :])
        mixed_prompt = lax.map(jax.checkpoint(prompt_block), (to_prompt(queries), prompt_keys, prompt_values))
        mixed_cont = lax.map(jax.checkpoint(cont_block), (to_cont(queries), to_cont(keys_all), to_cont(values_all), prompt_of, key_ok))
        mixed_one = rounded(jnp.concatenate([mixed_prompt.reshape(prompt_rows, -1), mixed_cont.reshape(cont_count * CONT_LEN, -1)]))
        after_self = stream + low_back(matmul(mixed_one, w_out))
        normed_two = low(rms_norm(after_self, norm_cross))
        cross_q = rounded(matmul(normed_two, x_query))
        cross_k = rounded(matmul(encoded, x_key)).reshape(GROUPS, ENC_LEN, HEADS, HEAD)
        cross_v = rounded(matmul(encoded, x_value)).reshape(GROUPS, ENC_LEN, HEADS, HEAD)

        def cross_prompt(operands):
            return attention(operands[0], operands[1], operands[2], None, None)

        def cross_cont(operands):
            return attention(operands[0], cross_k[operands[1]], cross_v[operands[1]], None, None)
        cross_p = lax.map(jax.checkpoint(cross_prompt), (to_prompt(cross_q), cross_k, cross_v))
        cross_c = lax.map(jax.checkpoint(cross_cont), (to_cont(cross_q), prompt_of))
        mixed_two = rounded(jnp.concatenate([cross_p.reshape(prompt_rows, -1), cross_c.reshape(cont_count * CONT_LEN, -1)]))
        after_cross = after_self + low_back(matmul(mixed_two, x_out))
        normed_three = low(rms_norm(after_cross, norm_ffn))
        gate_pre = low_back(matmul(normed_three, w_gate_in))
        upper = low_back(matmul(normed_three, w_up_in))
        hidden = rounded(jax.nn.gelu(gate_pre, approximate=True) * upper)
        layer_out = after_cross + low_back(matmul(hidden, w_down_in))
        deviation = layer_out[prompt_rows:] - teacher_f
        loss_value = jnp.sum(valid_f[:, None] * deviation * deviation) / token_count
        return (layer_out, loss_value)
    primals = (x_prompt.astype(jnp.float32), x_cont.astype(jnp.float32), enc_out.astype(jnp.float32), gain_self, gain_cross, gain_ffn, rel_table, w_q.astype(jnp.float32), w_k.astype(jnp.float32), w_v.astype(jnp.float32), w_o.astype(jnp.float32), c_q.astype(jnp.float32), c_k.astype(jnp.float32), c_v.astype(jnp.float32), c_o.astype(jnp.float32), w_gate.astype(jnp.float32), w_up.astype(jnp.float32), w_down.astype(jnp.float32))
    (layer_out, loss_value), pull = jax.vjp(forward, *primals)
    cotangent = jnp.concatenate([cot_prompt, cot_cont]).astype(jnp.float32)
    grads = pull((cotangent, jnp.ones_like(loss_value)))
    return (layer_out[:prompt_rows].astype(jnp.bfloat16), layer_out[prompt_rows:].astype(jnp.bfloat16), grads[0], grads[1], grads[2], grads[3], grads[4], grads[5], grads[6], grads[7], grads[8], grads[9], grads[10], grads[11], grads[12], grads[13], grads[14], grads[15], grads[16], grads[17], loss_value)
```

```python
import functools

import jax
import jax.numpy as jnp
from jax import lax
from jax.experimental import pallas as pl
from jax.experimental.pallas import tpu as pltpu
from jax.sharding import PartitionSpec as P

HEAD = 64
PROMPT = 1024
CONT_LEN = 128
ENC_LEN = 512
TILE = 128
DIST = PROMPT + CONT_LEN
LINE = DIST + 2 * TILE
SLAB = DIST + TILE

norm_eps = 1e-06
masked_value = -1e30
BF = jnp.bfloat16
F32 = jnp.float32
NT = (((1,), (1,)), ((), ()))
TN = (((0,), (0,)), ((), ()))
NN = (((1,), (0,)), ((), ()))


def mm(left, right, dims=NN):
    return lax.dot_general(left, right, dims, preferred_element_type=F32)


def from_ahead(block, step):
    count = lax.axis_size("tensor")
    return lax.ppermute(block, "tensor", [((i + step) % count, i) for i in range(count)])


def to_ahead(block, step):
    count = lax.axis_size("tensor")
    return lax.ppermute(block, "tensor", [(i, (i + step) % count) for i in range(count)])


def flip_bit(block, bit, axis="dp"):
    count = lax.axis_size(axis)
    return lax.ppermute(block, axis, [(i, i ^ (1 << bit)) for i in range(count)])


def bit_lists():
    count = lax.axis_size("dp")
    bits = count.bit_length() - 1
    up = list(range(1, bits))
    return (up, up[::-1])


def slice_order(bits):
    order = [0]
    for bit in bits + [0]:
        order = order + [entry ^ (1 << bit) for entry in order]
    return order


def spread(block, bits, axis):
    for bit in bits:
        block = jnp.concatenate([block, flip_bit(block, bit)], axis=axis)
    return block


def gather_weights(own):
    up, down = bit_lists()
    pieces = [own] + [from_ahead(own, step) for step in range(1, 4)]
    first = spread(jnp.concatenate(pieces[:2], axis=1), up, 3)
    second = spread(jnp.concatenate(pieces[2:], axis=1), down, 3)
    first_far = flip_bit(first, 0)
    second_far = flip_bit(second, 0)
    return jnp.concatenate(
        [
            jnp.concatenate([first, first_far], axis=3),
            jnp.concatenate([second, second_far], axis=3),
        ],
        axis=1,
    )


def fold(block, bit, axis):
    half = block.shape[axis] // 2
    low = lax.slice_in_dim(block, 0, half, axis=axis)
    high = lax.slice_in_dim(block, half, 2 * half, axis=axis)
    return (low.astype(F32) + flip_bit(high, bit).astype(F32)).astype(BF)


def reduce_grads(grads):
    up, down = bit_lists()
    first, second = grads[:, :2], grads[:, 2:]
    for bit in [0] + down:
        first = fold(first, bit, 3)
    for bit in [0] + up:
        second = fold(second, bit, 3)
    total = first[:, 0].astype(F32)
    for step, piece in ((1, first[:, 1]), (2, second[:, 0]), (3, second[:, 1])):
        total = total + to_ahead(piece, step).astype(F32)
    total = total.astype(BF)
    half = total.shape[-1] // 2
    left = spread(total[..., :half], up + [0], 2)
    right = spread(total[..., half:], down + [0], 2)
    return (left, right)


def slice_hot(order, parts, rows, rank):
    count = len(order)
    size = parts * count * rows
    place = jnp.arange(size)
    slot = place // rows % count
    table = sum(jnp.where(slot == index, entry, 0) for index, entry in enumerate(order))
    natural = place // (count * rows) * (count * rows) + (rank ^ table) * rows + place % rows
    return (natural[:, None] == jnp.arange(size)[None, :]).astype(BF)


def norm_scale(values):
    return lax.rsqrt(jnp.mean(values * values, axis=-1, keepdims=True) + norm_eps)


def rms_norm(values, weight):
    return values * norm_scale(values) * weight


def norm_back(values, weight, grad):
    scale = norm_scale(values)
    unit = values * scale
    weighted = grad * weight
    inner = jnp.mean(weighted * unit, axis=-1, keepdims=True)
    return (scale * (weighted - unit * inner), jnp.sum(grad * unit, axis=0))


def make_slab(line):
    wide = jnp.broadcast_to(line, (TILE, LINE))
    return pltpu.roll(wide, LINE - (TILE - 1), 1, stride=1, stride_axis=0)[:, :SLAB]


def head_mask(head, width, dtype):
    lane = lax.broadcasted_iota(jnp.int32, (1, width), 1)
    return (lane // HEAD == head).astype(dtype)


def prompt_fwd(line_ref, q_ref, k_ref, v_ref, o_ref, lse_ref, slab):
    head = pl.program_id(0)
    slab[...] = make_slab(line_ref[0])
    width = q_ref.shape[1]
    mask = head_mask(head, width, BF)
    mask_f = head_mask(head, width, F32)

    @pl.when(head == 0)
    def _():
        o_ref[...] = jnp.zeros_like(o_ref)
        lse_ref[...] = jnp.zeros_like(lse_ref)

    vm = v_ref[0:PROMPT, :] * mask
    block = 2 * TILE
    for idx in range(PROMPT // block):
        keys = block * (idx + 1)
        rows = pl.ds(idx * block, block)
        q = q_ref[rows, :] * mask
        s = mm(q, k_ref[0:keys, :], NT)
        start = PROMPT - block * idx
        s = s + jnp.concatenate(
            [slab[:, start : start + keys], slab[:, start - TILE : start - TILE + keys]], axis=0
        )
        top = jnp.max(s, axis=-1, keepdims=True)
        e = jnp.exp(s - top)
        total = jnp.sum(e, axis=-1, keepdims=True)
        o = mm(e.astype(BF), vm[0:keys, :]) / total
        o_ref[rows, :] = o_ref[rows, :] + o.astype(BF)
        lse_ref[rows, :] = lse_ref[rows, :] + (top + jnp.log(total)) * mask_f


def cont_rows(slot):
    return pl.ds(pl.multiple_of(slot * CONT_LEN, CONT_LEN), CONT_LEN)


def late_rows(slot):
    return pl.ds(pl.multiple_of(PROMPT + slot * CONT_LEN, CONT_LEN), CONT_LEN)


def cont_fwd(
    slot_ref, line_ref, ok_ref, q_ref, k_ref, v_ref, kf_ref, vf_ref, o_ref, lse_ref, slab
):
    head = pl.program_id(0)
    slab[...] = make_slab(line_ref[0])
    width = q_ref.shape[1]
    mask = head_mask(head, width, BF)
    mask_f = head_mask(head, width, F32)

    @pl.when(head == 0)
    def _():
        o_ref[...] = jnp.zeros_like(o_ref)
        lse_ref[...] = jnp.zeros_like(lse_ref)

    for pair in range(2):
        keys_ref, values_ref = (k_ref, v_ref) if pair == 0 else (kf_ref, vf_ref)
        slots = [slot_ref[2 * pair], slot_ref[2 * pair + 1]]
        qs = [q_ref[late_rows(slot), :] * mask for slot in slots]
        s = mm(jnp.concatenate(qs, axis=0), keys_ref[0:PROMPT, :], NT)
        s = s + jnp.concatenate([slab[:, 0:PROMPT], slab[:, 0:PROMPT]], axis=0)
        own = jnp.concatenate(
            [
                mm(q, k_ref[late_rows(slot), :], NT) + slab[:, PROMPT:DIST] + ok_ref[slot]
                for q, slot in zip(qs, slots)
            ],
            axis=0,
        )
        top = jnp.maximum(
            jnp.max(s, axis=-1, keepdims=True), jnp.max(own, axis=-1, keepdims=True)
        )
        e = jnp.exp(s - top)
        e_own = jnp.exp(own - top)
        total = jnp.sum(e, axis=-1, keepdims=True) + jnp.sum(e_own, axis=-1, keepdims=True)
        o = mm(e.astype(BF), values_ref[0:PROMPT, :] * mask)
        low = e_own.astype(BF)
        o_own = [
            mm(low[CONT_LEN * i : CONT_LEN * (i + 1), :], v_ref[late_rows(slot), :] * mask)
            for i, slot in enumerate(slots)
        ]
        o = (o + jnp.concatenate(o_own, axis=0)) / total
        lse = (top + jnp.log(total)) * mask_f
        for i, slot in enumerate(slots):
            part = slice(CONT_LEN * i, CONT_LEN * (i + 1))
            o_ref[cont_rows(slot), :] = o_ref[cont_rows(slot), :] + o[part, :].astype(BF)
            lse_ref[cont_rows(slot), :] = lse_ref[cont_rows(slot), :] + lse[part, :]


def row_of(lse, head):
    width = lse.shape[1]
    lane = lax.broadcasted_iota(jnp.int32, (1, width), 1)
    column = jnp.sum(jnp.where(lane == head * HEAD, lse, 0.0), axis=-1, keepdims=True)
    return jnp.broadcast_to(column, (lse.shape[0], TILE)).T[0:1, :]


def fold_slab(block):
    rows = TILE
    block = jnp.concatenate([block, jnp.zeros((TILE, LINE - SLAB), F32)], axis=1)
    while rows > 8:
        rows //= 2
        block = pltpu.roll(block[:rows], rows, 1) + block[rows:]
    line = jnp.zeros((1, LINE), F32)
    for r in range(rows):
        line = line + pltpu.roll(block, rows - 1 - r, 1)[r : r + 1]
    return line


def prompt_back(
    line_ref, q_ref, k_ref, kt_ref, v_ref, do_ref, lse_ref, dq_ref, dk_ref, dv_ref, gl_ref,
    slab, gslab, dqt,
):
    head = pl.program_id(0)
    slab[...] = make_slab(line_ref[0]).T
    gslab[...] = jnp.zeros_like(gslab)
    width = q_ref.shape[1]
    mask = head_mask(head, width, BF)

    @pl.when(head == 0)
    def _():
        dk_ref[...] = jnp.zeros_like(dk_ref)
        dv_ref[...] = jnp.zeros_like(dv_ref)

    mine = pl.ds(pl.multiple_of(head * HEAD, HEAD), HEAD)
    block = 2 * TILE
    for idx in range(PROMPT // block):
        keys = block * (idx + 1)
        rows = pl.ds(idx * block, block)
        q = q_ref[rows, :] * mask
        do = do_ref[rows, :] * mask
        s = mm(k_ref[0:keys, :], q, NT)
        start = PROMPT - block * idx
        s = s + jnp.concatenate(
            [slab[start : start + keys, :], slab[start - TILE : start - TILE + keys, :]], axis=1
        )
        p = jnp.exp(s - row_of(lse_ref[rows, :], head))
        dp = mm(v_ref[0:keys, :], do, NT)
        centre = jnp.sum(p * dp, axis=0, keepdims=True)
        ds = p * (dp - centre)
        low = ds.astype(BF)
        dv_ref[0:keys, :] = dv_ref[0:keys, :] + mm(p.astype(BF), do)
        dk_ref[0:keys, :] = dk_ref[0:keys, :] + mm(low, q)
        dqt[mine, rows] = mm(kt_ref[mine, 0:keys], low)
        gslab[start : start + keys, :] = gslab[start : start + keys, :] + ds[:, 0:TILE]
        gslab[start - TILE : start - TILE + keys, :] = (
            gslab[start - TILE : start - TILE + keys, :] + ds[:, TILE:block]
        )
    gl_ref[0] = fold_slab(gslab[...].T)

    @pl.when(head == pl.num_programs(0) - 1)
    def _():
        dq_ref[...] = (dqt[...].T * HEAD ** (-0.5)).astype(BF)


def cont_back(
    slot_ref, line_ref, ok_ref, q_ref, k_ref, kt_ref, v_ref, kf_ref, ktf_ref, vf_ref, do_ref,
    lse_ref, dq_ref, dkc_ref, dvc_ref, dk_ref, dv_ref, dkf_ref, dvf_ref, gl_ref,
    slab, gslab, dqt, dkc, dvc, dkf, dvf,
):
    head = pl.program_id(0)
    slab[...] = make_slab(line_ref[0]).T
    gslab[...] = jnp.zeros_like(gslab)
    width = q_ref.shape[1]
    mask = head_mask(head, width, BF)

    @pl.when(head == 0)
    def _():
        for ref in (dk_ref, dv_ref, dkf, dvf, dkc, dvc):
            ref[...] = jnp.zeros_like(ref)

    mine = pl.ds(pl.multiple_of(head * HEAD, HEAD), HEAD)
    for pair in range(2):
        keys_ref, kt, values_ref = (
            (k_ref, kt_ref, v_ref) if pair == 0 else (kf_ref, ktf_ref, vf_ref)
        )
        gk, gv = (dk_ref, dv_ref) if pair == 0 else (dkf, dvf)
        slots = [slot_ref[2 * pair], slot_ref[2 * pair + 1]]
        qs = [q_ref[late_rows(slot), :] * mask for slot in slots]
        dos = [do_ref[cont_rows(slot), :] * mask for slot in slots]
        q = jnp.concatenate(qs, axis=0)
        do = jnp.concatenate(dos, axis=0)
        lse = row_of(
            jnp.concatenate([lse_ref[cont_rows(slot), :] for slot in slots], axis=0), head
        )
        s = mm(keys_ref[0:PROMPT, :], q, NT)
        s = s + jnp.concatenate([slab[0:PROMPT, :], slab[0:PROMPT, :]], axis=1)
        own = jnp.concatenate(
            [
                mm(k_ref[late_rows(slot), :], qc, NT) + slab[PROMPT:DIST, :] + ok_ref[slot]
                for qc, slot in zip(qs, slots)
            ],
            axis=1,
        )
        p = jnp.exp(s - lse)
        p_own = jnp.exp(own - lse)
        dp = mm(values_ref[0:PROMPT, :], do, NT)
        dp_own = jnp.concatenate(
            [mm(v_ref[late_rows(slot), :], doc, NT) for doc, slot in zip(dos, slots)], axis=1
        )
        centre = jnp.sum(p * dp, axis=0, keepdims=True) + jnp.sum(
            p_own * dp_own, axis=0, keepdims=True
        )
        ds = p * (dp - centre)
        ds_own = p_own * (dp_own - centre)
        low = ds.astype(BF)
        low_own = ds_own.astype(BF)
        p_low = p_own.astype(BF)
        gv[...] = gv[...] + mm(p.astype(BF), do)
        gk[...] = gk[...] + mm(low, q)
        dq = mm(kt[mine, 0:PROMPT], low)
        for i, slot in enumerate(slots):
            part = slice(CONT_LEN * i, CONT_LEN * (i + 1))
            here = cont_rows(slot)
            dvc[here, :] = dvc[here, :] + mm(p_low[:, part], dos[i])
            dkc[here, :] = dkc[here, :] + mm(low_own[:, part], qs[i])
            kown = k_ref[late_rows(slot), :].T
            head_keys = kown[0:HEAD, :]
            for other in range(1, width // HEAD):
                head_keys = jnp.where(
                    head == other, kown[HEAD * other : HEAD * (other + 1), :], head_keys
                )
            dqt[slot, mine, :] = dq[:, part] + mm(head_keys, low_own[:, part])
            gslab[0:PROMPT, :] = gslab[0:PROMPT, :] + ds[:, part]
            gslab[PROMPT:DIST, :] = gslab[PROMPT:DIST, :] + ds_own[:, part]
    gl_ref[0] = fold_slab(gslab[...].T)

    @pl.when(head == pl.num_programs(0) - 1)
    def _():
        for slot in range(dqt.shape[0]):
            dq_ref[slot * CONT_LEN : (slot + 1) * CONT_LEN, :] = (
                dqt[slot].T * HEAD ** (-0.5)
            ).astype(BF)
        dkf_ref[...] = dkf[...].astype(BF)
        dvf_ref[...] = dvf[...].astype(BF)
        dkc_ref[...] = dkc[...].astype(BF)
        dvc_ref[...] = dvc[...].astype(BF)


def cross_fwd(far_ref, q_ref, k_ref, v_ref, o_ref, lse_ref):
    rows = q_ref.shape[0] - CONT_LEN
    far = pl.ds(pl.multiple_of(far_ref[0] * ENC_LEN, ENC_LEN), ENC_LEN)
    for part, keys in ((pl.ds(0, rows), pl.ds(0, ENC_LEN)), (pl.ds(rows, CONT_LEN), far)):
        q = q_ref[part, :]
        k = k_ref[keys, :]
        v = v_ref[keys, :]
        o = 0.0
        lse = 0.0
        for head in range(2):
            mask = head_mask(head, TILE, BF)
            s = mm(q * mask, k, NT)
            top = jnp.max(s, axis=-1, keepdims=True)
            e = jnp.exp(s - top)
            total = jnp.sum(e, axis=-1, keepdims=True)
            o = o + mm(e.astype(BF), v * mask) / total
            lse = lse + (top + jnp.log(total)) * head_mask(head, TILE, F32)
        o_ref[part, :] = o.astype(BF)
        lse_ref[part, :] = lse


def cross_back(far_ref, q_ref, k_ref, v_ref, do_ref, lse_ref, dq_ref, dk_ref, dv_ref, dk, dv):
    rows = q_ref.shape[0] - CONT_LEN
    far = pl.ds(pl.multiple_of(far_ref[0] * ENC_LEN, ENC_LEN), ENC_LEN)
    dk[ENC_LEN : 2 * ENC_LEN, :] = jnp.zeros((ENC_LEN, TILE), F32)
    dv[ENC_LEN : 2 * ENC_LEN, :] = jnp.zeros((ENC_LEN, TILE), F32)
    for index, (part, keys) in enumerate(
        ((pl.ds(0, rows), pl.ds(0, ENC_LEN)), (pl.ds(rows, CONT_LEN), far))
    ):
        q = q_ref[part, :]
        k = k_ref[keys, :]
        kt = k.T
        v = v_ref[keys, :]
        do = do_ref[part, :]
        lse = lse_ref[part, :].T
        gk, gv = (0.0, 0.0)
        dq = []
        for head in range(2):
            mask = head_mask(head, TILE, BF)
            qm = q * mask
            dom = do * mask
            s = mm(k, qm, NT)
            p = jnp.exp(s - lse[HEAD * head : HEAD * head + 1, :])
            dp = mm(v, dom, NT)
            centre = jnp.sum(p * dp, axis=0, keepdims=True)
            low = (p * (dp - centre)).astype(BF)
            gv = gv + mm(p.astype(BF), dom)
            gk = gk + mm(low, qm)
            dq.append(mm(kt[HEAD * head : HEAD * (head + 1), :], low))
        dq_ref[part, :] = (jnp.concatenate(dq, axis=0).T * HEAD ** (-0.5)).astype(BF)
        if index == 0:
            dk[0:ENC_LEN, :] = gk
            dv[0:ENC_LEN, :] = gv
        else:
            dk[keys, :] = dk[keys, :] + gk
            dv[keys, :] = dv[keys, :] + gv
    dk_ref[...] = dk[...].astype(BF)
    dv_ref[...] = dv[...].astype(BF)


def whole(shape):
    return pl.BlockSpec(shape, lambda *_: (0,) * len(shape))


def by_head(shape):
    return pl.BlockSpec((1,) + shape[1:], lambda head, *_: (head,) + (0,) * (len(shape) - 1))


def cost(flops, transcendentals, arrays):
    return pl.CostEstimate(
        flops=int(flops),
        transcendentals=int(transcendentals),
        bytes_accessed=int(sum(a.size * a.dtype.itemsize for a in arrays)),
    )


def shaped(*pairs):
    return [jax.ShapeDtypeStruct(shape, dtype) for shape, dtype in pairs]


def run_heads(kernel, heads, scalars, lines, arrays, outs, scratch, out_heads, cells, name):
    in_specs = [by_head(a.shape) for a in lines] + [whole(a.shape) for a in arrays]
    out_specs = [
        by_head(o.shape) if i in out_heads else whole(o.shape) for i, o in enumerate(outs)
    ]
    return pl.pallas_call(
        kernel,
        out_shape=outs,
        grid_spec=pltpu.PrefetchScalarGridSpec(
            num_scalar_prefetch=len(scalars),
            grid=(heads,),
            in_specs=in_specs,
            out_specs=out_specs,
            scratch_shapes=scratch,
        ),
        compiler_params=pltpu.CompilerParams(dimension_semantics=("arbitrary",)),
        cost_estimate=cost(
            cells * heads * 256 * 2 * (2 if not out_heads else 5), cells * heads,
            list(lines) + list(arrays) + list(outs),
        ),
        name=name,
    )(*scalars, *lines, *arrays)


def on_device(
    x_prompt,
    x_cont,
    enc_out,
    cot_prompt,
    cot_cont,
    teacher,
    valid,
    prompt_of,
    buckets,
    gain_self,
    gain_cross,
    gain_ffn,
    rel_table,
    w_q,
    w_k,
    w_v,
    w_o,
    c_q,
    c_k,
    c_v,
    c_o,
    w_gate,
    w_up,
    w_down,
):
    width = x_prompt.shape[1]
    cont_count = prompt_of.shape[0]
    heads = w_q.shape[1] // HEAD
    cols = heads * HEAD
    hidden_here = w_gate.shape[1]
    ranks = lax.axis_size("tensor")
    data_size = lax.axis_size("dp")
    share = PROMPT // ranks
    tensor_rank = lax.axis_index("tensor")
    data_rank = lax.axis_index("dp")
    factor = HEAD ** (-0.5)
    up, down = bit_lists()
    order_up, order_down = slice_order(up), slice_order(down)

    far = (prompt_of != data_rank).astype(jnp.int32)
    index = jnp.arange(cont_count, dtype=jnp.int32)
    before = index[None, :] < index[:, None]
    near_rank = jnp.sum(jnp.where(before, 1 - far[None, :], 0), axis=1)
    far_rank = jnp.sum(jnp.where(before, far[None, :], 0), axis=1)
    spot = jnp.where(far == 0, near_rank, cont_count // 2 + far_rank)
    slots = jnp.sum(jnp.where(spot[None, :] == index[:, None], index[None, :], 0), axis=1)
    far_here = lax.dynamic_slice_in_dim(far, tensor_rank, 1, 0)

    def own_rows(prompt_rows, conts):
        return jnp.concatenate(
            [
                lax.dynamic_slice_in_dim(prompt_rows, tensor_rank * share, share, 0),
                lax.dynamic_slice_in_dim(conts, tensor_rank * CONT_LEN, CONT_LEN, 0),
            ]
        )

    head_rows = HEAD // data_size
    attn_shard = jnp.stack([w_o, c_q.T, c_k.T, c_v.T, c_o]).reshape(
        5, 1, heads, data_size, head_rows, width
    )
    attn_own = lax.dynamic_slice_in_dim(attn_shard, data_rank, 1, 3)
    hidden_rows = hidden_here // data_size
    ffn_own = jnp.stack(
        [
            lax.dynamic_slice_in_dim(w_gate, data_rank * hidden_rows, hidden_rows, 1).T,
            lax.dynamic_slice_in_dim(w_up, data_rank * hidden_rows, hidden_rows, 1).T,
            lax.dynamic_slice_in_dim(w_down, data_rank * hidden_rows, hidden_rows, 0),
        ]
    ).reshape(3, 1, 1, 1, hidden_rows, width)
    enc_far = flip_bit(enc_out, 0)
    attn_full = gather_weights(attn_own)
    ffn_full = gather_weights(ffn_own)

    count = jnp.broadcast_to(jnp.sum(valid.astype(F32)), (8, 128))
    for bit in range(data_size.bit_length() - 1):
        count = count + flip_bit(count, bit)
    token_count = count[0, 0]

    bucket_hot = (buckets[::-1][:, None] == jnp.arange(rel_table.shape[0])[None, :]).astype(F32)
    table = jnp.dot(bucket_hot, rel_table, precision=lax.Precision.HIGHEST).T
    line = jnp.concatenate(
        [table, jnp.full((heads, LINE - DIST), masked_value, F32)], axis=1
    ).reshape(heads, 1, LINE)
    ok = jnp.where(valid > 0, 0.0, masked_value).astype(F32)
    ok_rows = jnp.broadcast_to(
        ok.reshape(cont_count, 1, CONT_LEN), (cont_count, CONT_LEN, CONT_LEN)
    )
    ok_cols = jnp.broadcast_to(
        ok.reshape(cont_count, CONT_LEN, 1), (cont_count, CONT_LEN, CONT_LEN)
    )

    stream = jnp.concatenate([x_prompt, x_cont]).astype(F32)
    n1 = rms_norm(stream, gain_self).astype(BF)
    key_s = mm(n1, w_k).astype(BF)
    value_s = mm(n1, w_v).astype(BF)
    query_s = (mm(n1, w_q).astype(F32) * factor).astype(BF)
    key_t = mm(w_k, n1, (((0,), (1,)), ((), ()))).astype(BF)
    pair_far = flip_bit(
        jnp.concatenate([key_s[:PROMPT], value_s[:PROMPT]], axis=0), 0
    )
    key_far, value_far = pair_far[:PROMPT], pair_far[PROMPT:]
    rows_all = query_s.shape[0]
    rows_late = rows_all - PROMPT
    slab = pltpu.VMEM((TILE, SLAB), F32)
    slab_t = pltpu.VMEM((SLAB, TILE), F32)
    o_prompt, lse_prompt = run_heads(
        prompt_fwd, heads, [], [line], [query_s, key_s, value_s],
        shaped(((PROMPT, cols), BF), ((PROMPT, cols), F32)), [slab], (),
        PROMPT * PROMPT * 5 // 8, "prompt_fwd",
    )
    o_cont, lse_cont = run_heads(
        cont_fwd, heads, [slots], [line], [ok_rows, query_s, key_s, value_s, key_far, value_far],
        shaped(((rows_late, cols), BF), ((rows_late, cols), F32)), [slab], (),
        rows_late * DIST, "cont_fwd",
    )

    def heads_to_rows(block, rows):
        out = []
        for step in range(ranks):
            dest = (tensor_rank - step + ranks) % ranks
            piece = lax.dynamic_slice_in_dim(block, dest * rows, rows, 0)
            out.append(piece if step == 0 else from_ahead(piece, step))
        return jnp.concatenate(out, axis=1)

    def rows_to_heads(block):
        out = []
        for step in range(ranks):
            piece = block[:, step * cols : (step + 1) * cols]
            out.append(piece if step == 0 else to_ahead(piece, step))
        rows = block.shape[0]
        held = jnp.concatenate(out, axis=0).reshape(ranks, rows, cols)
        pick = (tensor_rank - jnp.arange(ranks) + ranks) % ranks
        return (held, pick)

    mixed_self = jnp.concatenate(
        [heads_to_rows(o_prompt, share), heads_to_rows(o_cont, CONT_LEN)]
    )

    hot_up = slice_hot(order_up, heads, head_rows, data_rank)
    hot_down = slice_hot(order_down, heads, head_rows, data_rank)
    hot_four = jnp.stack([hot_up, hot_up, hot_down, hot_down])
    attn_flat = attn_full.reshape(5, ranks * cols, width)
    wo_full = (
        jnp.einsum(
            "zrn,zrd->znd",
            hot_four,
            attn_flat[0].reshape(ranks, cols, width),
            preferred_element_type=F32,
        )
        .astype(BF)
        .reshape(ranks * cols, width)
    )
    cq_t, ck_t, cv_t, co_full = attn_flat[1], attn_flat[2], attn_flat[3], attn_flat[4]
    x_own = own_rows(x_prompt, x_cont).astype(F32)
    x1 = x_own + mm(mixed_self, wo_full)
    n2 = rms_norm(x1, gain_cross).astype(BF)
    query_c = (mm(n2, cq_t, NT) * factor).astype(BF)
    enc_pair = jnp.concatenate([enc_out, enc_far])
    key_c = mm(enc_pair, ck_t, NT).astype(BF)
    value_c = mm(enc_pair, cv_t, NT).astype(BF)
    own_count = query_c.shape[0]
    pairs = query_c.shape[1] // TILE

    def columns(rows):
        return pl.BlockSpec((rows, TILE), lambda i, *_: (0, i))

    cross_cells = own_count * ENC_LEN * pairs * 2
    mixed_cross, lse_cross = pl.pallas_call(
        cross_fwd,
        out_shape=shaped(((own_count, pairs * TILE), BF), ((own_count, pairs * TILE), F32)),
        grid_spec=pltpu.PrefetchScalarGridSpec(
            num_scalar_prefetch=1,
            grid=(pairs,),
            in_specs=[columns(own_count), columns(2 * ENC_LEN), columns(2 * ENC_LEN)],
            out_specs=[columns(own_count), columns(own_count)],
        ),
        compiler_params=pltpu.CompilerParams(dimension_semantics=("arbitrary",)),
        cost_estimate=cost(cross_cells * 256 * 2 * 2, cross_cells, [query_c, key_c, value_c]),
        name="cross_fwd",
    )(far_here, query_c, key_c, value_c)
    x2 = x1 + mm(mixed_cross, co_full)
    n3 = rms_norm(x2, gain_ffn).astype(BF)
    ffn_flat = ffn_full.reshape(3, ranks * hidden_here, width)
    wg_t, wu_t, wd = ffn_flat[0], ffn_flat[1], ffn_flat[2]
    gate_pre = mm(n3, wg_t, NT)
    upper = mm(n3, wu_t, NT)
    hidden, gelu_pull = jax.vjp(
        lambda first_in, second_in: jax.nn.gelu(first_in, approximate=True) * second_in,
        gate_pre,
        upper,
    )
    hidden = hidden.astype(BF)
    x3 = x2 + mm(hidden, wd)
    valid_own = lax.dynamic_slice_in_dim(valid, tensor_rank * CONT_LEN, CONT_LEN, 0).astype(F32)[
        :, None
    ]
    deviation = x3[share:] - teacher.astype(F32)
    loss_part = jnp.sum(valid_own * deviation * deviation)
    g3 = jnp.concatenate(
        [
            cot_prompt.astype(F32),
            cot_cont.astype(F32) + 2.0 * valid_own * deviation / token_count,
        ]
    )
    y_all = x3.astype(BF)

    g3_low = g3.astype(BF)
    d_hidden = mm(g3_low, wd, NT).astype(BF).astype(F32)
    d_gate, d_upper = gelu_pull(d_hidden)
    d_gate = d_gate.astype(BF)
    d_upper = d_upper.astype(BF)
    d_n3 = mm(d_gate, wg_t) + mm(d_upper, wu_t)
    ffn_grads = jnp.stack(
        [
            mm(d_gate, n3, TN).astype(BF),
            mm(d_upper, n3, TN).astype(BF),
            mm(hidden, g3_low, TN).astype(BF),
        ]
    ).reshape(3, ranks, 1, data_size, hidden_rows, width)
    ffn_left, ffn_right = reduce_grads(ffn_grads)
    back3, gain_ffn_part = norm_back(x2, gain_ffn, d_n3)
    g2 = g3 + back3

    g2_low = g2.astype(BF)
    d_mixed_c = mm(g2_low, co_full, NT).astype(BF)
    d_query_c, d_key_c, d_value_c = pl.pallas_call(
        cross_back,
        out_shape=shaped(
            ((own_count, pairs * TILE), BF),
            ((2 * ENC_LEN, pairs * TILE), BF),
            ((2 * ENC_LEN, pairs * TILE), BF),
        ),
        grid_spec=pltpu.PrefetchScalarGridSpec(
            num_scalar_prefetch=1,
            grid=(pairs,),
            in_specs=[
                columns(own_count), columns(2 * ENC_LEN), columns(2 * ENC_LEN),
                columns(own_count), columns(own_count),
            ],
            out_specs=[columns(own_count), columns(2 * ENC_LEN), columns(2 * ENC_LEN)],
            scratch_shapes=[pltpu.VMEM((2 * ENC_LEN, TILE), F32)] * 2,
        ),
        compiler_params=pltpu.CompilerParams(dimension_semantics=("arbitrary",)),
        cost_estimate=cost(cross_cells * 256 * 2 * 5, cross_cells, [query_c, key_c, value_c]),
        name="cross_back",
    )(far_here, query_c, key_c, value_c, d_mixed_c, lse_cross)
    d_n2 = mm(d_query_c, cq_t)
    back2, gain_cross_part = norm_back(x1, gain_cross, d_n2)
    g1 = g2 + back2
    g1_low = g1.astype(BF)

    d_mixed_s = mm(g1_low, wo_full, NT).astype(BF)
    held, pick = rows_to_heads(d_mixed_s)
    place = (pick[None, :] == jnp.arange(ranks)[:, None]).astype(BF)
    ordered = jnp.einsum("ns,src->nrc", place, held, preferred_element_type=F32).astype(BF)
    do_prompt = ordered[:, :share].reshape(PROMPT, cols)
    do_cont = ordered[:, share:].reshape(rows_late, cols)

    key_far_t = key_far.T
    (dq_cont, dk_cont, dv_cont, dk_near, dv_near, dk_far, dv_far, line_cont) = run_heads(
        cont_back, heads, [slots], [line],
        [ok_cols, query_s, key_s, key_t, value_s, key_far, key_far_t, value_far, do_cont, lse_cont],
        shaped(
            ((rows_late, cols), BF), ((rows_late, cols), BF), ((rows_late, cols), BF),
            ((PROMPT, cols), F32), ((PROMPT, cols), F32),
            ((PROMPT, cols), BF), ((PROMPT, cols), BF), ((heads, 1, LINE), F32),
        ),
        [slab_t, slab_t, pltpu.VMEM((cont_count, cols, CONT_LEN), F32)]
        + [pltpu.VMEM((rows_late, cols), F32)] * 2 + [pltpu.VMEM((PROMPT, cols), F32)] * 2,
        (7,), rows_late * DIST, "cont_back",
    )
    lent = flip_bit(jnp.concatenate([dk_far, dv_far], axis=0), 0)
    dq_prompt, dk_prompt, dv_prompt, line_prompt = run_heads(
        prompt_back, heads, [], [line],
        [query_s, key_s, key_t, value_s, do_prompt, lse_prompt],
        shaped(
            ((PROMPT, cols), BF), ((PROMPT, cols), F32), ((PROMPT, cols), F32),
            ((heads, 1, LINE), F32),
        ),
        [slab_t, slab_t, pltpu.VMEM((cols, PROMPT), F32)], (3,),
        PROMPT * PROMPT * 5 // 8, "prompt_back",
    )
    dk_prompt = (dk_prompt + dk_near + lent[:PROMPT].astype(F32)).astype(BF)
    dv_prompt = (dv_prompt + dv_near + lent[PROMPT:].astype(F32)).astype(BF)

    def three(q, k, v):
        return mm(q, w_q, NT) + mm(k, w_k, NT) + mm(v, w_v, NT)

    def scatter_rows(block, rows):
        total = lax.dynamic_slice_in_dim(block, tensor_rank * rows, rows, 0).astype(F32)
        for step in range(1, ranks):
            dest = (tensor_rank + step) % ranks
            piece = lax.dynamic_slice_in_dim(block, dest * rows, rows, 0)
            total = total + to_ahead(piece, step).astype(F32)
        return total

    part_cont = three(dq_cont, dk_cont, dv_cont).astype(BF)
    part_prompt = three(dq_prompt, dk_prompt, dv_prompt).astype(BF)
    d_n1 = jnp.concatenate([scatter_rows(part_prompt, share), scatter_rows(part_cont, CONT_LEN)])
    back1, ignored = norm_back(x_own, gain_self, d_n1)
    grad_x = g1 + back1
    unit = stream * norm_scale(stream)
    gain_self_part = jnp.sum(part_prompt.astype(F32) * unit[:PROMPT], axis=0) + jnp.sum(
        part_cont.astype(F32) * unit[PROMPT:], axis=0
    )

    enc_part = mm(d_key_c, ck_t) + mm(d_value_c, cv_t)
    enc_sum = (enc_part[:ENC_LEN] + flip_bit(enc_part[ENC_LEN:].astype(BF), 0).astype(F32)).astype(
        BF
    )
    enc_rows = ENC_LEN // ranks
    enc_own = scatter_rows(enc_sum, enc_rows).astype(BF)
    enc_all = jnp.concatenate(
        [enc_own] + [from_ahead(enc_own, step) for step in range(1, ranks)]
    )
    enc_place = jnp.arange(ENC_LEN)
    enc_from = (tensor_rank + enc_place // enc_rows) % ranks * enc_rows + enc_place % enc_rows
    enc_hot = (enc_from[:, None] == enc_place[None, :]).astype(BF)
    grad_enc = mm(enc_hot, enc_all, TN)

    grad_wo_part = mm(mixed_self, g1_low, TN).astype(BF).reshape(ranks, cols, width)
    grad_wo_part = jnp.einsum(
        "zrn,znd->zrd", hot_four, grad_wo_part, preferred_element_type=F32
    ).astype(BF)
    attn_grads = jnp.stack(
        [
            grad_wo_part.reshape(ranks * cols, width),
            mm(d_query_c, n2, TN).astype(BF),
            mm(d_key_c, enc_pair, TN).astype(BF),
            mm(d_value_c, enc_pair, TN).astype(BF),
            mm(mixed_cross, g2_low, TN).astype(BF),
        ]
    ).reshape(5, ranks, heads, data_size, head_rows, width)
    attn_left, attn_right = reduce_grads(attn_grads)

    def finish(left, right, hots, matrix, transposed):
        halves = [
            half[matrix].reshape(-1, half.shape[-1]) for half in (left, right)
        ]
        if transposed:
            return jnp.concatenate([mm(a, hot, TN) for a, hot in zip(halves, hots)], axis=0)
        return jnp.concatenate([mm(hot, a, TN) for a, hot in zip(halves, hots)], axis=1)

    attn_hots = (hot_up, hot_down)
    ffn_hots = (
        slice_hot(order_up, 1, hidden_rows, data_rank),
        slice_hot(order_down, 1, hidden_rows, data_rank),
    )
    grad_w_o = finish(attn_left, attn_right, attn_hots, 0, False)
    grad_c_q = finish(attn_left, attn_right, attn_hots, 1, True)
    grad_c_k = finish(attn_left, attn_right, attn_hots, 2, True)
    grad_c_v = finish(attn_left, attn_right, attn_hots, 3, True)
    grad_c_o = finish(attn_left, attn_right, attn_hots, 4, False)
    grad_w_gate = finish(ffn_left, ffn_right, ffn_hots, 0, True)
    grad_w_up = finish(ffn_left, ffn_right, ffn_hots, 1, True)
    grad_w_down = finish(ffn_left, ffn_right, ffn_hots, 2, False)

    def by_rows(prompt_part, cont_part):
        return mm(n1[:PROMPT], prompt_part, TN) + mm(n1[PROMPT:], cont_part, TN)

    qkv_grads = jnp.concatenate(
        [
            by_rows(dq_prompt, dq_cont),
            by_rows(dk_prompt, dk_cont),
            by_rows(dv_prompt, dv_cont),
        ],
        axis=1,
    ).astype(BF)
    feat_rows = width // data_size
    qkv_width = qkv_grads.shape[1]
    qkv_hots = (
        slice_hot(order_up, 1, feat_rows, data_rank),
        slice_hot(order_down, 1, feat_rows, data_rank),
    )
    half = qkv_width // 2
    qkv_parts = []
    for hot, bits, cut in (
        (qkv_hots[0], up, qkv_grads[:, :half]),
        (qkv_hots[1], down, qkv_grads[:, half:]),
    ):
        moved = mm(hot, cut).astype(BF).reshape(1, 1, 1, data_size, feat_rows, half)
        for bit in [0] + bits[::-1]:
            moved = fold(moved, bit, 3)
        moved = spread(moved, bits + [0], 3).reshape(width, half)
        qkv_parts.append(mm(hot, moved, TN))
    qkv_all = jnp.concatenate(qkv_parts, axis=1)

    line_grad = (line_cont + line_prompt).reshape(heads, LINE)[:, :DIST]
    table_part = jnp.dot(line_grad, bucket_hot, precision=lax.Precision.HIGHEST)
    small = jnp.zeros((8, width), F32)
    small = small.at[0].set(gain_self_part).at[1].set(gain_cross_part).at[2].set(gain_ffn_part)
    small = small.at[3, 0].set(loss_part)
    small = small.at[4, : table_part.size].set(table_part.reshape(-1))
    for bit in range(data_size.bit_length() - 1):
        small = small + flip_bit(small, bit)
    grad_table = small[4, : table_part.size].reshape(table_part.shape).T
    for bit in range(ranks.bit_length() - 1):
        small = small + flip_bit(small, bit, "tensor")
    return (
        y_all[:share],
        y_all[share:],
        grad_x[:share],
        grad_x[share:],
        grad_enc,
        small[0],
        small[1],
        small[2],
        grad_table,
        qkv_all[:, :cols],
        qkv_all[:, cols : 2 * cols],
        qkv_all[:, 2 * cols :],
        grad_w_o,
        grad_c_q,
        grad_c_k,
        grad_c_v,
        grad_c_o,
        grad_w_gate,
        grad_w_up,
        grad_w_down,
        small[3, 0] / token_count,
    )


def solution(mesh):
    rows = P("dp", None)
    both = P(("dp", "tensor"), None)
    columns = P(None, "tensor")
    shards = P("tensor", None)
    return jax.shard_map(
        on_device,
        mesh=mesh,
        in_specs=(
            (rows,) * 3 + (both,) * 3 + (P("dp"),) * 2 + (P(),) * 4 + (columns,) * 4
            + (shards,) + (columns,) * 3 + (shards,) + (columns,) * 2 + (shards,)
        ),
        out_specs=(
            (both,) * 4 + (rows,) + (P(),) * 3 + (columns,) * 4 + (shards,) + (columns,) * 3
            + (shards,) + (columns,) * 2 + (shards, P())
        ),
        check_vma=False,
    )
```

```python
import functools

import jax
import jax.numpy as jnp
from jax import lax
from jax.experimental import pallas as pl
from jax.experimental.pallas import tpu as pltpu
from jax.sharding import PartitionSpec as P

HEAD = 64
PROMPT = 1024
CONT_LEN = 128
ENC_LEN = 512
TILE = 128
DIST = PROMPT + CONT_LEN
LINE = DIST + 2 * TILE
SLAB = DIST + TILE

norm_eps = 1e-06
masked_value = -1e30
BF = jnp.bfloat16
F32 = jnp.float32
NT = (((1,), (1,)), ((), ()))
TN = (((0,), (0,)), ((), ()))
NN = (((1,), (0,)), ((), ()))


def mm(left, right, dims=NN):
    return lax.dot_general(left, right, dims, preferred_element_type=F32)


def from_ahead(block, step):
    count = lax.axis_size("tensor")
    return lax.ppermute(block, "tensor", [((i + step) % count, i) for i in range(count)])


def to_ahead(block, step):
    count = lax.axis_size("tensor")
    return lax.ppermute(block, "tensor", [(i, (i + step) % count) for i in range(count)])


def flip_bit(block, bit, axis="dp"):
    count = lax.axis_size(axis)
    return lax.ppermute(block, axis, [(i, i ^ (1 << bit)) for i in range(count)])


def bit_lists():
    count = lax.axis_size("dp")
    bits = count.bit_length() - 1
    up = list(range(1, bits))
    return (up, up[::-1])


def slice_order(bits):
    order = [0]
    for bit in bits + [0]:
        order = order + [entry ^ (1 << bit) for entry in order]
    return order


def spread(block, bits, axis):
    for bit in bits:
        block = jnp.concatenate([block, flip_bit(block, bit)], axis=axis)
    return block


def gather_weights(own):
    up, down = bit_lists()
    pieces = [own] + [from_ahead(own, step) for step in range(1, 4)]
    first = spread(jnp.concatenate(pieces[:2], axis=1), up, 3)
    second = spread(jnp.concatenate(pieces[2:], axis=1), down, 3)
    first_far = flip_bit(first, 0)
    second_far = flip_bit(second, 0)
    return jnp.concatenate(
        [
            jnp.concatenate([first, first_far], axis=3),
            jnp.concatenate([second, second_far], axis=3),
        ],
        axis=1,
    )


def fold(block, bit, axis):
    half = block.shape[axis] // 2
    low = lax.slice_in_dim(block, 0, half, axis=axis)
    high = lax.slice_in_dim(block, half, 2 * half, axis=axis)
    return (low.astype(F32) + flip_bit(high, bit).astype(F32)).astype(BF)


def reduce_stages(grads):
    up, down = bit_lists()
    grads = fold(grads, 0, 3)
    yield grads
    first, second = grads[:, :2], grads[:, 2:]
    for one, two in zip(down, up):
        first = fold(first, one, 3)
        second = fold(second, two, 3)
        yield (first, second)
    total = first[:, 0].astype(F32)
    for step, piece in ((1, first[:, 1]), (2, second[:, 0]), (3, second[:, 1])):
        total = total + to_ahead(piece, step).astype(F32)
    total = total.astype(BF)
    yield total
    half = total.shape[-1] // 2
    left, right = total[..., :half], total[..., half:]
    for one, two in zip(up + [0], down + [0]):
        left = spread(left, [one], 2)
        right = spread(right, [two], 2)
        yield (left, right)


def after(value, *others):
    return lax.optimization_barrier((value, others))[0]


def slice_hot(order, parts, rows, rank):
    count = len(order)
    size = parts * count * rows
    place = jnp.arange(size)
    slot = place // rows % count
    table = sum(jnp.where(slot == index, entry, 0) for index, entry in enumerate(order))
    natural = place // (count * rows) * (count * rows) + (rank ^ table) * rows + place % rows
    return (natural[:, None] == jnp.arange(size)[None, :]).astype(BF)


def norm_scale(values):
    return lax.rsqrt(jnp.mean(values * values, axis=-1, keepdims=True) + norm_eps)


def rms_norm(values, weight):
    return values * norm_scale(values) * weight


def norm_back(values, weight, grad):
    scale = norm_scale(values)
    unit = values * scale
    weighted = grad * weight
    inner = jnp.mean(weighted * unit, axis=-1, keepdims=True)
    return (scale * (weighted - unit * inner), jnp.sum(grad * unit, axis=0))


def make_slab(line):
    wide = jnp.broadcast_to(line, (TILE, LINE))
    return pltpu.roll(wide, LINE - (TILE - 1), 1, stride=1, stride_axis=0)[:, :SLAB]


def head_mask(head, width, dtype):
    lane = lax.broadcasted_iota(jnp.int32, (1, width), 1)
    return (lane // HEAD == head).astype(dtype)


def prompt_fwd(line_ref, q_ref, k_ref, v_ref, o_ref, lse_ref, slab):
    head = pl.program_id(0)
    slab[...] = make_slab(line_ref[0])
    width = q_ref.shape[1]
    mask = head_mask(head, width, BF)
    mask_f = head_mask(head, width, F32)

    @pl.when(head == 0)
    def _():
        o_ref[...] = jnp.zeros_like(o_ref)
        lse_ref[...] = jnp.zeros_like(lse_ref)

    vm = v_ref[0:PROMPT, :] * mask
    block = 2 * TILE
    for idx in range(PROMPT // block):
        keys = block * (idx + 1)
        rows = pl.ds(idx * block, block)
        q = q_ref[rows, :] * mask
        s = mm(q, k_ref[0:keys, :], NT)
        start = PROMPT - block * idx
        s = s + jnp.concatenate(
            [slab[:, start : start + keys], slab[:, start - TILE : start - TILE + keys]], axis=0
        )
        top = jnp.max(s, axis=-1, keepdims=True)
        e = jnp.exp(s - top)
        total = jnp.sum(e, axis=-1, keepdims=True)
        o = mm(e.astype(BF), vm[0:keys, :]) / total
        o_ref[rows, :] = o_ref[rows, :] + o.astype(BF)
        lse_ref[rows, :] = lse_ref[rows, :] + (top + jnp.log(total)) * mask_f


def cont_rows(slot):
    return pl.ds(pl.multiple_of(slot * CONT_LEN, CONT_LEN), CONT_LEN)


def late_rows(slot):
    return pl.ds(pl.multiple_of(PROMPT + slot * CONT_LEN, CONT_LEN), CONT_LEN)


def cont_fwd(
    slot_ref, line_ref, ok_ref, q_ref, k_ref, v_ref, kf_ref, vf_ref, o_ref, lse_ref, slab
):
    head = pl.program_id(0)
    slab[...] = make_slab(line_ref[0])
    width = q_ref.shape[1]
    mask = head_mask(head, width, BF)
    mask_f = head_mask(head, width, F32)

    @pl.when(head == 0)
    def _():
        o_ref[...] = jnp.zeros_like(o_ref)
        lse_ref[...] = jnp.zeros_like(lse_ref)

    for pair in range(2):
        keys_ref, values_ref = (k_ref, v_ref) if pair == 0 else (kf_ref, vf_ref)
        slots = [slot_ref[2 * pair], slot_ref[2 * pair + 1]]
        qs = [q_ref[late_rows(slot), :] * mask for slot in slots]
        s = mm(jnp.concatenate(qs, axis=0), keys_ref[0:PROMPT, :], NT)
        s = s + jnp.concatenate([slab[:, 0:PROMPT], slab[:, 0:PROMPT]], axis=0)
        own = jnp.concatenate(
            [
                mm(q, k_ref[late_rows(slot), :], NT) + slab[:, PROMPT:DIST] + ok_ref[slot]
                for q, slot in zip(qs, slots)
            ],
            axis=0,
        )
        top = jnp.maximum(
            jnp.max(s, axis=-1, keepdims=True), jnp.max(own, axis=-1, keepdims=True)
        )
        e = jnp.exp(s - top)
        e_own = jnp.exp(own - top)
        total = jnp.sum(e, axis=-1, keepdims=True) + jnp.sum(e_own, axis=-1, keepdims=True)
        o = mm(e.astype(BF), values_ref[0:PROMPT, :] * mask)
        low = e_own.astype(BF)
        o_own = [
            mm(low[CONT_LEN * i : CONT_LEN * (i + 1), :], v_ref[late_rows(slot), :] * mask)
            for i, slot in enumerate(slots)
        ]
        o = (o + jnp.concatenate(o_own, axis=0)) / total
        lse = (top + jnp.log(total)) * mask_f
        for i, slot in enumerate(slots):
            part = slice(CONT_LEN * i, CONT_LEN * (i + 1))
            o_ref[cont_rows(slot), :] = o_ref[cont_rows(slot), :] + o[part, :].astype(BF)
            lse_ref[cont_rows(slot), :] = lse_ref[cont_rows(slot), :] + lse[part, :]


def row_of(lse, head):
    width = lse.shape[1]
    lane = lax.broadcasted_iota(jnp.int32, (1, width), 1)
    column = jnp.sum(jnp.where(lane == head * HEAD, lse, 0.0), axis=-1, keepdims=True)
    return jnp.broadcast_to(column, (lse.shape[0], TILE)).T[0:1, :]


def fold_slab(block):
    rows = TILE
    block = jnp.concatenate([block, jnp.zeros((TILE, LINE - SLAB), F32)], axis=1)
    while rows > 8:
        rows //= 2
        block = pltpu.roll(block[:rows], rows, 1) + block[rows:]
    line = jnp.zeros((1, LINE), F32)
    for r in range(rows):
        line = line + pltpu.roll(block, rows - 1 - r, 1)[r : r + 1]
    return line


def prompt_back(
    line_ref, q_ref, k_ref, kt_ref, v_ref, do_ref, lse_ref, dq_ref, dk_ref, dv_ref, gl_ref,
    slab, gslab, dqt,
):
    head = pl.program_id(0)
    slab[...] = make_slab(line_ref[0]).T
    gslab[...] = jnp.zeros_like(gslab)
    width = q_ref.shape[1]
    mask = head_mask(head, width, BF)

    @pl.when(head == 0)
    def _():
        dk_ref[...] = jnp.zeros_like(dk_ref)
        dv_ref[...] = jnp.zeros_like(dv_ref)

    mine = pl.ds(pl.multiple_of(head * HEAD, HEAD), HEAD)
    block = 2 * TILE
    for idx in range(PROMPT // block):
        keys = block * (idx + 1)
        rows = pl.ds(idx * block, block)
        q = q_ref[rows, :] * mask
        do = do_ref[rows, :] * mask
        s = mm(k_ref[0:keys, :], q, NT)
        start = PROMPT - block * idx
        s = s + jnp.concatenate(
            [slab[start : start + keys, :], slab[start - TILE : start - TILE + keys, :]], axis=1
        )
        p = jnp.exp(s - row_of(lse_ref[rows, :], head))
        dp = mm(v_ref[0:keys, :], do, NT)
        centre = jnp.sum(p * dp, axis=0, keepdims=True)
        ds = p * (dp - centre)
        low = ds.astype(BF)
        dv_ref[0:keys, :] = dv_ref[0:keys, :] + mm(p.astype(BF), do)
        dk_ref[0:keys, :] = dk_ref[0:keys, :] + mm(low, q)
        dqt[mine, rows] = mm(kt_ref[mine, 0:keys], low)
        gslab[start : start + keys, :] = gslab[start : start + keys, :] + ds[:, 0:TILE]
        gslab[start - TILE : start - TILE + keys, :] = (
            gslab[start - TILE : start - TILE + keys, :] + ds[:, TILE:block]
        )
    gl_ref[0] = fold_slab(gslab[...].T)

    @pl.when(head == pl.num_programs(0) - 1)
    def _():
        dq_ref[...] = (dqt[...].T * HEAD ** (-0.5)).astype(BF)


def cont_back(
    slot_ref, line_ref, ok_ref, q_ref, k_ref, kt_ref, v_ref, kf_ref, ktf_ref, vf_ref, do_ref,
    lse_ref, dq_ref, dkc_ref, dvc_ref, dk_ref, dv_ref, dkf_ref, dvf_ref, gl_ref,
    slab, gslab, dqt, dkc, dvc, dkf, dvf,
):
    head = pl.program_id(0)
    slab[...] = make_slab(line_ref[0]).T
    gslab[...] = jnp.zeros_like(gslab)
    width = q_ref.shape[1]
    mask = head_mask(head, width, BF)

    @pl.when(head == 0)
    def _():
        for ref in (dk_ref, dv_ref, dkf, dvf, dkc, dvc):
            ref[...] = jnp.zeros_like(ref)

    mine = pl.ds(pl.multiple_of(head * HEAD, HEAD), HEAD)
    for pair in range(2):
        keys_ref, kt, values_ref = (
            (k_ref, kt_ref, v_ref) if pair == 0 else (kf_ref, ktf_ref, vf_ref)
        )
        gk, gv = (dk_ref, dv_ref) if pair == 0 else (dkf, dvf)
        slots = [slot_ref[2 * pair], slot_ref[2 * pair + 1]]
        qs = [q_ref[late_rows(slot), :] * mask for slot in slots]
        dos = [do_ref[cont_rows(slot), :] * mask for slot in slots]
        q = jnp.concatenate(qs, axis=0)
        do = jnp.concatenate(dos, axis=0)
        lse = row_of(
            jnp.concatenate([lse_ref[cont_rows(slot), :] for slot in slots], axis=0), head
        )
        s = mm(keys_ref[0:PROMPT, :], q, NT)
        s = s + jnp.concatenate([slab[0:PROMPT, :], slab[0:PROMPT, :]], axis=1)
        own = jnp.concatenate(
            [
                mm(k_ref[late_rows(slot), :], qc, NT) + slab[PROMPT:DIST, :] + ok_ref[slot]
                for qc, slot in zip(qs, slots)
            ],
            axis=1,
        )
        p = jnp.exp(s - lse)
        p_own = jnp.exp(own - lse)
        dp = mm(values_ref[0:PROMPT, :], do, NT)
        dp_own = jnp.concatenate(
            [mm(v_ref[late_rows(slot), :], doc, NT) for doc, slot in zip(dos, slots)], axis=1
        )
        centre = jnp.sum(p * dp, axis=0, keepdims=True) + jnp.sum(
            p_own * dp_own, axis=0, keepdims=True
        )
        ds = p * (dp - centre)
        ds_own = p_own * (dp_own - centre)
        low = ds.astype(BF)
        low_own = ds_own.astype(BF)
        p_low = p_own.astype(BF)
        gv[...] = gv[...] + mm(p.astype(BF), do)
        gk[...] = gk[...] + mm(low, q)
        dq = mm(kt[mine, 0:PROMPT], low)
        for i, slot in enumerate(slots):
            part = slice(CONT_LEN * i, CONT_LEN * (i + 1))
            here = cont_rows(slot)
            dvc[here, :] = dvc[here, :] + mm(p_low[:, part], dos[i])
            dkc[here, :] = dkc[here, :] + mm(low_own[:, part], qs[i])
            kown = k_ref[late_rows(slot), :].T
            head_keys = kown[0:HEAD, :]
            for other in range(1, width // HEAD):
                head_keys = jnp.where(
                    head == other, kown[HEAD * other : HEAD * (other + 1), :], head_keys
                )
            dqt[slot, mine, :] = dq[:, part] + mm(head_keys, low_own[:, part])
            gslab[0:PROMPT, :] = gslab[0:PROMPT, :] + ds[:, part]
            gslab[PROMPT:DIST, :] = gslab[PROMPT:DIST, :] + ds_own[:, part]
    gl_ref[0] = fold_slab(gslab[...].T)

    @pl.when(head == pl.num_programs(0) - 1)
    def _():
        for slot in range(dqt.shape[0]):
            dq_ref[slot * CONT_LEN : (slot + 1) * CONT_LEN, :] = (
                dqt[slot].T * HEAD ** (-0.5)
            ).astype(BF)
        dkf_ref[...] = dkf[...].astype(BF)
        dvf_ref[...] = dvf[...].astype(BF)
        dkc_ref[...] = dkc[...].astype(BF)
        dvc_ref[...] = dvc[...].astype(BF)


def cross_fwd(far_ref, q_ref, k_ref, v_ref, o_ref, lse_ref):
    rows = q_ref.shape[0] - CONT_LEN
    far = pl.ds(pl.multiple_of(far_ref[0] * ENC_LEN, ENC_LEN), ENC_LEN)
    for part, keys in ((pl.ds(0, rows), pl.ds(0, ENC_LEN)), (pl.ds(rows, CONT_LEN), far)):
        q = q_ref[part, :]
        k = k_ref[keys, :]
        v = v_ref[keys, :]
        o = 0.0
        lse = 0.0
        for head in range(2):
            mask = head_mask(head, TILE, BF)
            s = mm(q * mask, k, NT)
            top = jnp.max(s, axis=-1, keepdims=True)
            e = jnp.exp(s - top)
            total = jnp.sum(e, axis=-1, keepdims=True)
            o = o + mm(e.astype(BF), v * mask) / total
            lse = lse + (top + jnp.log(total)) * head_mask(head, TILE, F32)
        o_ref[part, :] = o.astype(BF)
        lse_ref[part, :] = lse


def cross_back(far_ref, q_ref, k_ref, v_ref, do_ref, lse_ref, dq_ref, dk_ref, dv_ref, dk, dv):
    rows = q_ref.shape[0] - CONT_LEN
    far = pl.ds(pl.multiple_of(far_ref[0] * ENC_LEN, ENC_LEN), ENC_LEN)
    dk[ENC_LEN : 2 * ENC_LEN, :] = jnp.zeros((ENC_LEN, TILE), F32)
    dv[ENC_LEN : 2 * ENC_LEN, :] = jnp.zeros((ENC_LEN, TILE), F32)
    for index, (part, keys) in enumerate(
        ((pl.ds(0, rows), pl.ds(0, ENC_LEN)), (pl.ds(rows, CONT_LEN), far))
    ):
        q = q_ref[part, :]
        k = k_ref[keys, :]
        kt = k.T
        v = v_ref[keys, :]
        do = do_ref[part, :]
        lse = lse_ref[part, :].T
        gk, gv = (0.0, 0.0)
        dq = []
        for head in range(2):
            mask = head_mask(head, TILE, BF)
            qm = q * mask
            dom = do * mask
            s = mm(k, qm, NT)
            p = jnp.exp(s - lse[HEAD * head : HEAD * head + 1, :])
            dp = mm(v, dom, NT)
            centre = jnp.sum(p * dp, axis=0, keepdims=True)
            low = (p * (dp - centre)).astype(BF)
            gv = gv + mm(p.astype(BF), dom)
            gk = gk + mm(low, qm)
            dq.append(mm(kt[HEAD * head : HEAD * (head + 1), :], low))
        dq_ref[part, :] = (jnp.concatenate(dq, axis=0).T * HEAD ** (-0.5)).astype(BF)
        if index == 0:
            dk[0:ENC_LEN, :] = gk
            dv[0:ENC_LEN, :] = gv
        else:
            dk[keys, :] = dk[keys, :] + gk
            dv[keys, :] = dv[keys, :] + gv
    dk_ref[...] = dk[...].astype(BF)
    dv_ref[...] = dv[...].astype(BF)


def whole(shape):
    return pl.BlockSpec(shape, lambda *_: (0,) * len(shape))


def by_head(shape):
    return pl.BlockSpec((1,) + shape[1:], lambda head, *_: (head,) + (0,) * (len(shape) - 1))


def cost(flops, transcendentals, arrays):
    return pl.CostEstimate(
        flops=int(flops),
        transcendentals=int(transcendentals),
        bytes_accessed=int(sum(a.size * a.dtype.itemsize for a in arrays)),
    )


def shaped(*pairs):
    return [jax.ShapeDtypeStruct(shape, dtype) for shape, dtype in pairs]


def run_heads(kernel, heads, scalars, lines, arrays, outs, scratch, out_heads, cells, name):
    in_specs = [by_head(a.shape) for a in lines] + [whole(a.shape) for a in arrays]
    out_specs = [
        by_head(o.shape) if i in out_heads else whole(o.shape) for i, o in enumerate(outs)
    ]
    return pl.pallas_call(
        kernel,
        out_shape=outs,
        grid_spec=pltpu.PrefetchScalarGridSpec(
            num_scalar_prefetch=len(scalars),
            grid=(heads,),
            in_specs=in_specs,
            out_specs=out_specs,
            scratch_shapes=scratch,
        ),
        compiler_params=pltpu.CompilerParams(dimension_semantics=("arbitrary",)),
        cost_estimate=cost(
            cells * heads * 256 * 2 * (2 if not out_heads else 5), cells * heads,
            list(lines) + list(arrays) + list(outs),
        ),
        name=name,
    )(*scalars, *lines, *arrays)


def on_device(
    x_prompt,
    x_cont,
    enc_out,
    cot_prompt,
    cot_cont,
    teacher,
    valid,
    prompt_of,
    buckets,
    gain_self,
    gain_cross,
    gain_ffn,
    rel_table,
    w_q,
    w_k,
    w_v,
    w_o,
    c_q,
    c_k,
    c_v,
    c_o,
    w_gate,
    w_up,
    w_down,
):
    width = x_prompt.shape[1]
    cont_count = prompt_of.shape[0]
    heads = w_q.shape[1] // HEAD
    cols = heads * HEAD
    hidden_here = w_gate.shape[1]
    ranks = lax.axis_size("tensor")
    data_size = lax.axis_size("dp")
    share = PROMPT // ranks
    tensor_rank = lax.axis_index("tensor")
    data_rank = lax.axis_index("dp")
    factor = HEAD ** (-0.5)
    up, down = bit_lists()
    order_up, order_down = slice_order(up), slice_order(down)

    far = (prompt_of != data_rank).astype(jnp.int32)
    index = jnp.arange(cont_count, dtype=jnp.int32)
    before = index[None, :] < index[:, None]
    near_rank = jnp.sum(jnp.where(before, 1 - far[None, :], 0), axis=1)
    far_rank = jnp.sum(jnp.where(before, far[None, :], 0), axis=1)
    spot = jnp.where(far == 0, near_rank, cont_count // 2 + far_rank)
    slots = jnp.sum(jnp.where(spot[None, :] == index[:, None], index[None, :], 0), axis=1)
    far_here = lax.dynamic_slice_in_dim(far, tensor_rank, 1, 0)

    def own_rows(prompt_rows, conts):
        return jnp.concatenate(
            [
                lax.dynamic_slice_in_dim(prompt_rows, tensor_rank * share, share, 0),
                lax.dynamic_slice_in_dim(conts, tensor_rank * CONT_LEN, CONT_LEN, 0),
            ]
        )

    head_rows = HEAD // data_size
    attn_shard = jnp.stack([w_o, c_q.T, c_k.T, c_v.T, c_o]).reshape(
        5, 1, heads, data_size, head_rows, width
    )
    attn_own = lax.dynamic_slice_in_dim(attn_shard, data_rank, 1, 3)
    hidden_rows = hidden_here // data_size
    ffn_own = jnp.stack(
        [
            lax.dynamic_slice_in_dim(w_gate, data_rank * hidden_rows, hidden_rows, 1).T,
            lax.dynamic_slice_in_dim(w_up, data_rank * hidden_rows, hidden_rows, 1).T,
            lax.dynamic_slice_in_dim(w_down, data_rank * hidden_rows, hidden_rows, 0),
        ]
    ).reshape(3, 1, 1, 1, hidden_rows, width)
    enc_far = flip_bit(enc_out, 0)
    attn_full = gather_weights(attn_own)
    ffn_full = gather_weights(ffn_own)

    count = jnp.broadcast_to(jnp.sum(valid.astype(F32)), (8, 128))
    for bit in range(data_size.bit_length() - 1):
        count = count + flip_bit(count, bit)
    token_count = count[0, 0]

    bucket_hot = (buckets[::-1][:, None] == jnp.arange(rel_table.shape[0])[None, :]).astype(F32)
    table = jnp.dot(bucket_hot, rel_table, precision=lax.Precision.HIGHEST).T
    line = jnp.concatenate(
        [table, jnp.full((heads, LINE - DIST), masked_value, F32)], axis=1
    ).reshape(heads, 1, LINE)
    ok = jnp.where(valid > 0, 0.0, masked_value).astype(F32)
    ok_rows = jnp.broadcast_to(
        ok.reshape(cont_count, 1, CONT_LEN), (cont_count, CONT_LEN, CONT_LEN)
    )
    ok_cols = jnp.broadcast_to(
        ok.reshape(cont_count, CONT_LEN, 1), (cont_count, CONT_LEN, CONT_LEN)
    )

    stream = jnp.concatenate([x_prompt, x_cont]).astype(F32)
    n1 = rms_norm(stream, gain_self).astype(BF)
    key_s = mm(n1, w_k).astype(BF)
    value_s = mm(n1, w_v).astype(BF)
    query_s = (mm(n1, w_q).astype(F32) * factor).astype(BF)
    key_t = mm(w_k, n1, (((0,), (1,)), ((), ()))).astype(BF)
    pair_far = flip_bit(
        jnp.concatenate([key_s[:PROMPT], value_s[:PROMPT]], axis=0), 0
    )
    key_far, value_far = pair_far[:PROMPT], pair_far[PROMPT:]
    rows_all = query_s.shape[0]
    rows_late = rows_all - PROMPT
    slab = pltpu.VMEM((TILE, SLAB), F32)
    slab_t = pltpu.VMEM((SLAB, TILE), F32)
    o_prompt, lse_prompt = run_heads(
        prompt_fwd, heads, [], [line], [query_s, key_s, value_s],
        shaped(((PROMPT, cols), BF), ((PROMPT, cols), F32)), [slab], (),
        PROMPT * PROMPT * 5 // 8, "prompt_fwd",
    )
    o_cont, lse_cont = run_heads(
        cont_fwd, heads, [slots], [line], [ok_rows, query_s, key_s, value_s, key_far, value_far],
        shaped(((rows_late, cols), BF), ((rows_late, cols), F32)), [slab], (),
        rows_late * DIST, "cont_fwd",
    )

    def heads_to_rows(block, rows):
        out = []
        for step in range(ranks):
            dest = (tensor_rank - step + ranks) % ranks
            piece = lax.dynamic_slice_in_dim(block, dest * rows, rows, 0)
            out.append(piece if step == 0 else from_ahead(piece, step))
        return jnp.concatenate(out, axis=1)

    def rows_to_heads(block):
        out = []
        for step in range(ranks):
            piece = block[:, step * cols : (step + 1) * cols]
            out.append(piece if step == 0 else to_ahead(piece, step))
        rows = block.shape[0]
        held = jnp.concatenate(out, axis=0).reshape(ranks, rows, cols)
        pick = (tensor_rank - jnp.arange(ranks) + ranks) % ranks
        return (held, pick)

    mixed_self = jnp.concatenate(
        [heads_to_rows(o_prompt, share), heads_to_rows(o_cont, CONT_LEN)]
    )

    hot_up = slice_hot(order_up, heads, head_rows, data_rank)
    hot_down = slice_hot(order_down, heads, head_rows, data_rank)
    hot_four = jnp.stack([hot_up, hot_up, hot_down, hot_down])
    attn_flat = attn_full.reshape(5, ranks * cols, width)
    wo_full = (
        jnp.einsum(
            "zrn,zrd->znd",
            hot_four,
            attn_flat[0].reshape(ranks, cols, width),
            preferred_element_type=F32,
        )
        .astype(BF)
        .reshape(ranks * cols, width)
    )
    cq_t, ck_t, cv_t, co_full = attn_flat[1], attn_flat[2], attn_flat[3], attn_flat[4]
    x_own = own_rows(x_prompt, x_cont).astype(F32)
    x1 = x_own + mm(mixed_self, wo_full)
    n2 = rms_norm(x1, gain_cross).astype(BF)
    query_c = (mm(n2, cq_t, NT) * factor).astype(BF)
    enc_pair = jnp.concatenate([enc_out, enc_far])
    key_c = mm(enc_pair, ck_t, NT).astype(BF)
    value_c = mm(enc_pair, cv_t, NT).astype(BF)
    own_count = query_c.shape[0]
    pairs = query_c.shape[1] // TILE

    def columns(rows):
        return pl.BlockSpec((rows, TILE), lambda i, *_: (0, i))

    cross_cells = own_count * ENC_LEN * pairs * 2
    mixed_cross, lse_cross = pl.pallas_call(
        cross_fwd,
        out_shape=shaped(((own_count, pairs * TILE), BF), ((own_count, pairs * TILE), F32)),
        grid_spec=pltpu.PrefetchScalarGridSpec(
            num_scalar_prefetch=1,
            grid=(pairs,),
            in_specs=[columns(own_count), columns(2 * ENC_LEN), columns(2 * ENC_LEN)],
            out_specs=[columns(own_count), columns(own_count)],
        ),
        compiler_params=pltpu.CompilerParams(dimension_semantics=("arbitrary",)),
        cost_estimate=cost(cross_cells * 256 * 2 * 2, cross_cells, [query_c, key_c, value_c]),
        name="cross_fwd",
    )(far_here, query_c, key_c, value_c)
    x2 = x1 + mm(mixed_cross, co_full)
    n3 = rms_norm(x2, gain_ffn).astype(BF)
    ffn_flat = ffn_full.reshape(3, ranks * hidden_here, width)
    wg_t, wu_t, wd = ffn_flat[0], ffn_flat[1], ffn_flat[2]
    gate_pre = mm(n3, wg_t, NT)
    upper = mm(n3, wu_t, NT)
    hidden, gelu_pull = jax.vjp(
        lambda first_in, second_in: jax.nn.gelu(first_in, approximate=True) * second_in,
        gate_pre,
        upper,
    )
    hidden = hidden.astype(BF)
    x3 = x2 + mm(hidden, wd)
    valid_own = lax.dynamic_slice_in_dim(valid, tensor_rank * CONT_LEN, CONT_LEN, 0).astype(F32)[
        :, None
    ]
    deviation = x3[share:] - teacher.astype(F32)
    loss_part = jnp.sum(valid_own * deviation * deviation)
    g3 = jnp.concatenate(
        [
            cot_prompt.astype(F32),
            cot_cont.astype(F32) + 2.0 * valid_own * deviation / token_count,
        ]
    )
    y_all = x3.astype(BF)

    g3_low = g3.astype(BF)
    d_hidden = mm(g3_low, wd, NT).astype(BF).astype(F32)
    d_gate, d_upper = gelu_pull(d_hidden)
    d_gate = d_gate.astype(BF)
    d_upper = d_upper.astype(BF)
    ffn_grads = jnp.stack(
        [
            mm(d_gate, n3, TN).astype(BF),
            mm(d_upper, n3, TN).astype(BF),
            mm(hidden, g3_low, TN).astype(BF),
        ]
    ).reshape(3, ranks, 1, data_size, hidden_rows, width)
    ffn_steps = reduce_stages(ffn_grads)
    ffn_core = next(ffn_steps)
    d_gate, d_upper = after((d_gate, d_upper), ffn_grads)
    d_n3 = mm(d_gate, wg_t) + mm(d_upper, wu_t)
    back3, gain_ffn_part = norm_back(x2, gain_ffn, d_n3)
    g2 = g3 + back3

    g2_low = g2.astype(BF)
    d_mixed_c = after(mm(g2_low, co_full, NT).astype(BF), ffn_core)
    ffn_plane = next(ffn_steps)
    d_query_c, d_key_c, d_value_c = pl.pallas_call(
        cross_back,
        out_shape=shaped(
            ((own_count, pairs * TILE), BF),
            ((2 * ENC_LEN, pairs * TILE), BF),
            ((2 * ENC_LEN, pairs * TILE), BF),
        ),
        grid_spec=pltpu.PrefetchScalarGridSpec(
            num_scalar_prefetch=1,
            grid=(pairs,),
            in_specs=[
                columns(own_count), columns(2 * ENC_LEN), columns(2 * ENC_LEN),
                columns(own_count), columns(own_count),
            ],
            out_specs=[columns(own_count), columns(2 * ENC_LEN), columns(2 * ENC_LEN)],
            scratch_shapes=[pltpu.VMEM((2 * ENC_LEN, TILE), F32)] * 2,
        ),
        compiler_params=pltpu.CompilerParams(dimension_semantics=("arbitrary",)),
        cost_estimate=cost(cross_cells * 256 * 2 * 5, cross_cells, [query_c, key_c, value_c]),
        name="cross_back",
    )(far_here, query_c, key_c, value_c, d_mixed_c, lse_cross)
    d_n2 = mm(d_query_c, cq_t)
    back2, gain_cross_part = norm_back(x1, gain_cross, d_n2)
    g1 = g2 + back2
    g1_low = g1.astype(BF)

    grad_wo_part = mm(mixed_self, g1_low, TN).astype(BF).reshape(ranks, cols, width)
    grad_wo_part = jnp.einsum(
        "zrn,znd->zrd", hot_four, grad_wo_part, preferred_element_type=F32
    ).astype(BF)
    attn_grads = jnp.stack(
        [
            grad_wo_part.reshape(ranks * cols, width),
            mm(d_query_c, n2, TN).astype(BF),
            mm(d_key_c, enc_pair, TN).astype(BF),
            mm(d_value_c, enc_pair, TN).astype(BF),
            mm(mixed_cross, g2_low, TN).astype(BF),
        ]
    ).reshape(5, ranks, heads, data_size, head_rows, width)
    attn_steps = reduce_stages(attn_grads)
    attn_core = next(attn_steps)
    d_mixed_s = after(mm(g1_low, wo_full, NT).astype(BF), ffn_plane)
    ffn_line = next(ffn_steps)
    held, pick = rows_to_heads(d_mixed_s)
    place = (pick[None, :] == jnp.arange(ranks)[:, None]).astype(BF)
    ordered = jnp.einsum("ns,src->nrc", place, held, preferred_element_type=F32).astype(BF)
    do_prompt = ordered[:, :share].reshape(PROMPT, cols)
    do_cont = ordered[:, share:].reshape(rows_late, cols)

    do_cont = after(do_cont, ffn_line, attn_core)
    ffn_tensor = next(ffn_steps)
    attn_plane = next(attn_steps)
    key_far_t = key_far.T
    (dq_cont, dk_cont, dv_cont, dk_near, dv_near, dk_far, dv_far, line_cont) = run_heads(
        cont_back, heads, [slots], [line],
        [ok_cols, query_s, key_s, key_t, value_s, key_far, key_far_t, value_far, do_cont, lse_cont],
        shaped(
            ((rows_late, cols), BF), ((rows_late, cols), BF), ((rows_late, cols), BF),
            ((PROMPT, cols), F32), ((PROMPT, cols), F32),
            ((PROMPT, cols), BF), ((PROMPT, cols), BF), ((heads, 1, LINE), F32),
        ),
        [slab_t, slab_t, pltpu.VMEM((cont_count, cols, CONT_LEN), F32)]
        + [pltpu.VMEM((rows_late, cols), F32)] * 2 + [pltpu.VMEM((PROMPT, cols), F32)] * 2,
        (7,), rows_late * DIST, "cont_back",
    )
    lent = flip_bit(jnp.concatenate([dk_far, dv_far], axis=0), 0)
    do_prompt = after(do_prompt, dq_cont, ffn_tensor, attn_plane)
    ffn_back = next(ffn_steps)
    attn_line = next(attn_steps)
    dq_prompt, dk_prompt, dv_prompt, line_prompt = run_heads(
        prompt_back, heads, [], [line],
        [query_s, key_s, key_t, value_s, do_prompt, lse_prompt],
        shaped(
            ((PROMPT, cols), BF), ((PROMPT, cols), F32), ((PROMPT, cols), F32),
            ((heads, 1, LINE), F32),
        ),
        [slab_t, slab_t, pltpu.VMEM((cols, PROMPT), F32)], (3,),
        PROMPT * PROMPT * 5 // 8, "prompt_back",
    )
    dk_prompt = (dk_prompt + dk_near + lent[:PROMPT].astype(F32)).astype(BF)
    dv_prompt = (dv_prompt + dv_near + lent[PROMPT:].astype(F32)).astype(BF)

    def three(q, k, v):
        return mm(q, w_q, NT) + mm(k, w_k, NT) + mm(v, w_v, NT)

    def scatter_rows(block, rows):
        total = lax.dynamic_slice_in_dim(block, tensor_rank * rows, rows, 0).astype(F32)
        for step in range(1, ranks):
            dest = (tensor_rank + step) % ranks
            piece = lax.dynamic_slice_in_dim(block, dest * rows, rows, 0)
            total = total + to_ahead(piece, step).astype(F32)
        return total

    part_cont = three(dq_cont, dk_cont, dv_cont).astype(BF)
    part_prompt = three(dq_prompt, dk_prompt, dv_prompt).astype(BF)
    d_n1 = jnp.concatenate([scatter_rows(part_prompt, share), scatter_rows(part_cont, CONT_LEN)])
    back1, ignored = norm_back(x_own, gain_self, d_n1)
    grad_x = g1 + back1
    unit = stream * norm_scale(stream)
    gain_self_part = jnp.sum(part_prompt.astype(F32) * unit[:PROMPT], axis=0) + jnp.sum(
        part_cont.astype(F32) * unit[PROMPT:], axis=0
    )

    enc_part = mm(d_key_c, ck_t) + mm(d_value_c, cv_t)
    enc_sum = (enc_part[:ENC_LEN] + flip_bit(enc_part[ENC_LEN:].astype(BF), 0).astype(F32)).astype(
        BF
    )
    enc_rows = ENC_LEN // ranks
    enc_own = scatter_rows(enc_sum, enc_rows).astype(BF)
    enc_all = jnp.concatenate(
        [enc_own] + [from_ahead(enc_own, step) for step in range(1, ranks)]
    )
    enc_place = jnp.arange(ENC_LEN)
    enc_from = (tensor_rank + enc_place // enc_rows) % ranks * enc_rows + enc_place % enc_rows
    enc_hot = (enc_from[:, None] == enc_place[None, :]).astype(BF)
    grad_enc = mm(enc_hot, enc_all, TN)

    ffn_left, ffn_right = list(ffn_steps)[-1]
    attn_left, attn_right = list(attn_steps)[-1]

    def finish(left, right, hots, matrix, transposed):
        halves = [
            half[matrix].reshape(-1, half.shape[-1]) for half in (left, right)
        ]
        if transposed:
            return jnp.concatenate([mm(a, hot, TN) for a, hot in zip(halves, hots)], axis=0)
        return jnp.concatenate([mm(hot, a, TN) for a, hot in zip(halves, hots)], axis=1)

    attn_hots = (hot_up, hot_down)
    ffn_hots = (
        slice_hot(order_up, 1, hidden_rows, data_rank),
        slice_hot(order_down, 1, hidden_rows, data_rank),
    )
    grad_w_o = finish(attn_left, attn_right, attn_hots, 0, False)
    grad_c_q = finish(attn_left, attn_right, attn_hots, 1, True)
    grad_c_k = finish(attn_left, attn_right, attn_hots, 2, True)
    grad_c_v = finish(attn_left, attn_right, attn_hots, 3, True)
    grad_c_o = finish(attn_left, attn_right, attn_hots, 4, False)
    grad_w_gate = finish(ffn_left, ffn_right, ffn_hots, 0, True)
    grad_w_up = finish(ffn_left, ffn_right, ffn_hots, 1, True)
    grad_w_down = finish(ffn_left, ffn_right, ffn_hots, 2, False)

    def by_rows(prompt_part, cont_part):
        return mm(n1[:PROMPT], prompt_part, TN) + mm(n1[PROMPT:], cont_part, TN)

    qkv_grads = jnp.concatenate(
        [
            by_rows(dq_prompt, dq_cont),
            by_rows(dk_prompt, dk_cont),
            by_rows(dv_prompt, dv_cont),
        ],
        axis=1,
    ).astype(BF)
    feat_rows = width // data_size
    qkv_width = qkv_grads.shape[1]
    qkv_hots = (
        slice_hot(order_up, 1, feat_rows, data_rank),
        slice_hot(order_down, 1, feat_rows, data_rank),
    )
    half = qkv_width // 2
    qkv_parts = []
    for hot, bits, cut in (
        (qkv_hots[0], up, qkv_grads[:, :half]),
        (qkv_hots[1], down, qkv_grads[:, half:]),
    ):
        moved = mm(hot, cut).astype(BF).reshape(1, 1, 1, data_size, feat_rows, half)
        for bit in [0] + bits[::-1]:
            moved = fold(moved, bit, 3)
        moved = spread(moved, bits + [0], 3).reshape(width, half)
        qkv_parts.append(mm(hot, moved, TN))
    qkv_all = jnp.concatenate(qkv_parts, axis=1)

    line_grad = (line_cont + line_prompt).reshape(heads, LINE)[:, :DIST]
    table_part = jnp.dot(line_grad, bucket_hot, precision=lax.Precision.HIGHEST)
    small = jnp.zeros((8, width), F32)
    small = small.at[0].set(gain_self_part).at[1].set(gain_cross_part).at[2].set(gain_ffn_part)
    small = small.at[3, 0].set(loss_part)
    small = small.at[4, : table_part.size].set(table_part.reshape(-1))
    for bit in range(data_size.bit_length() - 1):
        small = small + flip_bit(small, bit)
    grad_table = small[4, : table_part.size].reshape(table_part.shape).T
    for bit in range(ranks.bit_length() - 1):
        small = small + flip_bit(small, bit, "tensor")
    return (
        y_all[:share],
        y_all[share:],
        grad_x[:share],
        grad_x[share:],
        grad_enc,
        small[0],
        small[1],
        small[2],
        grad_table,
        qkv_all[:, :cols],
        qkv_all[:, cols : 2 * cols],
        qkv_all[:, 2 * cols :],
        grad_w_o,
        grad_c_q,
        grad_c_k,
        grad_c_v,
        grad_c_o,
        grad_w_gate,
        grad_w_up,
        grad_w_down,
        small[3, 0] / token_count,
    )


def solution(mesh):
    rows = P("dp", None)
    both = P(("dp", "tensor"), None)
    columns = P(None, "tensor")
    shards = P("tensor", None)
    return jax.shard_map(
        on_device,
        mesh=mesh,
        in_specs=(
            (rows,) * 3 + (both,) * 3 + (P("dp"),) * 2 + (P(),) * 4 + (columns,) * 4
            + (shards,) + (columns,) * 3 + (shards,) + (columns,) * 2 + (shards,)
        ),
        out_specs=(
            (both,) * 4 + (rows,) + (P(),) * 3 + (columns,) * 4 + (shards,) + (columns,) * 3
            + (shards,) + (columns,) * 2 + (shards, P())
        ),
        check_vma=False,
    )
```

```python
import functools

import jax
import jax.numpy as jnp
from jax import lax
from jax.experimental import pallas as pl
from jax.experimental.pallas import tpu as pltpu
from jax.sharding import PartitionSpec as P

HEAD = 64
PROMPT = 1024
CONT_LEN = 128
ENC_LEN = 512
TILE = 128
DIST = PROMPT + CONT_LEN
LINE = DIST + 2 * TILE
SLAB = DIST + TILE

norm_eps = 1e-06
masked_value = -1e30
BF = jnp.bfloat16
F32 = jnp.float32
NT = (((1,), (1,)), ((), ()))
TN = (((0,), (0,)), ((), ()))
NN = (((1,), (0,)), ((), ()))


def mm(left, right, dims=NN):
    return lax.dot_general(left, right, dims, preferred_element_type=F32)


def from_ahead(block, step):
    count = lax.axis_size("tensor")
    return lax.ppermute(block, "tensor", [((i + step) % count, i) for i in range(count)])


def to_ahead(block, step):
    count = lax.axis_size("tensor")
    return lax.ppermute(block, "tensor", [(i, (i + step) % count) for i in range(count)])


def flip_bit(block, bit, axis="dp"):
    count = lax.axis_size(axis)
    return lax.ppermute(block, axis, [(i, i ^ (1 << bit)) for i in range(count)])


def norm_scale(values):
    return lax.rsqrt(jnp.mean(values * values, axis=-1, keepdims=True) + norm_eps)


def rms_norm(values, weight):
    return values * norm_scale(values) * weight


def norm_back(values, weight, grad):
    scale = norm_scale(values)
    unit = values * scale
    weighted = grad * weight
    inner = jnp.mean(weighted * unit, axis=-1, keepdims=True)
    return (scale * (weighted - unit * inner), jnp.sum(grad * unit, axis=0))


def make_slab(line):
    wide = jnp.broadcast_to(line, (TILE, LINE))
    return pltpu.roll(wide, LINE - (TILE - 1), 1, stride=1, stride_axis=0)[:, :SLAB]


def head_mask(head, width, dtype):
    lane = lax.broadcasted_iota(jnp.int32, (1, width), 1)
    return (lane // HEAD == head).astype(dtype)


def prompt_fwd(line_ref, q_ref, k_ref, v_ref, o_ref, lse_ref, slab):
    head = pl.program_id(0)
    slab[...] = make_slab(line_ref[0])
    width = q_ref.shape[1]
    mask = head_mask(head, width, BF)
    mask_f = head_mask(head, width, F32)

    @pl.when(head == 0)
    def _():
        o_ref[...] = jnp.zeros_like(o_ref)
        lse_ref[...] = jnp.zeros_like(lse_ref)

    vm = v_ref[0:PROMPT, :] * mask
    block = 2 * TILE
    for idx in range(PROMPT // block):
        keys = block * (idx + 1)
        rows = pl.ds(idx * block, block)
        q = q_ref[rows, :] * mask
        s = mm(q, k_ref[0:keys, :], NT)
        start = PROMPT - block * idx
        s = s + jnp.concatenate(
            [slab[:, start : start + keys], slab[:, start - TILE : start - TILE + keys]], axis=0
        )
        top = jnp.max(s, axis=-1, keepdims=True)
        e = jnp.exp(s - top)
        total = jnp.sum(e, axis=-1, keepdims=True)
        o = mm(e.astype(BF), vm[0:keys, :]) / total
        o_ref[rows, :] = o_ref[rows, :] + o.astype(BF)
        lse_ref[rows, :] = lse_ref[rows, :] + (top + jnp.log(total)) * mask_f


def cont_rows(slot):
    return pl.ds(pl.multiple_of(slot * CONT_LEN, CONT_LEN), CONT_LEN)


def late_rows(slot):
    return pl.ds(pl.multiple_of(PROMPT + slot * CONT_LEN, CONT_LEN), CONT_LEN)


def cont_fwd(
    slot_ref, line_ref, ok_ref, q_ref, k_ref, v_ref, kf_ref, vf_ref, o_ref, lse_ref, slab
):
    head = pl.program_id(0)
    slab[...] = make_slab(line_ref[0])
    width = q_ref.shape[1]
    mask = head_mask(head, width, BF)
    mask_f = head_mask(head, width, F32)

    @pl.when(head == 0)
    def _():
        o_ref[...] = jnp.zeros_like(o_ref)
        lse_ref[...] = jnp.zeros_like(lse_ref)

    for pair in range(2):
        keys_ref, values_ref = (k_ref, v_ref) if pair == 0 else (kf_ref, vf_ref)
        slots = [slot_ref[2 * pair], slot_ref[2 * pair + 1]]
        qs = [q_ref[late_rows(slot), :] * mask for slot in slots]
        s = mm(jnp.concatenate(qs, axis=0), keys_ref[0:PROMPT, :], NT)
        s = s + jnp.concatenate([slab[:, 0:PROMPT], slab[:, 0:PROMPT]], axis=0)
        own = jnp.concatenate(
            [
                mm(q, k_ref[late_rows(slot), :], NT) + slab[:, PROMPT:DIST] + ok_ref[slot]
                for q, slot in zip(qs, slots)
            ],
            axis=0,
        )
        top = jnp.maximum(
            jnp.max(s, axis=-1, keepdims=True), jnp.max(own, axis=-1, keepdims=True)
        )
        e = jnp.exp(s - top)
        e_own = jnp.exp(own - top)
        total = jnp.sum(e, axis=-1, keepdims=True) + jnp.sum(e_own, axis=-1, keepdims=True)
        o = mm(e.astype(BF), values_ref[0:PROMPT, :] * mask)
        low = e_own.astype(BF)
        o_own = [
            mm(low[CONT_LEN * i : CONT_LEN * (i + 1), :], v_ref[late_rows(slot), :] * mask)
            for i, slot in enumerate(slots)
        ]
        o = (o + jnp.concatenate(o_own, axis=0)) / total
        lse = (top + jnp.log(total)) * mask_f
        for i, slot in enumerate(slots):
            part = slice(CONT_LEN * i, CONT_LEN * (i + 1))
            o_ref[cont_rows(slot), :] = o_ref[cont_rows(slot), :] + o[part, :].astype(BF)
            lse_ref[cont_rows(slot), :] = lse_ref[cont_rows(slot), :] + lse[part, :]


def row_of(lse, head):
    width = lse.shape[1]
    lane = lax.broadcasted_iota(jnp.int32, (1, width), 1)
    column = jnp.sum(jnp.where(lane == head * HEAD, lse, 0.0), axis=-1, keepdims=True)
    return jnp.broadcast_to(column, (lse.shape[0], TILE)).T[0:1, :]


def fold_slab(block):
    rows = TILE
    block = jnp.concatenate([block, jnp.zeros((TILE, LINE - SLAB), F32)], axis=1)
    while rows > 8:
        rows //= 2
        block = pltpu.roll(block[:rows], rows, 1) + block[rows:]
    line = jnp.zeros((1, LINE), F32)
    for r in range(rows):
        line = line + pltpu.roll(block, rows - 1 - r, 1)[r : r + 1]
    return line


def prompt_back(
    line_ref, q_ref, k_ref, kt_ref, v_ref, do_ref, lse_ref, dq_ref, dk_ref, dv_ref, gl_ref,
    slab, gslab, dqt,
):
    head = pl.program_id(0)
    slab[...] = make_slab(line_ref[0]).T
    gslab[...] = jnp.zeros_like(gslab)
    width = q_ref.shape[1]
    mask = head_mask(head, width, BF)

    @pl.when(head == 0)
    def _():
        dk_ref[...] = jnp.zeros_like(dk_ref)
        dv_ref[...] = jnp.zeros_like(dv_ref)

    mine = pl.ds(pl.multiple_of(head * HEAD, HEAD), HEAD)
    block = 2 * TILE
    for idx in range(PROMPT // block):
        keys = block * (idx + 1)
        rows = pl.ds(idx * block, block)
        q = q_ref[rows, :] * mask
        do = do_ref[rows, :] * mask
        s = mm(k_ref[0:keys, :], q, NT)
        start = PROMPT - block * idx
        s = s + jnp.concatenate(
            [slab[start : start + keys, :], slab[start - TILE : start - TILE + keys, :]], axis=1
        )
        p = jnp.exp(s - row_of(lse_ref[rows, :], head))
        dp = mm(v_ref[0:keys, :], do, NT)
        centre = jnp.sum(p * dp, axis=0, keepdims=True)
        ds = p * (dp - centre)
        low = ds.astype(BF)
        dv_ref[0:keys, :] = dv_ref[0:keys, :] + mm(p.astype(BF), do)
        dk_ref[0:keys, :] = dk_ref[0:keys, :] + mm(low, q)
        dqt[mine, rows] = mm(kt_ref[mine, 0:keys], low)
        gslab[start : start + keys, :] = gslab[start : start + keys, :] + ds[:, 0:TILE]
        gslab[start - TILE : start - TILE + keys, :] = (
            gslab[start - TILE : start - TILE + keys, :] + ds[:, TILE:block]
        )
    gl_ref[0] = fold_slab(gslab[...].T)

    @pl.when(head == pl.num_programs(0) - 1)
    def _():
        dq_ref[...] = (dqt[...].T * HEAD ** (-0.5)).astype(BF)


def cont_back(
    slot_ref, line_ref, ok_ref, q_ref, k_ref, kt_ref, v_ref, kf_ref, ktf_ref, vf_ref, do_ref,
    lse_ref, dq_ref, dkc_ref, dvc_ref, dk_ref, dv_ref, dkf_ref, dvf_ref, gl_ref,
    slab, gslab, dqt, dkc, dvc, dkf, dvf,
):
    head = pl.program_id(0)
    slab[...] = make_slab(line_ref[0]).T
    gslab[...] = jnp.zeros_like(gslab)
    width = q_ref.shape[1]
    mask = head_mask(head, width, BF)

    @pl.when(head == 0)
    def _():
        for ref in (dk_ref, dv_ref, dkf, dvf, dkc, dvc):
            ref[...] = jnp.zeros_like(ref)

    mine = pl.ds(pl.multiple_of(head * HEAD, HEAD), HEAD)
    for pair in range(2):
        keys_ref, kt, values_ref = (
            (k_ref, kt_ref, v_ref) if pair == 0 else (kf_ref, ktf_ref, vf_ref)
        )
        gk, gv = (dk_ref, dv_ref) if pair == 0 else (dkf, dvf)
        slots = [slot_ref[2 * pair], slot_ref[2 * pair + 1]]
        qs = [q_ref[late_rows(slot), :] * mask for slot in slots]
        dos = [do_ref[cont_rows(slot), :] * mask for slot in slots]
        q = jnp.concatenate(qs, axis=0)
        do = jnp.concatenate(dos, axis=0)
        lse = row_of(
            jnp.concatenate([lse_ref[cont_rows(slot), :] for slot in slots], axis=0), head
        )
        s = mm(keys_ref[0:PROMPT, :], q, NT)
        s = s + jnp.concatenate([slab[0:PROMPT, :], slab[0:PROMPT, :]], axis=1)
        own = jnp.concatenate(
            [
                mm(k_ref[late_rows(slot), :], qc, NT) + slab[PROMPT:DIST, :] + ok_ref[slot]
                for qc, slot in zip(qs, slots)
            ],
            axis=1,
        )
        p = jnp.exp(s - lse)
        p_own = jnp.exp(own - lse)
        dp = mm(values_ref[0:PROMPT, :], do, NT)
        dp_own = jnp.concatenate(
            [mm(v_ref[late_rows(slot), :], doc, NT) for doc, slot in zip(dos, slots)], axis=1
        )
        centre = jnp.sum(p * dp, axis=0, keepdims=True) + jnp.sum(
            p_own * dp_own, axis=0, keepdims=True
        )
        ds = p * (dp - centre)
        ds_own = p_own * (dp_own - centre)
        low = ds.astype(BF)
        low_own = ds_own.astype(BF)
        p_low = p_own.astype(BF)
        gv[...] = gv[...] + mm(p.astype(BF), do)
        gk[...] = gk[...] + mm(low, q)
        dq = mm(kt[mine, 0:PROMPT], low)
        for i, slot in enumerate(slots):
            part = slice(CONT_LEN * i, CONT_LEN * (i + 1))
            here = cont_rows(slot)
            dvc[here, :] = dvc[here, :] + mm(p_low[:, part], dos[i])
            dkc[here, :] = dkc[here, :] + mm(low_own[:, part], qs[i])
            kown = k_ref[late_rows(slot), :].T
            head_keys = kown[0:HEAD, :]
            for other in range(1, width // HEAD):
                head_keys = jnp.where(
                    head == other, kown[HEAD * other : HEAD * (other + 1), :], head_keys
                )
            dqt[slot, mine, :] = dq[:, part] + mm(head_keys, low_own[:, part])
            gslab[0:PROMPT, :] = gslab[0:PROMPT, :] + ds[:, part]
            gslab[PROMPT:DIST, :] = gslab[PROMPT:DIST, :] + ds_own[:, part]
    gl_ref[0] = fold_slab(gslab[...].T)

    @pl.when(head == pl.num_programs(0) - 1)
    def _():
        for slot in range(dqt.shape[0]):
            dq_ref[slot * CONT_LEN : (slot + 1) * CONT_LEN, :] = (
                dqt[slot].T * HEAD ** (-0.5)
            ).astype(BF)
        dkf_ref[...] = dkf[...].astype(BF)
        dvf_ref[...] = dvf[...].astype(BF)
        dkc_ref[...] = dkc[...].astype(BF)
        dvc_ref[...] = dvc[...].astype(BF)


def cross_fwd(far_ref, q_ref, k_ref, v_ref, o_ref, lse_ref):
    rows = q_ref.shape[0] - CONT_LEN
    far = pl.ds(pl.multiple_of(far_ref[0] * ENC_LEN, ENC_LEN), ENC_LEN)
    for part, keys in ((pl.ds(0, rows), pl.ds(0, ENC_LEN)), (pl.ds(rows, CONT_LEN), far)):
        q = q_ref[part, :]
        k = k_ref[keys, :]
        v = v_ref[keys, :]
        o = 0.0
        lse = 0.0
        for head in range(2):
            mask = head_mask(head, TILE, BF)
            s = mm(q * mask, k, NT)
            top = jnp.max(s, axis=-1, keepdims=True)
            e = jnp.exp(s - top)
            total = jnp.sum(e, axis=-1, keepdims=True)
            o = o + mm(e.astype(BF), v * mask) / total
            lse = lse + (top + jnp.log(total)) * head_mask(head, TILE, F32)
        o_ref[part, :] = o.astype(BF)
        lse_ref[part, :] = lse


def cross_back(far_ref, q_ref, k_ref, v_ref, do_ref, lse_ref, dq_ref, dk_ref, dv_ref, dk, dv):
    rows = q_ref.shape[0] - CONT_LEN
    far = pl.ds(pl.multiple_of(far_ref[0] * ENC_LEN, ENC_LEN), ENC_LEN)
    dk[ENC_LEN : 2 * ENC_LEN, :] = jnp.zeros((ENC_LEN, TILE), F32)
    dv[ENC_LEN : 2 * ENC_LEN, :] = jnp.zeros((ENC_LEN, TILE), F32)
    for index, (part, keys) in enumerate(
        ((pl.ds(0, rows), pl.ds(0, ENC_LEN)), (pl.ds(rows, CONT_LEN), far))
    ):
        q = q_ref[part, :]
        k = k_ref[keys, :]
        kt = k.T
        v = v_ref[keys, :]
        do = do_ref[part, :]
        lse = lse_ref[part, :].T
        gk, gv = (0.0, 0.0)
        dq = []
        for head in range(2):
            mask = head_mask(head, TILE, BF)
            qm = q * mask
            dom = do * mask
            s = mm(k, qm, NT)
            p = jnp.exp(s - lse[HEAD * head : HEAD * head + 1, :])
            dp = mm(v, dom, NT)
            centre = jnp.sum(p * dp, axis=0, keepdims=True)
            low = (p * (dp - centre)).astype(BF)
            gv = gv + mm(p.astype(BF), dom)
            gk = gk + mm(low, qm)
            dq.append(mm(kt[HEAD * head : HEAD * (head + 1), :], low))
        dq_ref[part, :] = (jnp.concatenate(dq, axis=0).T * HEAD ** (-0.5)).astype(BF)
        if index == 0:
            dk[0:ENC_LEN, :] = gk
            dv[0:ENC_LEN, :] = gv
        else:
            dk[keys, :] = dk[keys, :] + gk
            dv[keys, :] = dv[keys, :] + gv
    dk_ref[...] = dk[...].astype(BF)
    dv_ref[...] = dv[...].astype(BF)


def whole(shape):
    return pl.BlockSpec(shape, lambda *_: (0,) * len(shape))


def by_head(shape):
    return pl.BlockSpec((1,) + shape[1:], lambda head, *_: (head,) + (0,) * (len(shape) - 1))


def cost(flops, transcendentals, arrays):
    return pl.CostEstimate(
        flops=int(flops),
        transcendentals=int(transcendentals),
        bytes_accessed=int(sum(a.size * a.dtype.itemsize for a in arrays)),
    )


def shaped(*pairs):
    return [jax.ShapeDtypeStruct(shape, dtype) for shape, dtype in pairs]


MESH = pl.DeviceIdType.MESH


class Links:
    def __init__(self, sends, receives, local, bits):
        self.sends, self.receives, self.local_sems = sends, receives, local
        self.used = 0
        self.used_local = 0
        self.bits = bits
        self.data = lax.axis_index("dp")
        self.tensor = lax.axis_index("tensor")
        self.ranks = lax.axis_size("tensor")

    def bit(self, index):
        return self.data // (1 << index) % 2

    def partner(self, index):
        return (self.data + (1 << index) * (1 - 2 * self.bit(index)), self.tensor)

    def ahead(self, step):
        return (self.data, (self.tensor + step) % self.ranks)

    def across(self, index):
        here = self.tensor // (1 << index) % 2
        return (self.data, self.tensor + (1 << index) * (1 - 2 * here))

    def barrier(self):
        sem = pltpu.get_barrier_semaphore()
        others = [self.partner(index) for index in range(self.bits)]
        others += [self.ahead(step) for step in range(1, self.ranks)]
        for other in others:
            pl.semaphore_signal(sem, inc=1, device_id=other, device_id_type=MESH)
        pl.semaphore_wait(sem, len(others))

    def send(self, source, target, device):
        copy = pltpu.make_async_remote_copy(
            src_ref=source,
            dst_ref=target,
            send_sem=self.sends.at[self.used],
            recv_sem=self.receives.at[self.used],
            device_id=device,
            device_id_type=MESH,
        )
        self.used += 1
        copy.start()
        return copy

    def local(self, source, target):
        copy = pltpu.make_async_copy(source, target, self.local_sems.at[self.used_local])
        self.used_local += 1
        copy.start()
        return copy


def span(start, size, step):
    return pl.ds(pl.multiple_of(start, step), size)


def run_pairs(streams, stages):
    pairs = [streams[i : i + 2] for i in range(0, len(streams), 2)]
    for step in range(len(pairs) + stages):
        for index in reversed(range(len(pairs))):
            if 0 <= step - index <= stages:
                for stream in pairs[index]:
                    next(stream, None)


def bit_order(place):
    return (1, 2) if place % 2 == 0 else (2, 1)


def split_chunks(sizes, unit):
    chunks = []
    for index, rows in enumerate(sizes):
        step = rows
        while step > unit:
            step //= 2
        chunks += [(index, start, step) for start in range(0, rows, step)]
    return chunks


def gather_stream(links, own, full, stage, first, rows, place):
    one, two = bit_order(place)
    width = own.shape[1]
    half = width // 2
    cols = span(links.bit(0) * half, half, 128)
    base = first + links.bit(one) * (rows // 2)
    quarter = span(base + links.bit(two) * (rows // 4), rows // 4, 16)
    mine = links.local(own.at[pl.ds(first, rows), :], stage)
    ranks = links.ranks
    copies = [
        links.send(own.at[quarter, cols], full.at[ranks - step, quarter, cols], links.ahead(step))
        for step in range(1, ranks)
    ]
    yield
    mine.wait()
    home = links.local(stage, full.at[0, pl.ds(first, rows), :])
    for copy in copies:
        copy.wait()
    others = pl.ds(1, ranks - 1)
    part = full.at[others, quarter, cols]
    copy = links.send(part, part, links.partner(two))
    yield
    copy.wait()
    part = full.at[others, span(base, rows // 2, 16), cols]
    copy = links.send(part, part, links.partner(one))
    yield
    copy.wait()
    part = full.at[others, pl.ds(first, rows), cols]
    copy = links.send(part, part, links.partner(0))
    yield
    copy.wait()
    home.wait()


def gather_kernel(count, bits, chunks, *refs):
    own, full = refs[:count], refs[count : 2 * count]
    scratch = refs[2 * count :]
    stages, (sends, receives, local) = scratch[:-3], scratch[-3:]
    links = Links(sends, receives, local, bits)
    links.barrier()
    streams = [
        gather_stream(links, own[index], full[index], stages[place], first, rows, place)
        for place, (index, first, rows) in enumerate(chunks)
    ]
    run_pairs(streams, 4)


def gather_all(own, bits):
    ranks = lax.axis_size("tensor")
    chunks = split_chunks([a.shape[0] for a in own], 256)
    any_space = pl.BlockSpec(memory_space=pl.ANY)
    copies = len(chunks) * (ranks + 2)
    return pl.pallas_call(
        functools.partial(gather_kernel, len(own), bits, chunks),
        out_shape=[jax.ShapeDtypeStruct((ranks,) + a.shape, a.dtype) for a in own],
        in_specs=[any_space] * len(own),
        out_specs=[any_space] * len(own),
        scratch_shapes=[pltpu.VMEM((rows, own[0].shape[1]), BF) for _, _, rows in chunks]
        + [
            pltpu.SemaphoreType.DMA((copies,)),
            pltpu.SemaphoreType.DMA((copies,)),
            pltpu.SemaphoreType.DMA((2 * len(chunks),)),
        ],
        compiler_params=pltpu.CompilerParams(
            collective_id=1, has_side_effects=True, vmem_limit_bytes=60 * 2**20
        ),
        name="gather_all",
    )(*own)


def reduce_stream(links, grad, total, room, first, rows, place, slabs):
    mine, from_core, from_one, from_two, from_far, from_more = room
    one, two = bit_order(place)
    half = grad.shape[2] // 2
    whole_rows = pl.ds(first, rows)
    here = span(links.bit(0) * half, half, 128)
    there = span((1 - links.bit(0)) * half, half, 128)
    kept = links.local(grad.at[:, whole_rows, here], mine)
    copy = links.send(grad.at[:, whole_rows, there], from_core, links.partner(0))
    yield
    kept.wait()
    copy.wait()
    mine[...] = mine[...] + from_core[...]
    base = links.bit(one) * (rows // 2)
    given = (1 - links.bit(one)) * (rows // 2)
    copy = links.send(
        mine.at[:, span(given, rows // 2, 16), :], from_one, links.partner(one)
    )
    yield
    copy.wait()
    keep = span(base, rows // 2, 16)
    mine[:, keep, :] = mine[:, keep, :] + from_one[...]
    given = base + (1 - links.bit(two)) * (rows // 4)
    base_two = base + links.bit(two) * (rows // 4)
    copy = links.send(
        mine.at[:, span(given, rows // 4, 16), :], from_two, links.partner(two)
    )
    yield
    copy.wait()
    keep = span(base_two, rows // 4, 16)
    if slabs > 1:
        mine[:, keep, :] = mine[:, keep, :] + from_two[...]
        copies = [
            links.send(mine.at[step, keep, :], from_far.at[step - 1], links.ahead(step))
            for step in range(1, slabs)
        ]
        yield
        for copy in copies:
            copy.wait()
        value = mine[0, keep, :].astype(F32)
        for step in range(slabs - 1):
            value = value + from_far[step].astype(F32)
        value = value.astype(BF)
    else:
        yield
        value = mine[0, keep, :] + from_two[0]
    quarter = span(first + base_two, rows // 4, 16)
    for index in range(3, links.bits):
        total[quarter, here] = value
        copy = links.send(
            total.at[quarter, here], from_more.at[index - 3], links.partner(index)
        )
        copy.wait()
        value = value + from_more[index - 3]
    total[quarter, here] = value
    copy = links.send(total.at[quarter, here], total.at[quarter, here], links.partner(two))
    yield
    copy.wait()
    part = total.at[span(first + base, rows // 2, 16), here]
    copy = links.send(part, part, links.partner(one))
    yield
    copy.wait()
    part = total.at[whole_rows, here]
    copy = links.send(part, part, links.partner(0))
    yield
    copy.wait()


def small_stream(links, small, held, came, grouped, final):
    held[0] = small[...]
    tensor_bits = links.ranks.bit_length() - 1
    for index in range(links.bits + tensor_bits):
        device = links.partner(index) if index < links.bits else links.across(index - links.bits)
        copy = links.send(held.at[index], came.at[index], device)
        yield
        copy.wait()
        value = held[index] + came[index]
        held[index + 1] = value
        if index == links.bits - 1:
            grouped[...] = value
    final[...] = value
    yield


def reduce_kernel(count, bits, chunks, parts, *refs):
    refs = list(refs)
    grads = [refs.pop(0) for _ in range(count)]
    sends_in = [refs.pop(0) for _ in range(parts)]
    small = refs.pop(0)
    totals = [refs.pop(0) for _ in range(count)]
    came_in = [refs.pop(0) for _ in range(parts)]
    grouped, final = refs.pop(0), refs.pop(0)
    local, receives, sends = refs.pop(), refs.pop(), refs.pop()
    came, held = refs.pop(), refs.pop()
    rooms = [refs[6 * i : 6 * i + 6] for i in range(len(chunks))]
    links = Links(sends, receives, local, bits)
    links.barrier()
    rows_moved = [
        links.send(source.at[(links.tensor + step) % links.ranks], target.at[step - 1],
                   links.ahead(step))
        for source, target in zip(sends_in, came_in)
        for step in range(1, links.ranks)
    ]
    streams = [small_stream(links, small, held, came, grouped, final)]
    streams = [
        reduce_stream(
            links, grads[index], totals[index], rooms[place], first, rows, place,
            grads[index].shape[0],
        )
        for place, (index, first, rows) in enumerate(chunks)
    ] + streams
    run_pairs(streams, max(7, bits + links.ranks.bit_length() - 1))
    for copy in rows_moved:
        copy.wait()


def reduce_all(grads, parts, small, bits):
    ranks = lax.axis_size("tensor")
    chunks = split_chunks([a.shape[1] for a in grads], 200)
    chunks = [c for c in chunks if grads[c[0]].shape[0] > 1] + [
        c for c in chunks if grads[c[0]].shape[0] == 1
    ]
    width = small.shape[1]
    half = width // 2
    more = max(bits - 3, 1)
    rooms = []
    for index, _, rows in chunks:
        slabs = grads[index].shape[0]
        rooms += [
            pltpu.VMEM((slabs, rows, half), BF),
            pltpu.VMEM((slabs, rows, half), BF),
            pltpu.VMEM((slabs, rows // 2, half), BF),
            pltpu.VMEM((slabs, rows // 4, half), BF),
            pltpu.VMEM((ranks - 1, rows // 4, half), BF),
            pltpu.VMEM((more, rows // 4, half), BF),
        ]
    small_steps = bits + ranks.bit_length() - 1
    copies = (
        len(chunks) * (6 + ranks - 1 + bits - 3) + len(parts) * (ranks - 1) + small_steps
    )
    any_space = pl.BlockSpec(memory_space=pl.ANY)
    vmem = pl.BlockSpec(memory_space=pltpu.VMEM)
    out = pl.pallas_call(
        functools.partial(reduce_kernel, len(grads), bits, chunks, len(parts)),
        out_shape=shaped(
            *[(a.shape[1:], BF) for a in grads],
            *[((ranks - 1,) + a.shape[1:], a.dtype) for a in parts],
            (small.shape, F32),
            (small.shape, F32),
        ),
        in_specs=[any_space] * (len(grads) + len(parts)) + [vmem],
        out_specs=[vmem] * len(grads) + [any_space] * len(parts) + [vmem] * 2,
        scratch_shapes=rooms
        + [
            pltpu.VMEM((small_steps + 1,) + small.shape, F32),
            pltpu.VMEM((small_steps,) + small.shape, F32),
            pltpu.SemaphoreType.DMA((copies,)),
            pltpu.SemaphoreType.DMA((copies,)),
            pltpu.SemaphoreType.DMA((len(chunks),)),
        ],
        compiler_params=pltpu.CompilerParams(
            collective_id=2, has_side_effects=True, vmem_limit_bytes=60 * 2**20
        ),
        name="reduce_all",
    )(*grads, *parts, small)
    count = len(grads)
    return out[:count], out[count:-2], out[-2], out[-1]


def run_heads(kernel, heads, scalars, lines, arrays, outs, scratch, out_heads, cells, name):
    in_specs = [by_head(a.shape) for a in lines] + [whole(a.shape) for a in arrays]
    out_specs = [
        by_head(o.shape) if i in out_heads else whole(o.shape) for i, o in enumerate(outs)
    ]
    return pl.pallas_call(
        kernel,
        out_shape=outs,
        grid_spec=pltpu.PrefetchScalarGridSpec(
            num_scalar_prefetch=len(scalars),
            grid=(heads,),
            in_specs=in_specs,
            out_specs=out_specs,
            scratch_shapes=scratch,
        ),
        compiler_params=pltpu.CompilerParams(dimension_semantics=("arbitrary",)),
        cost_estimate=cost(
            cells * heads * 256 * 2 * (2 if not out_heads else 5), cells * heads,
            list(lines) + list(arrays) + list(outs),
        ),
        name=name,
    )(*scalars, *lines, *arrays)


def on_device(
    x_prompt,
    x_cont,
    enc_out,
    cot_prompt,
    cot_cont,
    teacher,
    valid,
    prompt_of,
    buckets,
    gain_self,
    gain_cross,
    gain_ffn,
    rel_table,
    w_q,
    w_k,
    w_v,
    w_o,
    c_q,
    c_k,
    c_v,
    c_o,
    w_gate,
    w_up,
    w_down,
):
    width = x_prompt.shape[1]
    cont_count = prompt_of.shape[0]
    heads = w_q.shape[1] // HEAD
    cols = heads * HEAD
    hidden_here = w_gate.shape[1]
    ranks = lax.axis_size("tensor")
    data_size = lax.axis_size("dp")
    share = PROMPT // ranks
    tensor_rank = lax.axis_index("tensor")
    data_rank = lax.axis_index("dp")
    factor = HEAD ** (-0.5)
    bits = data_size.bit_length() - 1

    far = (prompt_of != data_rank).astype(jnp.int32)
    index = jnp.arange(cont_count, dtype=jnp.int32)
    before = index[None, :] < index[:, None]
    near_rank = jnp.sum(jnp.where(before, 1 - far[None, :], 0), axis=1)
    far_rank = jnp.sum(jnp.where(before, far[None, :], 0), axis=1)
    spot = jnp.where(far == 0, near_rank, cont_count // 2 + far_rank)
    slots = jnp.sum(jnp.where(spot[None, :] == index[:, None], index[None, :], 0), axis=1)
    far_here = lax.dynamic_slice_in_dim(far, tensor_rank, 1, 0)

    def own_rows(prompt_rows, conts):
        return jnp.concatenate(
            [
                lax.dynamic_slice_in_dim(prompt_rows, tensor_rank * share, share, 0),
                lax.dynamic_slice_in_dim(conts, tensor_rank * CONT_LEN, CONT_LEN, 0),
            ]
        )

    enc_far = flip_bit(enc_out, 0)
    wo_all, cq_all, ck_all, cv_all, co_all, wg_all, wu_all, wd_all = gather_all(
        [w_o, c_q.T, c_k.T, c_v.T, c_o, w_gate.T, w_up.T, w_down], bits
    )

    count = jnp.broadcast_to(jnp.sum(valid.astype(F32)), (8, 128))
    for bit in range(bits):
        count = count + flip_bit(count, bit)
    token_count = count[0, 0]

    bucket_hot = (buckets[::-1][:, None] == jnp.arange(rel_table.shape[0])[None, :]).astype(F32)
    table = jnp.dot(bucket_hot, rel_table, precision=lax.Precision.HIGHEST).T
    line = jnp.concatenate(
        [table, jnp.full((heads, LINE - DIST), masked_value, F32)], axis=1
    ).reshape(heads, 1, LINE)
    ok = jnp.where(valid > 0, 0.0, masked_value).astype(F32)
    ok_rows = jnp.broadcast_to(
        ok.reshape(cont_count, 1, CONT_LEN), (cont_count, CONT_LEN, CONT_LEN)
    )
    ok_cols = jnp.broadcast_to(
        ok.reshape(cont_count, CONT_LEN, 1), (cont_count, CONT_LEN, CONT_LEN)
    )

    stream = jnp.concatenate([x_prompt, x_cont]).astype(F32)
    n1 = rms_norm(stream, gain_self).astype(BF)
    key_s = mm(n1, w_k).astype(BF)
    value_s = mm(n1, w_v).astype(BF)
    query_s = (mm(n1, w_q).astype(F32) * factor).astype(BF)
    key_t = mm(w_k, n1, (((0,), (1,)), ((), ()))).astype(BF)
    pair_far = flip_bit(
        jnp.concatenate([key_s[:PROMPT], value_s[:PROMPT]], axis=0), 0
    )
    key_far, value_far = pair_far[:PROMPT], pair_far[PROMPT:]
    rows_all = query_s.shape[0]
    rows_late = rows_all - PROMPT
    slab = pltpu.VMEM((TILE, SLAB), F32)
    slab_t = pltpu.VMEM((SLAB, TILE), F32)
    o_prompt, lse_prompt = run_heads(
        prompt_fwd, heads, [], [line], [query_s, key_s, value_s],
        shaped(((PROMPT, cols), BF), ((PROMPT, cols), F32)), [slab], (),
        PROMPT * PROMPT * 5 // 8, "prompt_fwd",
    )
    o_cont, lse_cont = run_heads(
        cont_fwd, heads, [slots], [line], [ok_rows, query_s, key_s, value_s, key_far, value_far],
        shaped(((rows_late, cols), BF), ((rows_late, cols), F32)), [slab], (),
        rows_late * DIST, "cont_fwd",
    )

    def heads_to_rows(block, rows):
        out = []
        for step in range(ranks):
            dest = (tensor_rank - step + ranks) % ranks
            piece = lax.dynamic_slice_in_dim(block, dest * rows, rows, 0)
            out.append(piece if step == 0 else from_ahead(piece, step))
        return jnp.concatenate(out, axis=1)

    def rows_to_heads(block):
        out = []
        for step in range(ranks):
            piece = block[:, step * cols : (step + 1) * cols]
            out.append(piece if step == 0 else to_ahead(piece, step))
        rows = block.shape[0]
        held = jnp.concatenate(out, axis=0).reshape(ranks, rows, cols)
        pick = (tensor_rank - jnp.arange(ranks) + ranks) % ranks
        return (held, pick)

    mixed_self = jnp.concatenate(
        [heads_to_rows(o_prompt, share), heads_to_rows(o_cont, CONT_LEN)]
    )

    wo_full, cq_t, ck_t, cv_t, co_full = (
        a.reshape(ranks * cols, width) for a in (wo_all, cq_all, ck_all, cv_all, co_all)
    )
    x_own = own_rows(x_prompt, x_cont).astype(F32)
    x1 = x_own + mm(mixed_self, wo_full)
    n2 = rms_norm(x1, gain_cross).astype(BF)
    query_c = (mm(n2, cq_t, NT) * factor).astype(BF)
    enc_pair = jnp.concatenate([enc_out, enc_far])
    key_c = mm(enc_pair, ck_t, NT).astype(BF)
    value_c = mm(enc_pair, cv_t, NT).astype(BF)
    own_count = query_c.shape[0]
    pairs = query_c.shape[1] // TILE

    def columns(rows):
        return pl.BlockSpec((rows, TILE), lambda i, *_: (0, i))

    cross_cells = own_count * ENC_LEN * pairs * 2
    mixed_cross, lse_cross = pl.pallas_call(
        cross_fwd,
        out_shape=shaped(((own_count, pairs * TILE), BF), ((own_count, pairs * TILE), F32)),
        grid_spec=pltpu.PrefetchScalarGridSpec(
            num_scalar_prefetch=1,
            grid=(pairs,),
            in_specs=[columns(own_count), columns(2 * ENC_LEN), columns(2 * ENC_LEN)],
            out_specs=[columns(own_count), columns(own_count)],
        ),
        compiler_params=pltpu.CompilerParams(dimension_semantics=("arbitrary",)),
        cost_estimate=cost(cross_cells * 256 * 2 * 2, cross_cells, [query_c, key_c, value_c]),
        name="cross_fwd",
    )(far_here, query_c, key_c, value_c)
    x2 = x1 + mm(mixed_cross, co_full)
    n3 = rms_norm(x2, gain_ffn).astype(BF)
    wg_t, wu_t, wd = (a.reshape(ranks * hidden_here, width) for a in (wg_all, wu_all, wd_all))
    gate_pre = mm(n3, wg_t, NT)
    upper = mm(n3, wu_t, NT)
    hidden, gelu_pull = jax.vjp(
        lambda first_in, second_in: jax.nn.gelu(first_in, approximate=True) * second_in,
        gate_pre,
        upper,
    )
    hidden = hidden.astype(BF)
    x3 = x2 + mm(hidden, wd)
    valid_own = lax.dynamic_slice_in_dim(valid, tensor_rank * CONT_LEN, CONT_LEN, 0).astype(F32)[
        :, None
    ]
    deviation = x3[share:] - teacher.astype(F32)
    loss_part = jnp.sum(valid_own * deviation * deviation)
    g3 = jnp.concatenate(
        [
            cot_prompt.astype(F32),
            cot_cont.astype(F32) + 2.0 * valid_own * deviation / token_count,
        ]
    )
    y_all = x3.astype(BF)

    g3_low = g3.astype(BF)
    d_hidden = mm(g3_low, wd, NT).astype(BF).astype(F32)
    d_gate, d_upper = gelu_pull(d_hidden)
    d_gate = d_gate.astype(BF)
    d_upper = d_upper.astype(BF)
    ffn_grads = [
        mm(d_gate, n3, TN).astype(BF),
        mm(d_upper, n3, TN).astype(BF),
        mm(hidden, g3_low, TN).astype(BF),
    ]
    d_n3 = mm(d_gate, wg_t) + mm(d_upper, wu_t)
    back3, gain_ffn_part = norm_back(x2, gain_ffn, d_n3)
    g2 = g3 + back3

    g2_low = g2.astype(BF)
    d_mixed_c = mm(g2_low, co_full, NT).astype(BF)
    d_query_c, d_key_c, d_value_c = pl.pallas_call(
        cross_back,
        out_shape=shaped(
            ((own_count, pairs * TILE), BF),
            ((2 * ENC_LEN, pairs * TILE), BF),
            ((2 * ENC_LEN, pairs * TILE), BF),
        ),
        grid_spec=pltpu.PrefetchScalarGridSpec(
            num_scalar_prefetch=1,
            grid=(pairs,),
            in_specs=[
                columns(own_count), columns(2 * ENC_LEN), columns(2 * ENC_LEN),
                columns(own_count), columns(own_count),
            ],
            out_specs=[columns(own_count), columns(2 * ENC_LEN), columns(2 * ENC_LEN)],
            scratch_shapes=[pltpu.VMEM((2 * ENC_LEN, TILE), F32)] * 2,
        ),
        compiler_params=pltpu.CompilerParams(dimension_semantics=("arbitrary",)),
        cost_estimate=cost(cross_cells * 256 * 2 * 5, cross_cells, [query_c, key_c, value_c]),
        name="cross_back",
    )(far_here, query_c, key_c, value_c, d_mixed_c, lse_cross)
    d_n2 = mm(d_query_c, cq_t)
    back2, gain_cross_part = norm_back(x1, gain_cross, d_n2)
    g1 = g2 + back2
    g1_low = g1.astype(BF)

    attn_grads = [
        mm(mixed_self, g1_low, TN).astype(BF),
        mm(d_query_c, n2, TN).astype(BF),
        mm(d_key_c, enc_pair, TN).astype(BF),
        mm(d_value_c, enc_pair, TN).astype(BF),
        mm(mixed_cross, g2_low, TN).astype(BF),
    ]
    d_mixed_s = mm(g1_low, wo_full, NT).astype(BF)
    held, pick = rows_to_heads(d_mixed_s)
    place = (pick[None, :] == jnp.arange(ranks)[:, None]).astype(BF)
    ordered = jnp.einsum("ns,src->nrc", place, held, preferred_element_type=F32).astype(BF)
    do_prompt = ordered[:, :share].reshape(PROMPT, cols)
    do_cont = ordered[:, share:].reshape(rows_late, cols)

    key_far_t = key_far.T
    (dq_cont, dk_cont, dv_cont, dk_near, dv_near, dk_far, dv_far, line_cont) = run_heads(
        cont_back, heads, [slots], [line],
        [ok_cols, query_s, key_s, key_t, value_s, key_far, key_far_t, value_far, do_cont, lse_cont],
        shaped(
            ((rows_late, cols), BF), ((rows_late, cols), BF), ((rows_late, cols), BF),
            ((PROMPT, cols), F32), ((PROMPT, cols), F32),
            ((PROMPT, cols), BF), ((PROMPT, cols), BF), ((heads, 1, LINE), F32),
        ),
        [slab_t, slab_t, pltpu.VMEM((cont_count, cols, CONT_LEN), F32)]
        + [pltpu.VMEM((rows_late, cols), F32)] * 2 + [pltpu.VMEM((PROMPT, cols), F32)] * 2,
        (7,), rows_late * DIST, "cont_back",
    )
    lent = flip_bit(jnp.concatenate([dk_far, dv_far], axis=0), 0)
    dq_prompt, dk_prompt, dv_prompt, line_prompt = run_heads(
        prompt_back, heads, [], [line],
        [query_s, key_s, key_t, value_s, do_prompt, lse_prompt],
        shaped(
            ((PROMPT, cols), BF), ((PROMPT, cols), F32), ((PROMPT, cols), F32),
            ((heads, 1, LINE), F32),
        ),
        [slab_t, slab_t, pltpu.VMEM((cols, PROMPT), F32)], (3,),
        PROMPT * PROMPT * 5 // 8, "prompt_back",
    )
    dk_prompt = (dk_prompt + dk_near + lent[:PROMPT].astype(F32)).astype(BF)
    dv_prompt = (dv_prompt + dv_near + lent[PROMPT:].astype(F32)).astype(BF)

    def three(q, k, v):
        return mm(q, w_q, NT) + mm(k, w_k, NT) + mm(v, w_v, NT)

    def scatter_rows(block, rows):
        total = lax.dynamic_slice_in_dim(block, tensor_rank * rows, rows, 0).astype(F32)
        for step in range(1, ranks):
            dest = (tensor_rank + step) % ranks
            piece = lax.dynamic_slice_in_dim(block, dest * rows, rows, 0)
            total = total + to_ahead(piece, step).astype(F32)
        return total

    part_cont = three(dq_cont, dk_cont, dv_cont).astype(BF)
    part_prompt = three(dq_prompt, dk_prompt, dv_prompt).astype(BF)
    unit = stream * norm_scale(stream)
    gain_self_part = jnp.sum(part_prompt.astype(F32) * unit[:PROMPT], axis=0) + jnp.sum(
        part_cont.astype(F32) * unit[PROMPT:], axis=0
    )

    enc_part = mm(d_key_c, ck_t) + mm(d_value_c, cv_t)
    enc_sum = (enc_part[:ENC_LEN] + flip_bit(enc_part[ENC_LEN:].astype(BF), 0).astype(F32)).astype(
        BF
    )
    enc_rows = ENC_LEN // ranks
    enc_own = scatter_rows(enc_sum, enc_rows).astype(BF)
    enc_all = jnp.concatenate(
        [enc_own] + [from_ahead(enc_own, step) for step in range(1, ranks)]
    )
    enc_place = jnp.arange(ENC_LEN)
    enc_from = (tensor_rank + enc_place // enc_rows) % ranks * enc_rows + enc_place % enc_rows
    enc_hot = (enc_from[:, None] == enc_place[None, :]).astype(BF)
    grad_enc = mm(enc_hot, enc_all, TN)

    def by_rows(prompt_part, cont_part):
        return mm(prompt_part, n1[:PROMPT], TN) + mm(cont_part, n1[PROMPT:], TN)

    qkv_grads = [
        by_rows(dq_prompt, dq_cont).astype(BF),
        by_rows(dk_prompt, dk_cont).astype(BF),
        by_rows(dv_prompt, dv_cont).astype(BF),
    ]

    line_grad = (line_cont + line_prompt).reshape(heads, LINE)[:, :DIST]
    table_part = jnp.dot(line_grad, bucket_hot, precision=lax.Precision.HIGHEST)
    small = jnp.zeros((8, width), F32)
    small = small.at[0].set(gain_self_part).at[1].set(gain_cross_part).at[2].set(gain_ffn_part)
    small = small.at[3, 0].set(loss_part)
    small = small.at[4, : table_part.size].set(table_part.reshape(-1))

    totals, came, grouped, small = reduce_all(
        [a.reshape(ranks, hidden_here, width) for a in ffn_grads]
        + [a.reshape(ranks, cols, width) for a in attn_grads]
        + [a.reshape(1, cols, width) for a in qkv_grads],
        [part_prompt.reshape(ranks, share, width), part_cont.reshape(ranks, CONT_LEN, width)],
        small,
        bits,
    )
    totals = [total.astype(F32) for total in totals]
    grad_table = grouped[4, : table_part.size].reshape(table_part.shape).T

    def own_total(block, rows, others):
        total = lax.dynamic_slice_in_dim(block, tensor_rank * rows, rows, 0).astype(F32)
        return total + jnp.sum(others.astype(F32), axis=0)

    d_n1 = jnp.concatenate(
        [own_total(part_prompt, share, came[0]), own_total(part_cont, CONT_LEN, came[1])]
    )
    back1, ignored = norm_back(x_own, gain_self, d_n1)
    grad_x = g1 + back1
    return (
        y_all[:share],
        y_all[share:],
        grad_x[:share],
        grad_x[share:],
        grad_enc,
        small[0],
        small[1],
        small[2],
        grad_table,
        totals[8].T,
        totals[9].T,
        totals[10].T,
        totals[3],
        totals[4].T,
        totals[5].T,
        totals[6].T,
        totals[7],
        totals[0].T,
        totals[1].T,
        totals[2],
        small[3, 0] / token_count,
    )


def solution(mesh):
    rows = P("dp", None)
    both = P(("dp", "tensor"), None)
    columns = P(None, "tensor")
    shards = P("tensor", None)
    return jax.shard_map(
        on_device,
        mesh=mesh,
        in_specs=(
            (rows,) * 3 + (both,) * 3 + (P("dp"),) * 2 + (P(),) * 4 + (columns,) * 4
            + (shards,) + (columns,) * 3 + (shards,) + (columns,) * 2 + (shards,)
        ),
        out_specs=(
            (both,) * 4 + (rows,) + (P(),) * 3 + (columns,) * 4 + (shards,) + (columns,) * 3
            + (shards,) + (columns,) * 2 + (shards, P())
        ),
        check_vma=False,
    )
```

```python
import functools

import jax
import jax.numpy as jnp
from jax import lax
from jax.experimental import pallas as pl
from jax.experimental.pallas import tpu as pltpu
from jax.sharding import PartitionSpec as P

HEAD = 64
PROMPT = 1024
CONT_LEN = 128
ENC_LEN = 512
TILE = 128
DIST = PROMPT + CONT_LEN
LINE = DIST + 2 * TILE
SLAB = DIST + TILE

norm_eps = 1e-06
masked_value = -1e30
BF = jnp.bfloat16
F32 = jnp.float32
NT = (((1,), (1,)), ((), ()))
TN = (((0,), (0,)), ((), ()))
NN = (((1,), (0,)), ((), ()))


def mm(left, right, dims=NN):
    return lax.dot_general(left, right, dims, preferred_element_type=F32)


def from_ahead(block, step):
    count = lax.axis_size("tensor")
    return lax.ppermute(block, "tensor", [((i + step) % count, i) for i in range(count)])


def to_ahead(block, step):
    count = lax.axis_size("tensor")
    return lax.ppermute(block, "tensor", [(i, (i + step) % count) for i in range(count)])


def flip_bit(block, bit, axis="dp"):
    count = lax.axis_size(axis)
    return lax.ppermute(block, axis, [(i, i ^ (1 << bit)) for i in range(count)])


def norm_scale(values):
    return lax.rsqrt(jnp.mean(values * values, axis=-1, keepdims=True) + norm_eps)


def rms_norm(values, weight):
    return values * norm_scale(values) * weight


def norm_back(values, weight, grad):
    scale = norm_scale(values)
    unit = values * scale
    weighted = grad * weight
    inner = jnp.mean(weighted * unit, axis=-1, keepdims=True)
    return (scale * (weighted - unit * inner), jnp.sum(grad * unit, axis=0))


def make_slab(line):
    wide = jnp.broadcast_to(line, (TILE, LINE))
    return pltpu.roll(wide, LINE - (TILE - 1), 1, stride=1, stride_axis=0)[:, :SLAB]


def head_mask(head, width, dtype):
    lane = lax.broadcasted_iota(jnp.int32, (1, width), 1)
    return (lane // HEAD == head).astype(dtype)


def prompt_fwd(line_ref, q_ref, k_ref, v_ref, o_ref, lse_ref, slab):
    head = pl.program_id(0)
    slab[...] = make_slab(line_ref[0])
    width = q_ref.shape[1]
    mask = head_mask(head, width, BF)
    mask_f = head_mask(head, width, F32)

    @pl.when(head == 0)
    def _():
        o_ref[...] = jnp.zeros_like(o_ref)
        lse_ref[...] = jnp.zeros_like(lse_ref)

    vm = v_ref[0:PROMPT, :] * mask
    block = 2 * TILE
    for idx in range(PROMPT // block):
        keys = block * (idx + 1)
        rows = pl.ds(idx * block, block)
        q = q_ref[rows, :] * mask
        s = mm(q, k_ref[0:keys, :], NT)
        start = PROMPT - block * idx
        s = s + jnp.concatenate(
            [slab[:, start : start + keys], slab[:, start - TILE : start - TILE + keys]], axis=0
        )
        top = jnp.max(s, axis=-1, keepdims=True)
        e = jnp.exp(s - top)
        total = jnp.sum(e, axis=-1, keepdims=True)
        o = mm(e.astype(BF), vm[0:keys, :]) / total
        o_ref[rows, :] = o_ref[rows, :] + o.astype(BF)
        lse_ref[rows, :] = lse_ref[rows, :] + (top + jnp.log(total)) * mask_f


def cont_rows(slot):
    return pl.ds(slot * CONT_LEN, CONT_LEN)


def late_rows(slot):
    return pl.ds(PROMPT + slot * CONT_LEN, CONT_LEN)


def cont_fwd(
    line_ref, ok_ref, q_ref, k_ref, v_ref, kf_ref, vf_ref, o_ref, lse_ref, slab
):
    head = pl.program_id(0)
    slab[...] = make_slab(line_ref[0])
    width = q_ref.shape[1]
    mask = head_mask(head, width, BF)
    mask_f = head_mask(head, width, F32)

    @pl.when(head == 0)
    def _():
        o_ref[...] = jnp.zeros_like(o_ref)
        lse_ref[...] = jnp.zeros_like(lse_ref)

    for pair in range(2):
        keys_ref, values_ref = (k_ref, v_ref) if pair == 0 else (kf_ref, vf_ref)
        slots = [2 * pair, 2 * pair + 1]
        qs = [q_ref[late_rows(slot), :] * mask for slot in slots]
        s = mm(jnp.concatenate(qs, axis=0), keys_ref[0:PROMPT, :], NT)
        s = s + jnp.concatenate([slab[:, 0:PROMPT], slab[:, 0:PROMPT]], axis=0)
        own = jnp.concatenate(
            [
                mm(q, k_ref[late_rows(slot), :], NT) + slab[:, PROMPT:DIST] + ok_ref[slot]
                for q, slot in zip(qs, slots)
            ],
            axis=0,
        )
        top = jnp.maximum(
            jnp.max(s, axis=-1, keepdims=True), jnp.max(own, axis=-1, keepdims=True)
        )
        e = jnp.exp(s - top)
        e_own = jnp.exp(own - top)
        total = jnp.sum(e, axis=-1, keepdims=True) + jnp.sum(e_own, axis=-1, keepdims=True)
        o = mm(e.astype(BF), values_ref[0:PROMPT, :] * mask)
        low = e_own.astype(BF)
        o_own = [
            mm(low[CONT_LEN * i : CONT_LEN * (i + 1), :], v_ref[late_rows(slot), :] * mask)
            for i, slot in enumerate(slots)
        ]
        o = (o + jnp.concatenate(o_own, axis=0)) / total
        lse = (top + jnp.log(total)) * mask_f
        for i, slot in enumerate(slots):
            part = slice(CONT_LEN * i, CONT_LEN * (i + 1))
            o_ref[cont_rows(slot), :] = o_ref[cont_rows(slot), :] + o[part, :].astype(BF)
            lse_ref[cont_rows(slot), :] = lse_ref[cont_rows(slot), :] + lse[part, :]


def row_of(lse, head):
    width = lse.shape[1]
    lane = lax.broadcasted_iota(jnp.int32, (1, width), 1)
    column = jnp.sum(jnp.where(lane == head * HEAD, lse, 0.0), axis=-1, keepdims=True)
    return jnp.broadcast_to(column, (lse.shape[0], TILE)).T[0:1, :]


def fold_slab(block):
    rows = TILE
    block = jnp.concatenate([block, jnp.zeros((TILE, LINE - SLAB), F32)], axis=1)
    while rows > 8:
        rows //= 2
        block = pltpu.roll(block[:rows], rows, 1) + block[rows:]
    line = jnp.zeros((1, LINE), F32)
    for r in range(rows):
        line = line + pltpu.roll(block, rows - 1 - r, 1)[r : r + 1]
    return line


def cross_fwd(far_ref, q_ref, k_ref, v_ref, o_ref, lse_ref):
    rows = q_ref.shape[0] - CONT_LEN
    far = pl.ds(pl.multiple_of(far_ref[0] * ENC_LEN, ENC_LEN), ENC_LEN)
    for part, keys in ((pl.ds(0, rows), pl.ds(0, ENC_LEN)), (pl.ds(rows, CONT_LEN), far)):
        q = q_ref[part, :]
        k = k_ref[keys, :]
        v = v_ref[keys, :]
        o = 0.0
        lse = 0.0
        for head in range(2):
            mask = head_mask(head, TILE, BF)
            s = mm(q * mask, k, NT)
            top = jnp.max(s, axis=-1, keepdims=True)
            e = jnp.exp(s - top)
            total = jnp.sum(e, axis=-1, keepdims=True)
            o = o + mm(e.astype(BF), v * mask) / total
            lse = lse + (top + jnp.log(total)) * head_mask(head, TILE, F32)
        o_ref[part, :] = o.astype(BF)
        lse_ref[part, :] = lse


def cross_back(far_ref, q_ref, k_ref, v_ref, do_ref, lse_ref, dq_ref, dk_ref, dv_ref, dk, dv):
    rows = q_ref.shape[0] - CONT_LEN
    far = pl.ds(pl.multiple_of(far_ref[0] * ENC_LEN, ENC_LEN), ENC_LEN)
    dk[ENC_LEN : 2 * ENC_LEN, :] = jnp.zeros((ENC_LEN, TILE), F32)
    dv[ENC_LEN : 2 * ENC_LEN, :] = jnp.zeros((ENC_LEN, TILE), F32)
    for index, (part, keys) in enumerate(
        ((pl.ds(0, rows), pl.ds(0, ENC_LEN)), (pl.ds(rows, CONT_LEN), far))
    ):
        q = q_ref[part, :]
        k = k_ref[keys, :]
        kt = k.T
        v = v_ref[keys, :]
        do = do_ref[part, :]
        lse = lse_ref[part, :].T
        gk, gv = (0.0, 0.0)
        dq = []
        for head in range(2):
            mask = head_mask(head, TILE, BF)
            qm = q * mask
            dom = do * mask
            s = mm(k, qm, NT)
            p = jnp.exp(s - lse[HEAD * head : HEAD * head + 1, :])
            dp = mm(v, dom, NT)
            centre = jnp.sum(p * dp, axis=0, keepdims=True)
            low = (p * (dp - centre)).astype(BF)
            gv = gv + mm(p.astype(BF), dom)
            gk = gk + mm(low, qm)
            dq.append(mm(kt[HEAD * head : HEAD * (head + 1), :], low))
        dq_ref[part, :] = (jnp.concatenate(dq, axis=0).T * HEAD ** (-0.5)).astype(BF)
        if index == 0:
            dk[0:ENC_LEN, :] = gk
            dv[0:ENC_LEN, :] = gv
        else:
            dk[keys, :] = dk[keys, :] + gk
            dv[keys, :] = dv[keys, :] + gv
    dk_ref[...] = dk[...].astype(BF)
    dv_ref[...] = dv[...].astype(BF)


def whole(shape):
    return pl.BlockSpec(shape, lambda *_: (0,) * len(shape))


def by_head(shape):
    return pl.BlockSpec((1,) + shape[1:], lambda head, *_: (head,) + (0,) * (len(shape) - 1))


def cost(flops, transcendentals, arrays):
    return pl.CostEstimate(
        flops=int(flops),
        transcendentals=int(transcendentals),
        bytes_accessed=int(sum(a.size * a.dtype.itemsize for a in arrays)),
    )


def shaped(*pairs):
    return [jax.ShapeDtypeStruct(shape, dtype) for shape, dtype in pairs]


MESH = pl.DeviceIdType.MESH


class Links:
    def __init__(self, sends, receives, local, bits):
        self.sends, self.receives, self.local_sems = sends, receives, local
        self.used = 0
        self.used_local = 0
        self.bits = bits
        self.data = lax.axis_index("dp")
        self.tensor = lax.axis_index("tensor")
        self.ranks = lax.axis_size("tensor")

    def bit(self, index):
        return self.data // (1 << index) % 2

    def partner(self, index):
        return (self.data + (1 << index) * (1 - 2 * self.bit(index)), self.tensor)

    def ahead(self, step):
        return (self.data, (self.tensor + step) % self.ranks)

    def across(self, index):
        here = self.tensor // (1 << index) % 2
        return (self.data, self.tensor + (1 << index) * (1 - 2 * here))

    def barrier(self):
        sem = pltpu.get_barrier_semaphore()
        others = [self.partner(index) for index in range(self.bits)]
        others += [self.ahead(step) for step in range(1, self.ranks)]
        for other in others:
            pl.semaphore_signal(sem, inc=1, device_id=other, device_id_type=MESH)
        pl.semaphore_wait(sem, len(others))

    def send(self, source, target, device):
        copy = pltpu.make_async_remote_copy(
            src_ref=source,
            dst_ref=target,
            send_sem=self.sends.at[self.used],
            recv_sem=self.receives.at[self.used],
            device_id=device,
            device_id_type=MESH,
        )
        self.used += 1
        copy.start()
        return copy

    def local(self, source, target):
        copy = pltpu.make_async_copy(source, target, self.local_sems.at[self.used_local])
        self.used_local += 1
        copy.start()
        return copy


def span(start, size, step):
    return pl.ds(pl.multiple_of(start, step), size)


def bit_order(place):
    return (1, 2) if place % 2 == 0 else (2, 1)


def split_chunks(sizes, unit):
    chunks = []
    for index, rows in enumerate(sizes):
        step = rows
        while step > unit:
            step //= 2
        chunks += [(index, start, step) for start in range(0, rows, step)]
    return chunks


def gather_stream(links, own, full, stage, first, rows, place):
    one, two = bit_order(place)
    width = own.shape[1]
    half = width // 2
    cols = span(links.bit(0) * half, half, 128)
    base = first + links.bit(one) * (rows // 2)
    quarter = span(base + links.bit(two) * (rows // 4), rows // 4, 16)
    mine = links.local(own.at[pl.ds(first, rows), :], stage)
    ranks = links.ranks
    copies = [
        links.send(own.at[quarter, cols], full.at[ranks - step, quarter, cols], links.ahead(step))
        for step in range(1, ranks)
    ]
    yield
    mine.wait()
    home = links.local(stage, full.at[0, pl.ds(first, rows), :])
    for copy in copies:
        copy.wait()
    others = pl.ds(1, ranks - 1)
    part = full.at[others, quarter, cols]
    copy = links.send(part, part, links.partner(two))
    yield
    copy.wait()
    part = full.at[others, span(base, rows // 2, 16), cols]
    copy = links.send(part, part, links.partner(one))
    yield
    copy.wait()
    part = full.at[others, pl.ds(first, rows), cols]
    copy = links.send(part, part, links.partner(0))
    yield
    copy.wait()
    home.wait()


def gather_kernel(count, bits, chunks, *refs):
    own, full = refs[:count], refs[count : 2 * count]
    scratch = refs[2 * count :]
    stages, (sends, receives, local) = scratch[:-3], scratch[-3:]
    links = Links(sends, receives, local, bits)
    links.barrier()
    streams = [
        gather_stream(links, own[index], full[index], stages[place], first, rows, place)
        for place, (index, first, rows) in enumerate(chunks)
    ]
    for ignored in pair_steps(streams, 4):
        pass


def gather_all(own, bits):
    ranks = lax.axis_size("tensor")
    chunks = split_chunks([a.shape[0] for a in own], 256)
    any_space = pl.BlockSpec(memory_space=pl.ANY)
    copies = len(chunks) * (ranks + 2)
    return pl.pallas_call(
        functools.partial(gather_kernel, len(own), bits, chunks),
        out_shape=[jax.ShapeDtypeStruct((ranks,) + a.shape, a.dtype) for a in own],
        in_specs=[any_space] * len(own),
        out_specs=[any_space] * len(own),
        scratch_shapes=[pltpu.VMEM((rows, own[0].shape[1]), BF) for _, _, rows in chunks]
        + [
            pltpu.SemaphoreType.DMA((copies,)),
            pltpu.SemaphoreType.DMA((copies,)),
            pltpu.SemaphoreType.DMA((2 * len(chunks),)),
        ],
        compiler_params=pltpu.CompilerParams(
            collective_id=1, has_side_effects=True, vmem_limit_bytes=60 * 2**20
        ),
        name="gather_all",
    )(*own)


CORE_ROOMS = 8


def flip_rank(rank, bits):
    for bit in bits:
        rank = rank + bit * (1 - 2 * (rank // bit % 2))
    return rank


def pair_steps(streams, stages):
    pairs = [streams[i : i + 2] for i in range(0, len(streams), 2)]
    for step in range(len(pairs) + stages):
        for index in reversed(range(len(pairs))):
            if 0 <= step - index <= stages:
                for stream in pairs[index]:
                    next(stream, None)
        yield


def reduce_stream(links, grad, total, core_room, room, first, rows, place, slabs):
    mine, from_one, from_two, from_far, from_more = room
    from_core = core_room.at[pl.ds(0, slabs), pl.ds(0, rows), :]
    one, two = bit_order(place)
    half = grad.shape[2] // 2
    whole_rows = pl.ds(first, rows)
    here = span(links.bit(0) * half, half, 128)
    there = span((1 - links.bit(0)) * half, half, 128)
    kept = links.local(grad.at[:, whole_rows, here], mine)
    copy = links.send(grad.at[:, whole_rows, there], from_core, links.partner(0))
    yield
    kept.wait()
    copy.wait()
    mine[...] = mine[...] + from_core[...]
    base = links.bit(one) * (rows // 2)
    given = (1 - links.bit(one)) * (rows // 2)
    copy = links.send(
        mine.at[:, span(given, rows // 2, 16), :], from_one, links.partner(one)
    )
    yield
    copy.wait()
    keep = span(base, rows // 2, 16)
    mine[:, keep, :] = mine[:, keep, :] + from_one[...]
    given = base + (1 - links.bit(two)) * (rows // 4)
    base_two = base + links.bit(two) * (rows // 4)
    copy = links.send(
        mine.at[:, span(given, rows // 4, 16), :], from_two, links.partner(two)
    )
    yield
    copy.wait()
    keep = span(base_two, rows // 4, 16)
    if slabs > 1:
        mine[:, keep, :] = mine[:, keep, :] + from_two[...]
        slab = [
            (flip_rank(links.tensor, flips) - links.tensor + slabs) % slabs
            for flips in ((), (1,), (2,), (1, 2))
        ]
        copies = [
            links.send(mine.at[slab[1], keep, :], from_far.at[0], links.across(0)),
            links.send(mine.at[slab[3], keep, :], from_far.at[1], links.across(0)),
        ]
        yield
        for copy in copies:
            copy.wait()
        mine[slab[2], keep, :] = mine[slab[2], keep, :] + from_far[1]
        copy = links.send(mine.at[slab[2], keep, :], from_far.at[2], links.across(1))
        yield
        copy.wait()
        value = mine[0, keep, :].astype(F32) + from_far[0].astype(F32)
        value = (value + from_far[2].astype(F32)).astype(BF)
    else:
        value = mine[0, keep, :] + from_two[0]
    quarter = span(first + base_two, rows // 4, 16)
    for index in range(3, links.bits):
        total[quarter, here] = value
        copy = links.send(
            total.at[quarter, here], from_more.at[index - 3], links.partner(index)
        )
        copy.wait()
        value = value + from_more[index - 3]
    total[quarter, here] = value
    copy = links.send(total.at[quarter, here], total.at[quarter, here], links.partner(two))
    yield
    copy.wait()
    part = total.at[span(first + base, rows // 2, 16), here]
    copy = links.send(part, part, links.partner(one))
    yield
    copy.wait()
    part = total.at[whole_rows, here]
    copy = links.send(part, part, links.partner(0))
    yield
    copy.wait()


def small_stream(links, held, came, grouped, final):
    tensor_bits = links.ranks.bit_length() - 1
    for index in range(links.bits + tensor_bits):
        device = links.partner(index) if index < links.bits else links.across(index - links.bits)
        copy = links.send(held.at[index], came.at[index], device)
        yield
        copy.wait()
        value = held[index] + came[index]
        held[index + 1] = value
        if index == links.bits - 1:
            grouped[...] = value
    final[...] = value


def rows_stream(links, parts, came, out, rows):
    copy = links.send(
        parts.at[pl.ds(2, 2), rows, :], came.at[pl.ds(0, 2), rows, :], links.across(0)
    )
    yield
    copy.wait()
    parts[1, rows, :] = parts[1, rows, :] + came[1, rows, :]
    copy = links.send(parts.at[1, rows, :], came.at[2, rows, :], links.across(1))
    yield
    copy.wait()
    out[rows, :] = (
        parts[0, rows, :].astype(F32) + came[0, rows, :].astype(F32) + came[2, rows, :].astype(F32)
    )


def rows_streams(links, parts, came, out, pieces):
    size = out.shape[0] // pieces
    active = []
    for piece in range(pieces + 2):
        if piece < pieces:
            active.append(rows_stream(links, parts, came, out, pl.ds(piece * size, size)))
        for stream in reversed(active):
            next(stream, None)
        yield


def encoder_stream(links, enc, from_core, total, came, final):
    count = from_core.shape[0]
    here = [flip_rank(links.tensor, flips) for flips in ((), (1,), (2,), (1, 2))]
    kept = links.local(enc.at[pl.ds(0, count)], total)
    copy = links.send(enc.at[pl.ds(count, count)], from_core, links.partner(0))
    yield
    kept.wait()
    copy.wait()
    total[...] = total[...] + from_core[...]
    copies = [
        links.send(total.at[here[1]], came.at[0], links.across(0)),
        links.send(total.at[here[3]], came.at[1], links.across(0)),
    ]
    yield
    for copy in copies:
        copy.wait()
    total[here[2]] = total[here[2]] + came[1]
    copy = links.send(total.at[here[2]], came.at[2], links.across(1))
    yield
    copy.wait()
    value = total[here[0]].astype(F32) + came[0].astype(F32) + came[2].astype(F32)
    final[here[0]] = value.astype(BF)
    copies = [links.send(final.at[here[0]], final.at[here[0]], links.across(1))]
    yield
    copies[0].wait()
    copies = [
        links.send(final.at[place], final.at[place], links.across(0))
        for place in (here[0], here[2])
    ]
    yield
    for copy in copies:
        copy.wait()


def attend_back(ins, work, heads):
    line_ref, ok_ref, q_ref, k_ref, v_ref, kt_ref, kf_ref, vf_ref, ktf_ref, lse_ref, late_ref = ins
    do_ref, do_late, slab, gslab, dqt, dqc, dk, dv, dkc, dvc, dkf, dvf, held = work
    width = q_ref.shape[1]
    block = 2 * TILE
    for ref in (dk, dv, dkf, dvf, dkc, dvc):
        ref[...] = jnp.zeros_like(ref)
    for head in range(heads):
        slab[...] = make_slab(line_ref[head]).T
        gslab[...] = jnp.zeros_like(gslab)
        mask = head_mask(head, width, BF)
        mine = pl.ds(head * HEAD, HEAD)
        for pair in range(2):
            keys_ref, kt, values_ref = (
                (k_ref, kt_ref, v_ref) if pair == 0 else (kf_ref, ktf_ref, vf_ref)
            )
            gk, gv = (dk, dv) if pair == 0 else (dkf, dvf)
            slots = [2 * pair, 2 * pair + 1]
            qs = [q_ref[late_rows(slot), :] * mask for slot in slots]
            dos = [do_late[slot] * mask for slot in slots]
            q = jnp.concatenate(qs, axis=0)
            do = jnp.concatenate(dos, axis=0)
            lse = row_of(
                jnp.concatenate([late_ref[cont_rows(slot), :] for slot in slots], axis=0), head
            )
            s = mm(keys_ref[0:PROMPT, :], q, NT)
            s = s + jnp.concatenate([slab[0:PROMPT, :], slab[0:PROMPT, :]], axis=1)
            keys_own = [k_ref[late_rows(slot), :] for slot in slots]
            own = jnp.concatenate(
                [
                    mm(keys, qc, NT) + slab[PROMPT:DIST, :] + ok_ref[slot]
                    for keys, qc, slot in zip(keys_own, qs, slots)
                ],
                axis=1,
            )
            p = jnp.exp(s - lse)
            p_own = jnp.exp(own - lse)
            dp = mm(values_ref[0:PROMPT, :], do, NT)
            dp_own = jnp.concatenate(
                [mm(v_ref[late_rows(slot), :], doc, NT) for doc, slot in zip(dos, slots)], axis=1
            )
            centre = jnp.sum(p * dp, axis=0, keepdims=True) + jnp.sum(
                p_own * dp_own, axis=0, keepdims=True
            )
            ds = p * (dp - centre)
            ds_own = p_own * (dp_own - centre)
            low = ds.astype(BF)
            low_own = ds_own.astype(BF)
            p_low = p_own.astype(BF)
            gv[...] = gv[...] + mm(p.astype(BF), do)
            gk[...] = gk[...] + mm(low, q)
            dq = mm(kt[mine, 0:PROMPT], low)
            for i in range(2):
                part = slice(CONT_LEN * i, CONT_LEN * (i + 1))
                spot = 2 * pair + i
                here = pl.ds(spot * CONT_LEN, CONT_LEN)
                dvc[here, :] = dvc[here, :] + mm(p_low[:, part], dos[i])
                dkc[here, :] = dkc[here, :] + mm(low_own[:, part], qs[i])
                head_keys = keys_own[i].T[head * HEAD : (head + 1) * HEAD, :]
                dqc[spot, mine, :] = dq[:, part] + mm(head_keys, low_own[:, part])
                gslab[0:PROMPT, :] = gslab[0:PROMPT, :] + ds[:, part]
                gslab[PROMPT:DIST, :] = gslab[PROMPT:DIST, :] + ds_own[:, part]
            yield
        for idx in range(PROMPT // block):
            keys = block * (idx + 1)
            rows = pl.ds(idx * block, block)
            q = q_ref[rows, :] * mask
            do = do_ref[idx, pl.ds(0, block), :] * mask
            s = mm(k_ref[0:keys, :], q, NT)
            start = PROMPT - block * idx
            s = s + jnp.concatenate(
                [slab[start : start + keys, :], slab[start - TILE : start - TILE + keys, :]],
                axis=1,
            )
            p = jnp.exp(s - row_of(lse_ref[rows, :], head))
            dp = mm(v_ref[0:keys, :], do, NT)
            centre = jnp.sum(p * dp, axis=0, keepdims=True)
            ds = p * (dp - centre)
            low = ds.astype(BF)
            dv[0:keys, :] = dv[0:keys, :] + mm(p.astype(BF), do)
            dk[0:keys, :] = dk[0:keys, :] + mm(low, q)
            dqt[mine, rows] = mm(kt_ref[mine, 0:keys], low)
            gslab[start : start + keys, :] = gslab[start : start + keys, :] + ds[:, 0:TILE]
            gslab[start - TILE : start - TILE + keys, :] = (
                gslab[start - TILE : start - TILE + keys, :] + ds[:, TILE:block]
            )
            yield
        held[0, pl.ds(4 + head, 1), :] = fold_slab(gslab[...].T)


def reduce_kernel(count, bits, chunks, heads, pace, *refs):
    refs = list(refs)

    def take(number):
        taken, refs[:number] = refs[:number], []
        return taken

    (hot_ref,) = take(1)
    ins = take(11)
    n1_ref, unit_ref, wq_ref, wk_ref, wv_ref, small_ref, do_in, enc_in = take(8)
    grads = take(count)
    totals = take(count + 3)
    enc_final, out, grouped, final = take(4)
    do_ref, do_late, slab, gslab, dqt, dqc, dk, dv, dkc, dvc, dkf, dvf = take(12)
    lent_out, lent_in, dq_all, dk_all, dv_all, parts, came_rows = take(7)
    grads = grads + take(3)
    held, came, enc_core, enc_total, enc_came = take(5)
    core_rooms = take(CORE_ROOMS)
    sends, receives, local = refs[-3:]
    rooms = [refs[5 * i : 5 * i + 5] for i in range(len(chunks))]
    links = Links(sends, receives, local, bits)
    links.barrier()
    ranks = links.ranks
    width = n1_ref.shape[1]
    moved = [
        links.send(do_in.at[step], do_ref.at[links.tensor], links.ahead(step))
        for step in range(1, ranks)
    ]
    stay = links.local(do_in.at[0], do_ref.at[links.tensor])
    streams = [
        reduce_stream(
            links, grads[index], totals[index], core_rooms[place % CORE_ROOMS], rooms[place], first,
            rows, place, grads[index].shape[0],
        )
        for place, (index, first, rows) in enumerate(chunks)
    ]
    encoder = encoder_stream(links, enc_in, enc_core, enc_total, enc_came, enc_final)
    pairs = pair_steps(streams, 8)

    def steps():
        for ignored in pairs:
            next(encoder, None)
            yield

    comm = steps()
    next(comm)
    next(comm)
    next(comm)
    held[0] = small_ref[...]
    stay.wait()
    for copy in moved:
        copy.wait()
    conts = dqc.shape[0]
    share = PROMPT // ranks
    for i in range(conts):
        value = 0.0
        for cont in range(conts):
            late = do_ref[cont, pl.ds(share, CONT_LEN), :].astype(F32)
            value = value + late * hot_ref[cont, i][0:1, 0:1]
        do_late[i] = value.astype(BF)
    work = (do_ref, do_late, slab, gslab, dqt, dqc, dk, dv, dkc, dvc, dkf, dvf, held)
    for number, ignored in enumerate(attend_back(ins, work, heads)):
        if number % pace == pace - 1:
            next(comm)

    lent_out[0] = dkf[...].astype(BF)
    lent_out[1] = dvf[...].astype(BF)
    lent = links.send(lent_out, lent_in, links.partner(0))
    dq_all[0:PROMPT, :] = (dqt[...].T * HEAD ** (-0.5)).astype(BF)
    for i in range(conts):
        here = late_rows(i)
        spot = cont_rows(i)
        dq_all[here, :] = (dqc[i].T * HEAD ** (-0.5)).astype(BF)
        dk_all[here, :] = dkc[spot, :].astype(BF)
        dv_all[here, :] = dvc[spot, :].astype(BF)
    lent.wait()
    dk_all[0:PROMPT, :] = (dk[...] + lent_in[0].astype(F32)).astype(BF)
    dv_all[0:PROMPT, :] = (dv[...] + lent_in[1].astype(F32)).astype(BF)
    gain = jnp.zeros((1, width), F32)

    def input_grad(rows):
        value = (
            mm(dq_all[rows, :], wq_ref[...], NT)
            + mm(dk_all[rows, :], wk_ref[...], NT)
            + mm(dv_all[rows, :], wv_ref[...], NT)
        )
        return value, jnp.sum(value * unit_ref[rows, :].astype(F32), axis=0, keepdims=True)

    late = []
    for i in range(conts):
        value, term = input_grad(late_rows(i))
        late.append(value)
        gain = gain + term
    for place, flips in ((2, (1,)), (3, (1, 2)), (1, (2,)), (0, ())):
        rank = flip_rank(links.tensor, flips)
        value, term = input_grad(span(rank * share, share, 16))
        gain = gain + term
        parts[place, pl.ds(0, share), :] = value.astype(BF)
        total = 0.0
        for i in range(conts):
            total = total + late[i] * hot_ref[rank, i][0:1, 0:1]
        parts[place, pl.ds(share, CONT_LEN), :] = total.astype(BF)
    held[0, 0:1, 0:width] = gain
    extras = [
        rows_streams(links, parts, came_rows, out, 8),
        small_stream(links, held, came, grouped, final),
    ]
    for stream in extras:
        next(stream)
    for index, whole_ref in enumerate((dq_all, dk_all, dv_all)):
        grads[count + index][0] = mm(whole_ref[...], n1_ref[...], TN).astype(BF)
    for ignored in comm:
        for stream in extras:
            next(stream, None)
    for stream in extras:
        for ignored in stream:
            pass


def reduce_all(hot, ins, mats, small, do_in, enc, grads, bits, heads, pace):
    ranks = lax.axis_size("tensor")
    width = mats[0].shape[1]
    cols = heads * HEAD
    half = width // 2
    chunks = split_chunks([a.shape[1] for a in grads], 200)
    chunks += [(len(grads) + i, 0, cols) for i in range(3)]
    more = max(bits - 3, 1)
    conts = hot.shape[0]
    late = conts * CONT_LEN
    own = PROMPT // ranks + CONT_LEN
    rooms = []
    for index, _, rows in chunks:
        slabs = grads[index].shape[0] if index < len(grads) else 1
        rooms += [
            pltpu.VMEM((slabs, rows, half), BF),
            pltpu.VMEM((slabs, rows // 2, half), BF),
            pltpu.VMEM((slabs, rows // 4, half), BF),
            pltpu.VMEM((3, rows // 4, half), BF),
            pltpu.VMEM((more, rows // 4, half), BF),
        ]
    small_steps = bits + ranks.bit_length() - 1
    copies = len(chunks) * (9 + bits - 3) + small_steps + ranks + 24
    enc_block = (enc.shape[1], width)
    any_space = pl.BlockSpec(memory_space=pl.ANY)
    vmem = pl.BlockSpec(memory_space=pltpu.VMEM)
    out = pl.pallas_call(
        functools.partial(reduce_kernel, len(grads), bits, chunks, heads, pace),
        out_shape=shaped(
            *[(a.shape[1:], BF) for a in grads],
            *[((cols, width), BF)] * 3,
            ((ranks,) + enc_block, BF),
            ((own, width), F32),
            (small.shape, F32),
            (small.shape, F32),
        ),
        in_specs=[vmem] * (len(ins) + len(mats) + 2)
        + [any_space] * (2 + len(grads)),
        out_specs=[vmem] * (len(grads) + 7),
        scratch_shapes=[
            pltpu.VMEM(do_in.shape, BF),
            pltpu.VMEM((conts, CONT_LEN, cols), BF),
            pltpu.VMEM((SLAB, TILE), F32),
            pltpu.VMEM((SLAB, TILE), F32),
            pltpu.VMEM((cols, PROMPT), F32),
            pltpu.VMEM((conts, cols, CONT_LEN), F32),
            pltpu.VMEM((PROMPT, cols), F32),
            pltpu.VMEM((PROMPT, cols), F32),
            pltpu.VMEM((late, cols), F32),
            pltpu.VMEM((late, cols), F32),
            pltpu.VMEM((PROMPT, cols), F32),
            pltpu.VMEM((PROMPT, cols), F32),
            pltpu.VMEM((2, PROMPT, cols), BF),
            pltpu.VMEM((2, PROMPT, cols), BF),
            pltpu.VMEM((PROMPT + late, cols), BF),
            pltpu.VMEM((PROMPT + late, cols), BF),
            pltpu.VMEM((PROMPT + late, cols), BF),
            pltpu.VMEM((ranks, own, width), BF),
            pltpu.VMEM((ranks - 1, own, width), BF),
            pltpu.VMEM((1, cols, width), BF),
            pltpu.VMEM((1, cols, width), BF),
            pltpu.VMEM((1, cols, width), BF),
            pltpu.VMEM((small_steps + 1,) + small.shape, F32),
            pltpu.VMEM((small_steps,) + small.shape, F32),
            pltpu.VMEM((ranks,) + enc_block, BF),
            pltpu.VMEM((ranks,) + enc_block, BF),
            pltpu.VMEM((ranks - 1,) + enc_block, BF),
        ]
        + [pltpu.VMEM((ranks, max(c[2] for c in chunks), half), BF)] * CORE_ROOMS
        + rooms
        + [
            pltpu.SemaphoreType.DMA((copies,)),
            pltpu.SemaphoreType.DMA((copies,)),
            pltpu.SemaphoreType.DMA((len(chunks) + 2,)),
        ],
        compiler_params=pltpu.CompilerParams(
            collective_id=2, has_side_effects=True, vmem_limit_bytes=67043328
        ),
        name="reduce_all",
    )(hot, *ins, *mats, small, do_in, enc, *grads)
    return out[: len(grads) + 3], out[-4], out[-3], out[-2], out[-1]


def run_heads(kernel, heads, scalars, lines, arrays, outs, scratch, out_heads, cells, name):
    in_specs = [by_head(a.shape) for a in lines] + [whole(a.shape) for a in arrays]
    out_specs = [
        by_head(o.shape) if i in out_heads else whole(o.shape) for i, o in enumerate(outs)
    ]
    return pl.pallas_call(
        kernel,
        out_shape=outs,
        grid_spec=pltpu.PrefetchScalarGridSpec(
            num_scalar_prefetch=len(scalars),
            grid=(heads,),
            in_specs=in_specs,
            out_specs=out_specs,
            scratch_shapes=scratch,
        ),
        compiler_params=pltpu.CompilerParams(dimension_semantics=("arbitrary",)),
        cost_estimate=cost(
            cells * heads * 256 * 2 * (2 if not out_heads else 5), cells * heads,
            list(lines) + list(arrays) + list(outs),
        ),
        name=name,
    )(*scalars, *lines, *arrays)


def on_device(
    x_prompt,
    x_cont,
    enc_out,
    cot_prompt,
    cot_cont,
    teacher,
    valid,
    prompt_of,
    buckets,
    gain_self,
    gain_cross,
    gain_ffn,
    rel_table,
    w_q,
    w_k,
    w_v,
    w_o,
    c_q,
    c_k,
    c_v,
    c_o,
    w_gate,
    w_up,
    w_down,
):
    width = x_prompt.shape[1]
    cont_count = prompt_of.shape[0]
    heads = w_q.shape[1] // HEAD
    cols = heads * HEAD
    hidden_here = w_gate.shape[1]
    ranks = lax.axis_size("tensor")
    data_size = lax.axis_size("dp")
    share = PROMPT // ranks
    tensor_rank = lax.axis_index("tensor")
    data_rank = lax.axis_index("dp")
    factor = HEAD ** (-0.5)
    bits = data_size.bit_length() - 1

    far = (prompt_of != data_rank).astype(jnp.int32)
    index = jnp.arange(cont_count, dtype=jnp.int32)
    before = index[None, :] < index[:, None]
    near_rank = jnp.sum(jnp.where(before, 1 - far[None, :], 0), axis=1)
    far_rank = jnp.sum(jnp.where(before, far[None, :], 0), axis=1)
    spot = jnp.where(far == 0, near_rank, cont_count // 2 + far_rank)
    slots = jnp.sum(jnp.where(spot[None, :] == index[:, None], index[None, :], 0), axis=1)
    hot = jnp.broadcast_to(
        (spot[:, None] == index[None, :]).astype(F32)[:, :, None, None],
        (cont_count, cont_count, 8, 128),
    )

    def by_place(rows):
        return jnp.concatenate(
            [
                lax.dynamic_slice_in_dim(rows, slots[i] * CONT_LEN, CONT_LEN, 0)
                for i in range(cont_count)
            ]
        )

    far_here = lax.dynamic_slice_in_dim(far, tensor_rank, 1, 0)

    def own_rows(prompt_rows, conts):
        return jnp.concatenate(
            [
                lax.dynamic_slice_in_dim(prompt_rows, tensor_rank * share, share, 0),
                lax.dynamic_slice_in_dim(conts, tensor_rank * CONT_LEN, CONT_LEN, 0),
            ]
        )

    enc_far = flip_bit(enc_out, 0)
    wo_all, cq_all, ck_all, cv_all, co_all, wg_all, wu_all, wd_all = gather_all(
        [w_o, c_q.T, c_k.T, c_v.T, c_o, w_gate.T, w_up.T, w_down], bits
    )

    count = jnp.broadcast_to(jnp.sum(valid.astype(F32)), (8, 128))
    for bit in range(bits):
        count = count + flip_bit(count, bit)
    token_count = count[0, 0]

    bucket_hot = (buckets[::-1][:, None] == jnp.arange(rel_table.shape[0])[None, :]).astype(F32)
    table = jnp.dot(bucket_hot, rel_table, precision=lax.Precision.HIGHEST).T
    line = jnp.concatenate(
        [table, jnp.full((heads, LINE - DIST), masked_value, F32)], axis=1
    ).reshape(heads, 1, LINE)
    ok = jnp.where(by_place(valid) > 0, 0.0, masked_value).astype(F32)
    ok_rows = jnp.broadcast_to(
        ok.reshape(cont_count, 1, CONT_LEN), (cont_count, CONT_LEN, CONT_LEN)
    )
    ok_cols = jnp.broadcast_to(
        ok.reshape(cont_count, CONT_LEN, 1), (cont_count, CONT_LEN, CONT_LEN)
    )

    stream = jnp.concatenate([x_prompt, by_place(x_cont)]).astype(F32)
    n1 = rms_norm(stream, gain_self).astype(BF)
    key_s = mm(n1, w_k).astype(BF)
    value_s = mm(n1, w_v).astype(BF)
    query_s = (mm(n1, w_q).astype(F32) * factor).astype(BF)
    key_t = mm(w_k, n1, (((0,), (1,)), ((), ()))).astype(BF)
    pair_far = flip_bit(
        jnp.concatenate([key_s[:PROMPT], value_s[:PROMPT]], axis=0), 0
    )
    key_far, value_far = pair_far[:PROMPT], pair_far[PROMPT:]
    rows_all = query_s.shape[0]
    rows_late = rows_all - PROMPT
    slab = pltpu.VMEM((TILE, SLAB), F32)
    slab_t = pltpu.VMEM((SLAB, TILE), F32)
    o_prompt, lse_prompt = run_heads(
        prompt_fwd, heads, [], [line], [query_s, key_s, value_s],
        shaped(((PROMPT, cols), BF), ((PROMPT, cols), F32)), [slab], (),
        PROMPT * PROMPT * 5 // 8, "prompt_fwd",
    )
    o_cont, lse_cont = run_heads(
        cont_fwd, heads, [], [line], [ok_rows, query_s, key_s, value_s, key_far, value_far],
        shaped(((rows_late, cols), BF), ((rows_late, cols), F32)), [slab], (),
        rows_late * DIST, "cont_fwd",
    )

    def heads_to_rows(block, rows, places):
        out = []
        for step in range(ranks):
            dest = (tensor_rank - step + ranks) % ranks
            piece = lax.dynamic_slice_in_dim(block, places[dest] * rows, rows, 0)
            out.append(piece if step == 0 else from_ahead(piece, step))
        return jnp.concatenate(out, axis=1)

    mixed_self = jnp.concatenate(
        [heads_to_rows(o_prompt, share, index), heads_to_rows(o_cont, CONT_LEN, spot)]
    )

    wo_full, cq_t, ck_t, cv_t, co_full = (
        a.reshape(ranks * cols, width) for a in (wo_all, cq_all, ck_all, cv_all, co_all)
    )
    x_own = own_rows(x_prompt, x_cont).astype(F32)
    x1 = x_own + mm(mixed_self, wo_full)
    n2 = rms_norm(x1, gain_cross).astype(BF)
    query_c = (mm(n2, cq_t, NT) * factor).astype(BF)
    enc_pair = jnp.concatenate([enc_out, enc_far])
    key_c = mm(enc_pair, ck_t, NT).astype(BF)
    value_c = mm(enc_pair, cv_t, NT).astype(BF)
    own_count = query_c.shape[0]
    pairs = query_c.shape[1] // TILE

    def columns(rows):
        return pl.BlockSpec((rows, TILE), lambda i, *_: (0, i))

    cross_cells = own_count * ENC_LEN * pairs * 2
    mixed_cross, lse_cross = pl.pallas_call(
        cross_fwd,
        out_shape=shaped(((own_count, pairs * TILE), BF), ((own_count, pairs * TILE), F32)),
        grid_spec=pltpu.PrefetchScalarGridSpec(
            num_scalar_prefetch=1,
            grid=(pairs,),
            in_specs=[columns(own_count), columns(2 * ENC_LEN), columns(2 * ENC_LEN)],
            out_specs=[columns(own_count), columns(own_count)],
        ),
        compiler_params=pltpu.CompilerParams(dimension_semantics=("arbitrary",)),
        cost_estimate=cost(cross_cells * 256 * 2 * 2, cross_cells, [query_c, key_c, value_c]),
        name="cross_fwd",
    )(far_here, query_c, key_c, value_c)
    x2 = x1 + mm(mixed_cross, co_full)
    n3 = rms_norm(x2, gain_ffn).astype(BF)
    wg_t, wu_t, wd = (a.reshape(ranks * hidden_here, width) for a in (wg_all, wu_all, wd_all))
    gate_pre = mm(n3, wg_t, NT)
    upper = mm(n3, wu_t, NT)
    hidden, gelu_pull = jax.vjp(
        lambda first_in, second_in: jax.nn.gelu(first_in, approximate=True) * second_in,
        gate_pre,
        upper,
    )
    hidden = hidden.astype(BF)
    x3 = x2 + mm(hidden, wd)
    valid_own = lax.dynamic_slice_in_dim(valid, tensor_rank * CONT_LEN, CONT_LEN, 0).astype(F32)[
        :, None
    ]
    deviation = x3[share:] - teacher.astype(F32)
    loss_part = jnp.sum(valid_own * deviation * deviation)
    g3 = jnp.concatenate(
        [
            cot_prompt.astype(F32),
            cot_cont.astype(F32) + 2.0 * valid_own * deviation / token_count,
        ]
    )
    y_all = x3.astype(BF)

    g3_low = g3.astype(BF)
    d_hidden = mm(g3_low, wd, NT).astype(BF).astype(F32)
    d_gate, d_upper = gelu_pull(d_hidden)
    d_gate = d_gate.astype(BF)
    d_upper = d_upper.astype(BF)
    ffn_grads = [
        mm(d_gate, n3, TN).astype(BF),
        mm(d_upper, n3, TN).astype(BF),
        mm(hidden, g3_low, TN).astype(BF),
    ]
    d_n3 = mm(d_gate, wg_t) + mm(d_upper, wu_t)
    back3, gain_ffn_part = norm_back(x2, gain_ffn, d_n3)
    g2 = g3 + back3

    g2_low = g2.astype(BF)
    d_mixed_c = mm(g2_low, co_full, NT).astype(BF)
    d_query_c, d_key_c, d_value_c = pl.pallas_call(
        cross_back,
        out_shape=shaped(
            ((own_count, pairs * TILE), BF),
            ((2 * ENC_LEN, pairs * TILE), BF),
            ((2 * ENC_LEN, pairs * TILE), BF),
        ),
        grid_spec=pltpu.PrefetchScalarGridSpec(
            num_scalar_prefetch=1,
            grid=(pairs,),
            in_specs=[
                columns(own_count), columns(2 * ENC_LEN), columns(2 * ENC_LEN),
                columns(own_count), columns(own_count),
            ],
            out_specs=[columns(own_count), columns(2 * ENC_LEN), columns(2 * ENC_LEN)],
            scratch_shapes=[pltpu.VMEM((2 * ENC_LEN, TILE), F32)] * 2,
        ),
        compiler_params=pltpu.CompilerParams(dimension_semantics=("arbitrary",)),
        cost_estimate=cost(cross_cells * 256 * 2 * 5, cross_cells, [query_c, key_c, value_c]),
        name="cross_back",
    )(far_here, query_c, key_c, value_c, d_mixed_c, lse_cross)
    d_n2 = mm(d_query_c, cq_t)
    back2, gain_cross_part = norm_back(x1, gain_cross, d_n2)
    g1 = g2 + back2
    g1_low = g1.astype(BF)

    attn_grads = [
        mm(mixed_self, g1_low, TN).astype(BF),
        mm(d_query_c, n2, TN).astype(BF),
        mm(d_key_c, enc_pair, TN).astype(BF),
        mm(d_value_c, enc_pair, TN).astype(BF),
        mm(mixed_cross, g2_low, TN).astype(BF),
    ]
    d_mixed_s = jnp.einsum("nd,zcd->znc", g1_low, wo_all, preferred_element_type=F32).astype(BF)
    enc_part = (mm(d_key_c, ck_t) + mm(d_value_c, cv_t)).astype(BF)

    small = jnp.zeros((8, LINE), F32)
    small = small.at[1, :width].set(gain_cross_part).at[2, :width].set(gain_ffn_part)
    small = small.at[3, 0].set(loss_part)
    unit = (stream * norm_scale(stream)).astype(BF)
    totals, enc_sum, d_n1, grouped, small = reduce_all(
        hot,
        [line, ok_cols, query_s, key_s, value_s, key_t, key_far, value_far, key_far.T,
         lse_prompt, lse_cont],
        [n1, unit, w_q, w_k, w_v],
        small,
        d_mixed_s,
        enc_part.reshape(2 * ranks, ENC_LEN // ranks, width),
        [a.reshape(ranks, hidden_here, width) for a in ffn_grads]
        + [a.reshape(ranks, cols, width) for a in attn_grads],
        bits,
        heads,
        4,
    )
    totals = [total.astype(F32) for total in totals]
    grad_enc = enc_sum.reshape(ENC_LEN, width).astype(F32)
    grad_table = jnp.dot(
        grouped[4 : 4 + heads, :DIST], bucket_hot, precision=lax.Precision.HIGHEST
    ).T
    back1, ignored = norm_back(x_own, gain_self, d_n1)
    grad_x = g1 + back1
    return (
        y_all[:share],
        y_all[share:],
        grad_x[:share],
        grad_x[share:],
        grad_enc,
        small[0, :width],
        small[1, :width],
        small[2, :width],
        grad_table,
        totals[8].T,
        totals[9].T,
        totals[10].T,
        totals[3],
        totals[4].T,
        totals[5].T,
        totals[6].T,
        totals[7],
        totals[0].T,
        totals[1].T,
        totals[2],
        small[3, 0] / token_count,
    )


def solution(mesh):
    rows = P("dp", None)
    both = P(("dp", "tensor"), None)
    columns = P(None, "tensor")
    shards = P("tensor", None)
    return jax.shard_map(
        on_device,
        mesh=mesh,
        in_specs=(
            (rows,) * 3 + (both,) * 3 + (P("dp"),) * 2 + (P(),) * 4 + (columns,) * 4
            + (shards,) + (columns,) * 3 + (shards,) + (columns,) * 2 + (shards,)
        ),
        out_specs=(
            (both,) * 4 + (rows,) + (P(),) * 3 + (columns,) * 4 + (shards,) + (columns,) * 3
            + (shards,) + (columns,) * 2 + (shards, P())
        ),
        check_vma=False,
    )
```

```python
import functools

import jax
import jax.numpy as jnp
from jax import lax
from jax.experimental import pallas as pl
from jax.experimental.pallas import tpu as pltpu
from jax.sharding import PartitionSpec as P

HEAD = 64
PROMPT = 1024
CONT_LEN = 128
ENC_LEN = 512
TILE = 128
DIST = PROMPT + CONT_LEN
LINE = DIST + 2 * TILE
SLAB = DIST + TILE

norm_eps = 1e-06
masked_value = -1e30
BF = jnp.bfloat16
F32 = jnp.float32
NT = (((1,), (1,)), ((), ()))
TN = (((0,), (0,)), ((), ()))
NN = (((1,), (0,)), ((), ()))


def mm(left, right, dims=NN):
    return lax.dot_general(left, right, dims, preferred_element_type=F32)


def from_ahead(block, step):
    count = lax.axis_size("tensor")
    return lax.ppermute(block, "tensor", [((i + step) % count, i) for i in range(count)])


def to_ahead(block, step):
    count = lax.axis_size("tensor")
    return lax.ppermute(block, "tensor", [(i, (i + step) % count) for i in range(count)])


def flip_bit(block, bit, axis="dp"):
    count = lax.axis_size(axis)
    return lax.ppermute(block, axis, [(i, i ^ (1 << bit)) for i in range(count)])


def norm_scale(values):
    return lax.rsqrt(jnp.mean(values * values, axis=-1, keepdims=True) + norm_eps)


def rms_norm(values, weight):
    return values * norm_scale(values) * weight


def norm_back(values, weight, grad):
    scale = norm_scale(values)
    unit = values * scale
    weighted = grad * weight
    inner = jnp.mean(weighted * unit, axis=-1, keepdims=True)
    return (scale * (weighted - unit * inner), jnp.sum(grad * unit, axis=0))


def make_slab(line):
    wide = jnp.broadcast_to(line, (TILE, LINE))
    return pltpu.roll(wide, LINE - (TILE - 1), 1, stride=1, stride_axis=0)[:, :SLAB]


def head_mask(head, width, dtype):
    lane = lax.broadcasted_iota(jnp.int32, (1, width), 1)
    return (lane // HEAD == head).astype(dtype)


def cont_rows(slot):
    return pl.ds(slot * CONT_LEN, CONT_LEN)


def late_rows(slot):
    return pl.ds(PROMPT + slot * CONT_LEN, CONT_LEN)


def row_of(lse, head):
    width = lse.shape[1]
    lane = lax.broadcasted_iota(jnp.int32, (1, width), 1)
    column = jnp.sum(jnp.where(lane == head * HEAD, lse, 0.0), axis=-1, keepdims=True)
    return jnp.broadcast_to(column, (lse.shape[0], TILE)).T[0:1, :]


def fold_slab(block):
    rows = TILE
    block = jnp.concatenate([block, jnp.zeros((TILE, LINE - SLAB), F32)], axis=1)
    while rows > 8:
        rows //= 2
        block = pltpu.roll(block[:rows], rows, 1) + block[rows:]
    line = jnp.zeros((1, LINE), F32)
    for r in range(rows):
        line = line + pltpu.roll(block, rows - 1 - r, 1)[r : r + 1]
    return line


def cross_fwd(far_ref, q_ref, k_ref, v_ref, o_ref, lse_ref):
    rows = q_ref.shape[0] - CONT_LEN
    far = pl.ds(pl.multiple_of(far_ref[0] * ENC_LEN, ENC_LEN), ENC_LEN)
    for part, keys in ((pl.ds(0, rows), pl.ds(0, ENC_LEN)), (pl.ds(rows, CONT_LEN), far)):
        q = q_ref[part, :]
        k = k_ref[keys, :]
        v = v_ref[keys, :]
        o = 0.0
        lse = 0.0
        for head in range(2):
            mask = head_mask(head, TILE, BF)
            s = mm(q * mask, k, NT)
            top = jnp.max(s, axis=-1, keepdims=True)
            e = jnp.exp(s - top)
            total = jnp.sum(e, axis=-1, keepdims=True)
            o = o + mm(e.astype(BF), v * mask) / total
            lse = lse + (top + jnp.log(total)) * head_mask(head, TILE, F32)
        o_ref[part, :] = o.astype(BF)
        lse_ref[part, :] = lse


def cross_back(far_ref, q_ref, k_ref, v_ref, do_ref, lse_ref, dq_ref, dk_ref, dv_ref, dk, dv):
    rows = q_ref.shape[0] - CONT_LEN
    far = pl.ds(pl.multiple_of(far_ref[0] * ENC_LEN, ENC_LEN), ENC_LEN)
    dk[ENC_LEN : 2 * ENC_LEN, :] = jnp.zeros((ENC_LEN, TILE), F32)
    dv[ENC_LEN : 2 * ENC_LEN, :] = jnp.zeros((ENC_LEN, TILE), F32)
    for index, (part, keys) in enumerate(
        ((pl.ds(0, rows), pl.ds(0, ENC_LEN)), (pl.ds(rows, CONT_LEN), far))
    ):
        q = q_ref[part, :]
        k = k_ref[keys, :]
        kt = k.T
        v = v_ref[keys, :]
        do = do_ref[part, :]
        lse = lse_ref[part, :].T
        gk, gv = (0.0, 0.0)
        dq = []
        for head in range(2):
            mask = head_mask(head, TILE, BF)
            qm = q * mask
            dom = do * mask
            s = mm(k, qm, NT)
            p = jnp.exp(s - lse[HEAD * head : HEAD * head + 1, :])
            dp = mm(v, dom, NT)
            centre = jnp.sum(p * dp, axis=0, keepdims=True)
            low = (p * (dp - centre)).astype(BF)
            gv = gv + mm(p.astype(BF), dom)
            gk = gk + mm(low, qm)
            dq.append(mm(kt[HEAD * head : HEAD * (head + 1), :], low))
        dq_ref[part, :] = (jnp.concatenate(dq, axis=0).T * HEAD ** (-0.5)).astype(BF)
        if index == 0:
            dk[0:ENC_LEN, :] = gk
            dv[0:ENC_LEN, :] = gv
        else:
            dk[keys, :] = dk[keys, :] + gk
            dv[keys, :] = dv[keys, :] + gv
    dk_ref[...] = dk[...].astype(BF)
    dv_ref[...] = dv[...].astype(BF)


def whole(shape):
    return pl.BlockSpec(shape, lambda *_: (0,) * len(shape))


def by_head(shape):
    return pl.BlockSpec((1,) + shape[1:], lambda head, *_: (head,) + (0,) * (len(shape) - 1))


def cost(flops, transcendentals, arrays):
    return pl.CostEstimate(
        flops=int(flops),
        transcendentals=int(transcendentals),
        bytes_accessed=int(sum(a.size * a.dtype.itemsize for a in arrays)),
    )


def shaped(*pairs):
    return [jax.ShapeDtypeStruct(shape, dtype) for shape, dtype in pairs]


MESH = pl.DeviceIdType.MESH


class Links:
    def __init__(self, sends, receives, local, bits):
        self.sends, self.receives, self.local_sems = sends, receives, local
        self.used = 0
        self.used_local = 0
        self.bits = bits
        self.data = lax.axis_index("dp")
        self.tensor = lax.axis_index("tensor")
        self.ranks = lax.axis_size("tensor")

    def bit(self, index):
        return self.data // (1 << index) % 2

    def partner(self, index):
        return (self.data + (1 << index) * (1 - 2 * self.bit(index)), self.tensor)

    def ahead(self, step):
        return (self.data, (self.tensor + step) % self.ranks)

    def across(self, index):
        here = self.tensor // (1 << index) % 2
        return (self.data, self.tensor + (1 << index) * (1 - 2 * here))

    def barrier(self):
        sem = pltpu.get_barrier_semaphore()
        others = [self.partner(index) for index in range(self.bits)]
        others += [self.ahead(step) for step in range(1, self.ranks)]
        for other in others:
            pl.semaphore_signal(sem, inc=1, device_id=other, device_id_type=MESH)
        pl.semaphore_wait(sem, len(others))

    def send(self, source, target, device):
        copy = pltpu.make_async_remote_copy(
            src_ref=source,
            dst_ref=target,
            send_sem=self.sends.at[self.used],
            recv_sem=self.receives.at[self.used],
            device_id=device,
            device_id_type=MESH,
        )
        self.used += 1
        copy.start()
        return copy

    def local(self, source, target):
        copy = pltpu.make_async_copy(source, target, self.local_sems.at[self.used_local])
        self.used_local += 1
        copy.start()
        return copy


def span(start, size, step):
    return pl.ds(pl.multiple_of(start, step), size)


def bit_order(place):
    return (1, 2) if place % 2 == 0 else (2, 1)


def split_chunks(sizes, unit):
    chunks = []
    for index, rows in enumerate(sizes):
        step = rows
        while step > unit:
            step //= 2
        chunks += [(index, start, step) for start in range(0, rows, step)]
    return chunks


def gather_stream(links, own, full, stage, first, rows, place):
    one, two = bit_order(place)
    width = own.shape[1]
    half = width // 2
    cols = span(links.bit(0) * half, half, 128)
    base = first + links.bit(one) * (rows // 2)
    quarter = span(base + links.bit(two) * (rows // 4), rows // 4, 16)
    mine = links.local(own.at[pl.ds(first, rows), :], stage)
    ranks = links.ranks
    copies = [links.send(own.at[quarter, cols], full.at[2, quarter, cols], links.across(1))]
    yield
    mine.wait()
    home = links.local(stage, full.at[0, pl.ds(first, rows), :])
    copies[0].wait()
    near = (links.tensor - flip_rank(links.tensor, (1,)) + ranks) % ranks
    copies = [
        links.send(own.at[quarter, cols], full.at[near, quarter, cols], links.across(0)),
        links.send(
            full.at[2, quarter, cols], full.at[(near + 2) % ranks, quarter, cols], links.across(0)
        ),
    ]
    yield
    for copy in copies:
        copy.wait()
    others = pl.ds(1, ranks - 1)
    part = full.at[others, quarter, cols]
    copy = links.send(part, part, links.partner(two))
    yield
    copy.wait()
    part = full.at[others, span(base, rows // 2, 16), cols]
    copy = links.send(part, part, links.partner(one))
    yield
    copy.wait()
    part = full.at[others, pl.ds(first, rows), cols]
    copy = links.send(part, part, links.partner(0))
    yield
    copy.wait()
    home.wait()


def count_stream(links, count, held, came, final):
    held[0] = count[...]
    for index in range(links.bits):
        copy = links.send(held.at[index], came.at[index], links.partner(index))
        yield
        copy.wait()
        value = held[index] + came[index]
        held[index + 1] = value
    final[...] = value


def attend(ins, far_refs, lent, work, heads):
    line_ref, ok_ref, q_ref, k_ref, v_ref = ins
    o_ref, o_late, lse_ref, lse_late, slab = work
    width = q_ref.shape[1]
    block = 2 * TILE
    for ref in (o_ref, o_late, lse_ref, lse_late):
        ref[...] = jnp.zeros_like(ref)
    for head in range(heads):
        slab[...] = make_slab(line_ref[head])
        mask = head_mask(head, width, BF)
        mask_f = head_mask(head, width, F32)
        for idx in range(PROMPT // block):
            keys = block * (idx + 1)
            rows = pl.ds(idx * block, block)
            s = mm(q_ref[rows, :] * mask, k_ref[0:keys, :], NT)
            start = PROMPT - block * idx
            s = s + jnp.concatenate(
                [slab[:, start : start + keys], slab[:, start - TILE : start - TILE + keys]],
                axis=0,
            )
            top = jnp.max(s, axis=-1, keepdims=True)
            e = jnp.exp(s - top)
            total = jnp.sum(e, axis=-1, keepdims=True)
            o = mm(e.astype(BF), v_ref[0:keys, :] * mask) / total
            o_ref[rows, :] = o_ref[rows, :] + o.astype(BF)
            lse_ref[rows, :] = lse_ref[rows, :] + (top + jnp.log(total)) * mask_f
            yield
        if head == 0:
            for copy in lent:
                copy.wait()
        for pair in range(2):
            keys_ref, values_ref = (k_ref, v_ref) if pair == 0 else far_refs
            slots = [2 * pair, 2 * pair + 1]
            qs = [q_ref[late_rows(slot), :] * mask for slot in slots]
            s = mm(jnp.concatenate(qs, axis=0), keys_ref[0:PROMPT, :], NT)
            s = s + jnp.concatenate([slab[:, 0:PROMPT], slab[:, 0:PROMPT]], axis=0)
            own = jnp.concatenate(
                [
                    mm(q, k_ref[late_rows(slot), :], NT)
                    + slab[:, PROMPT:DIST]
                    + ok_ref[slot][0:1, :]
                    for q, slot in zip(qs, slots)
                ],
                axis=0,
            )
            top = jnp.maximum(
                jnp.max(s, axis=-1, keepdims=True), jnp.max(own, axis=-1, keepdims=True)
            )
            e = jnp.exp(s - top)
            e_own = jnp.exp(own - top)
            total = jnp.sum(e, axis=-1, keepdims=True) + jnp.sum(e_own, axis=-1, keepdims=True)
            o = mm(e.astype(BF), values_ref[0:PROMPT, :] * mask)
            low = e_own.astype(BF)
            o_own = [
                mm(low[CONT_LEN * i : CONT_LEN * (i + 1), :], v_ref[late_rows(slot), :] * mask)
                for i, slot in enumerate(slots)
            ]
            o = (o + jnp.concatenate(o_own, axis=0)) / total
            here = pl.ds(2 * pair * CONT_LEN, 2 * CONT_LEN)
            o_late[here, :] = o_late[here, :] + o.astype(BF)
            lse_late[here, :] = lse_late[here, :] + (top + jnp.log(total)) * mask_f
            yield


def gather_kernel(count, bits, chunks, heads, pace, *refs):
    refs = list(refs)

    def take(number):
        taken, refs[:number] = refs[:number], []
        return taken

    (hot_ref,) = take(1)
    ins = take(5)
    count_ref, enc_in = take(2)
    own = take(count)
    full = take(count)
    k_far, v_far, lse_ref, lse_late, mixed, enc_far, count_out = take(7)
    o_ref, o_late, slab, leave, arrive, held, came = take(7)
    stages, (sends, receives, local) = refs[:-3], refs[-3:]
    links = Links(sends, receives, local, bits)
    links.barrier()
    ranks = links.ranks
    streams = [
        gather_stream(links, own[index], full[index], stages[place], first, rows, place)
        for place, (index, first, rows) in enumerate(chunks)
    ]
    prompt_rows = pl.ds(0, PROMPT)
    lent = [
        links.send(ins[3].at[prompt_rows, :], k_far, links.partner(0)),
        links.send(ins[4].at[prompt_rows, :], v_far, links.partner(0)),
    ]
    swap = links.send(enc_in, enc_far, links.partner(0))
    counter = count_stream(links, count_ref, held, came, count_out)
    pairs = pair_steps(streams, 5)

    def steps():
        for ignored in pairs:
            next(counter, None)
            yield

    comm = steps()
    next(comm)
    work = (o_ref, o_late, lse_ref, lse_late, slab)
    for number, ignored in enumerate(attend(ins, (k_far, v_far), lent, work, heads)):
        if number % pace == pace - 1:
            next(comm)
    share = PROMPT // ranks
    conts = hot_ref.shape[0]
    moved = []
    for step in (2, 1, 3, 0):
        rank = (links.tensor + step) % ranks
        target = leave if step else arrive
        target[step, pl.ds(0, share), :] = o_ref[span(rank * share, share, 16), :]
        late = 0.0
        for i in range(conts):
            late = late + o_late[cont_rows(i), :].astype(F32) * hot_ref[rank, i][0:1, 0:1]
        target[step, pl.ds(share, CONT_LEN), :] = late.astype(BF)
        if step:
            moved.append(
                links.send(leave.at[step], arrive.at[ranks - step], links.ahead(step))
            )
    for ignored in comm:
        pass
    for copy in moved:
        copy.wait()
    cols = o_ref.shape[1]
    for step in range(ranks):
        mixed[:, step * cols : (step + 1) * cols] = arrive[step]
    swap.wait()
    for ignored in counter:
        pass


def gather_all(hot, ins, count, enc, own, bits, heads, pace):
    ranks = lax.axis_size("tensor")
    chunks = split_chunks([a.shape[0] for a in own], 200)
    any_space = pl.BlockSpec(memory_space=pl.ANY)
    vmem = pl.BlockSpec(memory_space=pltpu.VMEM)
    cols = heads * HEAD
    late = hot.shape[0] * CONT_LEN
    rows_own = PROMPT // ranks + CONT_LEN
    copies = len(chunks) * 6 + ranks + 2 + bits
    out = pl.pallas_call(
        functools.partial(gather_kernel, len(own), bits, chunks, heads, pace),
        out_shape=[jax.ShapeDtypeStruct((ranks,) + a.shape, a.dtype) for a in own]
        + shaped(
            ((PROMPT, cols), BF),
            ((PROMPT, cols), BF),
            ((PROMPT, cols), F32),
            ((late, cols), F32),
            ((rows_own, ranks * cols), BF),
            (enc.shape, BF),
            (count.shape, F32),
        ),
        in_specs=[vmem] * (2 + len(ins)) + [any_space] * (1 + len(own)),
        out_specs=[any_space] * len(own) + [vmem] * 5 + [any_space, vmem],
        scratch_shapes=[
            pltpu.VMEM((PROMPT, cols), BF),
            pltpu.VMEM((late, cols), BF),
            pltpu.VMEM((TILE, SLAB), F32),
            pltpu.VMEM((ranks, rows_own, cols), BF),
            pltpu.VMEM((ranks, rows_own, cols), BF),
            pltpu.VMEM((bits + 1,) + count.shape, F32),
            pltpu.VMEM((bits,) + count.shape, F32),
        ]
        + [pltpu.VMEM((rows, own[0].shape[1]), BF) for _, _, rows in chunks]
        + [
            pltpu.SemaphoreType.DMA((copies,)),
            pltpu.SemaphoreType.DMA((copies,)),
            pltpu.SemaphoreType.DMA((2 * len(chunks),)),
        ],
        compiler_params=pltpu.CompilerParams(
            collective_id=1, has_side_effects=True, vmem_limit_bytes=60 * 2**20
        ),
        name="gather_all",
    )(hot, *ins, count, enc, *own)
    return out[: len(own)], out[len(own) :]


CORE_ROOMS = 8


def flip_rank(rank, bits):
    for bit in bits:
        rank = rank + bit * (1 - 2 * (rank // bit % 2))
    return rank


def pair_steps(streams, stages):
    pairs = [streams[i : i + 2] for i in range(0, len(streams), 2)]
    for step in range(len(pairs) + stages):
        for index in reversed(range(len(pairs))):
            if 0 <= step - index <= stages:
                for stream in pairs[index]:
                    next(stream, None)
        yield


def reduce_stream(links, grad, total, core_room, room, first, rows, place, slabs):
    mine, from_one, from_two, from_far, from_more = room
    from_core = core_room.at[pl.ds(0, slabs), pl.ds(0, rows), :]
    one, two = bit_order(place)
    half = grad.shape[2] // 2
    whole_rows = pl.ds(first, rows)
    here = span(links.bit(0) * half, half, 128)
    there = span((1 - links.bit(0)) * half, half, 128)
    kept = links.local(grad.at[:, whole_rows, here], mine)
    copy = links.send(grad.at[:, whole_rows, there], from_core, links.partner(0))
    yield
    kept.wait()
    copy.wait()
    mine[...] = mine[...] + from_core[...]
    base = links.bit(one) * (rows // 2)
    given = (1 - links.bit(one)) * (rows // 2)
    copy = links.send(
        mine.at[:, span(given, rows // 2, 16), :], from_one, links.partner(one)
    )
    yield
    copy.wait()
    keep = span(base, rows // 2, 16)
    mine[:, keep, :] = mine[:, keep, :] + from_one[...]
    given = base + (1 - links.bit(two)) * (rows // 4)
    base_two = base + links.bit(two) * (rows // 4)
    copy = links.send(
        mine.at[:, span(given, rows // 4, 16), :], from_two, links.partner(two)
    )
    yield
    copy.wait()
    keep = span(base_two, rows // 4, 16)
    if slabs > 1:
        mine[:, keep, :] = mine[:, keep, :] + from_two[...]
        slab = [
            (flip_rank(links.tensor, flips) - links.tensor + slabs) % slabs
            for flips in ((), (1,), (2,), (1, 2))
        ]
        copies = [
            links.send(mine.at[slab[1], keep, :], from_far.at[0], links.across(0)),
            links.send(mine.at[slab[3], keep, :], from_far.at[1], links.across(0)),
        ]
        yield
        for copy in copies:
            copy.wait()
        mine[slab[2], keep, :] = mine[slab[2], keep, :] + from_far[1]
        copy = links.send(mine.at[slab[2], keep, :], from_far.at[2], links.across(1))
        yield
        copy.wait()
        value = mine[0, keep, :].astype(F32) + from_far[0].astype(F32)
        value = (value + from_far[2].astype(F32)).astype(BF)
    else:
        value = mine[0, keep, :] + from_two[0]
    quarter = span(first + base_two, rows // 4, 16)
    for index in range(3, links.bits):
        total[quarter, here] = value
        copy = links.send(
            total.at[quarter, here], from_more.at[index - 3], links.partner(index)
        )
        copy.wait()
        value = value + from_more[index - 3]
    total[quarter, here] = value
    copy = links.send(total.at[quarter, here], total.at[quarter, here], links.partner(two))
    yield
    copy.wait()
    part = total.at[span(first + base, rows // 2, 16), here]
    copy = links.send(part, part, links.partner(one))
    yield
    copy.wait()
    part = total.at[whole_rows, here]
    copy = links.send(part, part, links.partner(0))
    yield
    copy.wait()


def small_stream(links, held, came, grouped, final):
    tensor_bits = links.ranks.bit_length() - 1
    for index in range(links.bits + tensor_bits):
        device = links.partner(index) if index < links.bits else links.across(index - links.bits)
        copy = links.send(held.at[index], came.at[index], device)
        yield
        copy.wait()
        value = held[index] + came[index]
        held[index + 1] = value
        if index == links.bits - 1:
            grouped[...] = value
    final[...] = value


def rows_stream(links, parts, came, out, rows):
    copy = links.send(
        parts.at[pl.ds(2, 2), rows, :], came.at[pl.ds(0, 2), rows, :], links.across(0)
    )
    yield
    copy.wait()
    parts[1, rows, :] = parts[1, rows, :] + came[1, rows, :]
    copy = links.send(parts.at[1, rows, :], came.at[2, rows, :], links.across(1))
    yield
    copy.wait()
    out[rows, :] = (
        parts[0, rows, :].astype(F32) + came[0, rows, :].astype(F32) + came[2, rows, :].astype(F32)
    )


def rows_streams(links, parts, came, out, pieces):
    size = out.shape[0] // pieces
    active = []
    for piece in range(pieces + 2):
        if piece < pieces:
            active.append(rows_stream(links, parts, came, out, pl.ds(piece * size, size)))
        for stream in reversed(active):
            next(stream, None)
        yield


def encoder_stream(links, enc, from_core, total, came, final):
    count = from_core.shape[0]
    here = [flip_rank(links.tensor, flips) for flips in ((), (1,), (2,), (1, 2))]
    kept = links.local(enc.at[pl.ds(0, count)], total)
    copy = links.send(enc.at[pl.ds(count, count)], from_core, links.partner(0))
    yield
    kept.wait()
    copy.wait()
    total[...] = total[...] + from_core[...]
    copies = [
        links.send(total.at[here[1]], came.at[0], links.across(0)),
        links.send(total.at[here[3]], came.at[1], links.across(0)),
    ]
    yield
    for copy in copies:
        copy.wait()
    total[here[2]] = total[here[2]] + came[1]
    copy = links.send(total.at[here[2]], came.at[2], links.across(1))
    yield
    copy.wait()
    value = total[here[0]].astype(F32) + came[0].astype(F32) + came[2].astype(F32)
    final[here[0]] = value.astype(BF)
    copies = [links.send(final.at[here[0]], final.at[here[0]], links.across(1))]
    yield
    copies[0].wait()
    copies = [
        links.send(final.at[place], final.at[place], links.across(0))
        for place in (here[0], here[2])
    ]
    yield
    for copy in copies:
        copy.wait()


def attend_back(ins, work, heads):
    line_ref, ok_ref, q_ref, k_ref, v_ref, kt_ref, kf_ref, vf_ref, ktf_ref, lse_ref, late_ref = ins
    do_ref, do_late, slab, gslab, dqt, dqc, dk, dv, dkc, dvc, dkf, dvf, held = work
    width = q_ref.shape[1]
    block = 2 * TILE
    for ref in (dk, dv, dkf, dvf, dkc, dvc):
        ref[...] = jnp.zeros_like(ref)
    for head in range(heads):
        slab[...] = make_slab(line_ref[head]).T
        gslab[...] = jnp.zeros_like(gslab)
        mask = head_mask(head, width, BF)
        mine = pl.ds(head * HEAD, HEAD)
        for pair in range(2):
            keys_ref, kt, values_ref = (
                (k_ref, kt_ref, v_ref) if pair == 0 else (kf_ref, ktf_ref, vf_ref)
            )
            gk, gv = (dk, dv) if pair == 0 else (dkf, dvf)
            slots = [2 * pair, 2 * pair + 1]
            qs = [q_ref[late_rows(slot), :] * mask for slot in slots]
            dos = [do_late[slot] * mask for slot in slots]
            q = jnp.concatenate(qs, axis=0)
            do = jnp.concatenate(dos, axis=0)
            lse = row_of(
                jnp.concatenate([late_ref[cont_rows(slot), :] for slot in slots], axis=0), head
            )
            s = mm(keys_ref[0:PROMPT, :], q, NT)
            s = s + jnp.concatenate([slab[0:PROMPT, :], slab[0:PROMPT, :]], axis=1)
            keys_own = [k_ref[late_rows(slot), :] for slot in slots]
            own = jnp.concatenate(
                [
                    mm(keys, qc, NT) + slab[PROMPT:DIST, :] + ok_ref[slot]
                    for keys, qc, slot in zip(keys_own, qs, slots)
                ],
                axis=1,
            )
            p = jnp.exp(s - lse)
            p_own = jnp.exp(own - lse)
            dp = mm(values_ref[0:PROMPT, :], do, NT)
            dp_own = jnp.concatenate(
                [mm(v_ref[late_rows(slot), :], doc, NT) for doc, slot in zip(dos, slots)], axis=1
            )
            centre = jnp.sum(p * dp, axis=0, keepdims=True) + jnp.sum(
                p_own * dp_own, axis=0, keepdims=True
            )
            ds = p * (dp - centre)
            ds_own = p_own * (dp_own - centre)
            low = ds.astype(BF)
            low_own = ds_own.astype(BF)
            p_low = p_own.astype(BF)
            gv[...] = gv[...] + mm(p.astype(BF), do)
            gk[...] = gk[...] + mm(low, q)
            dq = mm(kt[mine, 0:PROMPT], low)
            for i in range(2):
                part = slice(CONT_LEN * i, CONT_LEN * (i + 1))
                spot = 2 * pair + i
                here = pl.ds(spot * CONT_LEN, CONT_LEN)
                dvc[here, :] = dvc[here, :] + mm(p_low[:, part], dos[i])
                dkc[here, :] = dkc[here, :] + mm(low_own[:, part], qs[i])
                head_keys = keys_own[i].T[head * HEAD : (head + 1) * HEAD, :]
                dqc[spot, mine, :] = dq[:, part] + mm(head_keys, low_own[:, part])
                gslab[0:PROMPT, :] = gslab[0:PROMPT, :] + ds[:, part]
                gslab[PROMPT:DIST, :] = gslab[PROMPT:DIST, :] + ds_own[:, part]
            yield
        for idx in range(PROMPT // block):
            keys = block * (idx + 1)
            rows = pl.ds(idx * block, block)
            q = q_ref[rows, :] * mask
            do = do_ref[idx, pl.ds(0, block), :] * mask
            s = mm(k_ref[0:keys, :], q, NT)
            start = PROMPT - block * idx
            s = s + jnp.concatenate(
                [slab[start : start + keys, :], slab[start - TILE : start - TILE + keys, :]],
                axis=1,
            )
            p = jnp.exp(s - row_of(lse_ref[rows, :], head))
            dp = mm(v_ref[0:keys, :], do, NT)
            centre = jnp.sum(p * dp, axis=0, keepdims=True)
            ds = p * (dp - centre)
            low = ds.astype(BF)
            dv[0:keys, :] = dv[0:keys, :] + mm(p.astype(BF), do)
            dk[0:keys, :] = dk[0:keys, :] + mm(low, q)
            dqt[mine, rows] = mm(kt_ref[mine, 0:keys], low)
            gslab[start : start + keys, :] = gslab[start : start + keys, :] + ds[:, 0:TILE]
            gslab[start - TILE : start - TILE + keys, :] = (
                gslab[start - TILE : start - TILE + keys, :] + ds[:, TILE:block]
            )
            yield
        held[0, pl.ds(4 + head, 1), :] = fold_slab(gslab[...].T)


def reduce_kernel(count, bits, chunks, heads, pace, *refs):
    refs = list(refs)

    def take(number):
        taken, refs[:number] = refs[:number], []
        return taken

    (hot_ref,) = take(1)
    ins = take(11)
    n1_ref, unit_ref, wq_ref, wk_ref, wv_ref, small_ref, do_in, enc_in = take(8)
    grads = take(count)
    totals = take(count + 3)
    enc_final, out, grouped, final = take(4)
    do_ref, do_late, slab, gslab, dqt, dqc, dk, dv, dkc, dvc, dkf, dvf = take(12)
    lent_out, lent_in, dq_all, dk_all, dv_all, parts, came_rows = take(7)
    grads = grads + take(3)
    held, came, enc_core, enc_total, enc_came = take(5)
    core_rooms = take(CORE_ROOMS)
    sends, receives, local = refs[-3:]
    rooms = [refs[5 * i : 5 * i + 5] for i in range(len(chunks))]
    links = Links(sends, receives, local, bits)
    links.barrier()
    ranks = links.ranks
    width = n1_ref.shape[1]
    moved = [
        links.send(do_in.at[step], do_ref.at[links.tensor], links.ahead(step))
        for step in range(1, ranks)
    ]
    stay = links.local(do_in.at[0], do_ref.at[links.tensor])
    streams = [
        reduce_stream(
            links, grads[index], totals[index], core_rooms[place % CORE_ROOMS], rooms[place], first,
            rows, place, grads[index].shape[0],
        )
        for place, (index, first, rows) in enumerate(chunks)
    ]
    encoder = encoder_stream(links, enc_in, enc_core, enc_total, enc_came, enc_final)
    pairs = pair_steps(streams, 8)

    def steps():
        for ignored in pairs:
            next(encoder, None)
            yield

    comm = steps()
    next(comm)
    next(comm)
    next(comm)
    held[0] = small_ref[...]
    stay.wait()
    for copy in moved:
        copy.wait()
    conts = dqc.shape[0]
    share = PROMPT // ranks
    for i in range(conts):
        value = 0.0
        for cont in range(conts):
            late = do_ref[cont, pl.ds(share, CONT_LEN), :].astype(F32)
            value = value + late * hot_ref[cont, i][0:1, 0:1]
        do_late[i] = value.astype(BF)
    work = (do_ref, do_late, slab, gslab, dqt, dqc, dk, dv, dkc, dvc, dkf, dvf, held)
    for number, ignored in enumerate(attend_back(ins, work, heads)):
        if number % pace == pace - 1:
            next(comm)

    lent_out[0] = dkf[...].astype(BF)
    lent_out[1] = dvf[...].astype(BF)
    lent = links.send(lent_out, lent_in, links.partner(0))
    dq_all[0:PROMPT, :] = (dqt[...].T * HEAD ** (-0.5)).astype(BF)
    for i in range(conts):
        here = late_rows(i)
        spot = cont_rows(i)
        dq_all[here, :] = (dqc[i].T * HEAD ** (-0.5)).astype(BF)
        dk_all[here, :] = dkc[spot, :].astype(BF)
        dv_all[here, :] = dvc[spot, :].astype(BF)
    lent.wait()
    dk_all[0:PROMPT, :] = (dk[...] + lent_in[0].astype(F32)).astype(BF)
    dv_all[0:PROMPT, :] = (dv[...] + lent_in[1].astype(F32)).astype(BF)
    gain = jnp.zeros((1, width), F32)

    def input_grad(rows):
        value = (
            mm(dq_all[rows, :], wq_ref[...], NT)
            + mm(dk_all[rows, :], wk_ref[...], NT)
            + mm(dv_all[rows, :], wv_ref[...], NT)
        )
        return value, jnp.sum(value * unit_ref[rows, :].astype(F32), axis=0, keepdims=True)

    late = []
    for i in range(conts):
        value, term = input_grad(late_rows(i))
        late.append(value)
        gain = gain + term
    for place, flips in ((2, (1,)), (3, (1, 2)), (1, (2,)), (0, ())):
        rank = flip_rank(links.tensor, flips)
        value, term = input_grad(span(rank * share, share, 16))
        gain = gain + term
        parts[place, pl.ds(0, share), :] = value.astype(BF)
        total = 0.0
        for i in range(conts):
            total = total + late[i] * hot_ref[rank, i][0:1, 0:1]
        parts[place, pl.ds(share, CONT_LEN), :] = total.astype(BF)
    held[0, 0:1, 0:width] = gain
    extras = [
        rows_streams(links, parts, came_rows, out, 8),
        small_stream(links, held, came, grouped, final),
    ]
    for stream in extras:
        next(stream)
    for index, whole_ref in enumerate((dq_all, dk_all, dv_all)):
        grads[count + index][0] = mm(whole_ref[...], n1_ref[...], TN).astype(BF)
    for ignored in comm:
        for stream in extras:
            next(stream, None)
    for stream in extras:
        for ignored in stream:
            pass


def reduce_all(hot, ins, mats, small, do_in, enc, grads, bits, heads, pace):
    ranks = lax.axis_size("tensor")
    width = mats[0].shape[1]
    cols = heads * HEAD
    half = width // 2
    chunks = split_chunks([a.shape[1] for a in grads], 200)
    chunks += [(len(grads) + i, 0, cols) for i in range(3)]
    more = max(bits - 3, 1)
    conts = hot.shape[0]
    late = conts * CONT_LEN
    own = PROMPT // ranks + CONT_LEN
    rooms = []
    for index, _, rows in chunks:
        slabs = grads[index].shape[0] if index < len(grads) else 1
        rooms += [
            pltpu.VMEM((slabs, rows, half), BF),
            pltpu.VMEM((slabs, rows // 2, half), BF),
            pltpu.VMEM((slabs, rows // 4, half), BF),
            pltpu.VMEM((3, rows // 4, half), BF),
            pltpu.VMEM((more, rows // 4, half), BF),
        ]
    small_steps = bits + ranks.bit_length() - 1
    copies = len(chunks) * (9 + bits - 3) + small_steps + ranks + 24
    enc_block = (enc.shape[1], width)
    any_space = pl.BlockSpec(memory_space=pl.ANY)
    vmem = pl.BlockSpec(memory_space=pltpu.VMEM)
    out = pl.pallas_call(
        functools.partial(reduce_kernel, len(grads), bits, chunks, heads, pace),
        out_shape=shaped(
            *[(a.shape[1:], BF) for a in grads],
            *[((cols, width), BF)] * 3,
            ((ranks,) + enc_block, BF),
            ((own, width), F32),
            (small.shape, F32),
            (small.shape, F32),
        ),
        in_specs=[vmem] * (len(ins) + len(mats) + 2)
        + [any_space] * (2 + len(grads)),
        out_specs=[vmem] * (len(grads) + 7),
        scratch_shapes=[
            pltpu.VMEM(do_in.shape, BF),
            pltpu.VMEM((conts, CONT_LEN, cols), BF),
            pltpu.VMEM((SLAB, TILE), F32),
            pltpu.VMEM((SLAB, TILE), F32),
            pltpu.VMEM((cols, PROMPT), F32),
            pltpu.VMEM((conts, cols, CONT_LEN), F32),
            pltpu.VMEM((PROMPT, cols), F32),
            pltpu.VMEM((PROMPT, cols), F32),
            pltpu.VMEM((late, cols), F32),
            pltpu.VMEM((late, cols), F32),
            pltpu.VMEM((PROMPT, cols), F32),
            pltpu.VMEM((PROMPT, cols), F32),
            pltpu.VMEM((2, PROMPT, cols), BF),
            pltpu.VMEM((2, PROMPT, cols), BF),
            pltpu.VMEM((PROMPT + late, cols), BF),
            pltpu.VMEM((PROMPT + late, cols), BF),
            pltpu.VMEM((PROMPT + late, cols), BF),
            pltpu.VMEM((ranks, own, width), BF),
            pltpu.VMEM((ranks - 1, own, width), BF),
            pltpu.VMEM((1, cols, width), BF),
            pltpu.VMEM((1, cols, width), BF),
            pltpu.VMEM((1, cols, width), BF),
            pltpu.VMEM((small_steps + 1,) + small.shape, F32),
            pltpu.VMEM((small_steps,) + small.shape, F32),
            pltpu.VMEM((ranks,) + enc_block, BF),
            pltpu.VMEM((ranks,) + enc_block, BF),
            pltpu.VMEM((ranks - 1,) + enc_block, BF),
        ]
        + [pltpu.VMEM((ranks, max(c[2] for c in chunks), half), BF)] * CORE_ROOMS
        + rooms
        + [
            pltpu.SemaphoreType.DMA((copies,)),
            pltpu.SemaphoreType.DMA((copies,)),
            pltpu.SemaphoreType.DMA((len(chunks) + 2,)),
        ],
        compiler_params=pltpu.CompilerParams(
            collective_id=2, has_side_effects=True, vmem_limit_bytes=67043328
        ),
        name="reduce_all",
    )(hot, *ins, *mats, small, do_in, enc, *grads)
    return out[: len(grads) + 3], out[-4], out[-3], out[-2], out[-1]


def run_heads(kernel, heads, scalars, lines, arrays, outs, scratch, out_heads, cells, name):
    in_specs = [by_head(a.shape) for a in lines] + [whole(a.shape) for a in arrays]
    out_specs = [
        by_head(o.shape) if i in out_heads else whole(o.shape) for i, o in enumerate(outs)
    ]
    return pl.pallas_call(
        kernel,
        out_shape=outs,
        grid_spec=pltpu.PrefetchScalarGridSpec(
            num_scalar_prefetch=len(scalars),
            grid=(heads,),
            in_specs=in_specs,
            out_specs=out_specs,
            scratch_shapes=scratch,
        ),
        compiler_params=pltpu.CompilerParams(dimension_semantics=("arbitrary",)),
        cost_estimate=cost(
            cells * heads * 256 * 2 * (2 if not out_heads else 5), cells * heads,
            list(lines) + list(arrays) + list(outs),
        ),
        name=name,
    )(*scalars, *lines, *arrays)


def on_device(
    x_prompt,
    x_cont,
    enc_out,
    cot_prompt,
    cot_cont,
    teacher,
    valid,
    prompt_of,
    buckets,
    gain_self,
    gain_cross,
    gain_ffn,
    rel_table,
    w_q,
    w_k,
    w_v,
    w_o,
    c_q,
    c_k,
    c_v,
    c_o,
    w_gate,
    w_up,
    w_down,
):
    width = x_prompt.shape[1]
    cont_count = prompt_of.shape[0]
    heads = w_q.shape[1] // HEAD
    cols = heads * HEAD
    hidden_here = w_gate.shape[1]
    ranks = lax.axis_size("tensor")
    data_size = lax.axis_size("dp")
    share = PROMPT // ranks
    tensor_rank = lax.axis_index("tensor")
    data_rank = lax.axis_index("dp")
    factor = HEAD ** (-0.5)
    bits = data_size.bit_length() - 1

    far = (prompt_of != data_rank).astype(jnp.int32)
    index = jnp.arange(cont_count, dtype=jnp.int32)
    before = index[None, :] < index[:, None]
    near_rank = jnp.sum(jnp.where(before, 1 - far[None, :], 0), axis=1)
    far_rank = jnp.sum(jnp.where(before, far[None, :], 0), axis=1)
    spot = jnp.where(far == 0, near_rank, cont_count // 2 + far_rank)
    slots = jnp.sum(jnp.where(spot[None, :] == index[:, None], index[None, :], 0), axis=1)
    hot = jnp.broadcast_to(
        (spot[:, None] == index[None, :]).astype(F32)[:, :, None, None],
        (cont_count, cont_count, 8, 128),
    )

    def by_place(rows):
        return jnp.concatenate(
            [
                lax.dynamic_slice_in_dim(rows, slots[i] * CONT_LEN, CONT_LEN, 0)
                for i in range(cont_count)
            ]
        )

    far_here = lax.dynamic_slice_in_dim(far, tensor_rank, 1, 0)

    def own_rows(prompt_rows, conts):
        return jnp.concatenate(
            [
                lax.dynamic_slice_in_dim(prompt_rows, tensor_rank * share, share, 0),
                lax.dynamic_slice_in_dim(conts, tensor_rank * CONT_LEN, CONT_LEN, 0),
            ]
        )

    count = jnp.broadcast_to(jnp.sum(valid.astype(F32)), (8, 128))

    bucket_hot = (buckets[::-1][:, None] == jnp.arange(rel_table.shape[0])[None, :]).astype(F32)
    table = jnp.dot(bucket_hot, rel_table, precision=lax.Precision.HIGHEST).T
    line = jnp.concatenate(
        [table, jnp.full((heads, LINE - DIST), masked_value, F32)], axis=1
    ).reshape(heads, 1, LINE)
    ok = jnp.where(by_place(valid) > 0, 0.0, masked_value).astype(F32)
    ok_rows = jnp.broadcast_to(ok.reshape(cont_count, 1, CONT_LEN), (cont_count, 8, CONT_LEN))
    ok_cols = jnp.broadcast_to(
        ok.reshape(cont_count, CONT_LEN, 1), (cont_count, CONT_LEN, CONT_LEN)
    )

    stream = jnp.concatenate([x_prompt, by_place(x_cont)]).astype(F32)
    n1 = rms_norm(stream, gain_self).astype(BF)
    key_s = mm(n1, w_k).astype(BF)
    value_s = mm(n1, w_v).astype(BF)
    query_s = (mm(n1, w_q).astype(F32) * factor).astype(BF)
    key_t = mm(w_k, n1, (((0,), (1,)), ((), ()))).astype(BF)
    weights, (key_far, value_far, lse_prompt, lse_cont, mixed_self, enc_far, count) = gather_all(
        hot,
        [line, ok_rows, query_s, key_s, value_s],
        count,
        enc_out,
        [w_o, c_q.T, c_k.T, c_v.T, c_o, w_gate.T, w_up.T, w_down],
        bits,
        heads,
        6,
    )
    wo_all, cq_all, ck_all, cv_all, co_all, wg_all, wu_all, wd_all = weights
    token_count = count[0, 0]

    wo_full, cq_t, ck_t, cv_t, co_full = (
        a.reshape(ranks * cols, width) for a in (wo_all, cq_all, ck_all, cv_all, co_all)
    )
    x_own = own_rows(x_prompt, x_cont).astype(F32)
    x1 = x_own + mm(mixed_self, wo_full)
    n2 = rms_norm(x1, gain_cross).astype(BF)
    query_c = (mm(n2, cq_t, NT) * factor).astype(BF)
    enc_pair = jnp.concatenate([enc_out, enc_far])
    key_c = mm(enc_pair, ck_t, NT).astype(BF)
    value_c = mm(enc_pair, cv_t, NT).astype(BF)
    own_count = query_c.shape[0]
    pairs = query_c.shape[1] // TILE

    def columns(rows):
        return pl.BlockSpec((rows, TILE), lambda i, *_: (0, i))

    cross_cells = own_count * ENC_LEN * pairs * 2
    mixed_cross, lse_cross = pl.pallas_call(
        cross_fwd,
        out_shape=shaped(((own_count, pairs * TILE), BF), ((own_count, pairs * TILE), F32)),
        grid_spec=pltpu.PrefetchScalarGridSpec(
            num_scalar_prefetch=1,
            grid=(pairs,),
            in_specs=[columns(own_count), columns(2 * ENC_LEN), columns(2 * ENC_LEN)],
            out_specs=[columns(own_count), columns(own_count)],
        ),
        compiler_params=pltpu.CompilerParams(dimension_semantics=("arbitrary",)),
        cost_estimate=cost(cross_cells * 256 * 2 * 2, cross_cells, [query_c, key_c, value_c]),
        name="cross_fwd",
    )(far_here, query_c, key_c, value_c)
    x2 = x1 + mm(mixed_cross, co_full)
    n3 = rms_norm(x2, gain_ffn).astype(BF)
    wg_t, wu_t, wd = (a.reshape(ranks * hidden_here, width) for a in (wg_all, wu_all, wd_all))
    gate_pre = mm(n3, wg_t, NT)
    upper = mm(n3, wu_t, NT)
    hidden, gelu_pull = jax.vjp(
        lambda first_in, second_in: jax.nn.gelu(first_in, approximate=True) * second_in,
        gate_pre,
        upper,
    )
    hidden = hidden.astype(BF)
    x3 = x2 + mm(hidden, wd)
    valid_own = lax.dynamic_slice_in_dim(valid, tensor_rank * CONT_LEN, CONT_LEN, 0).astype(F32)[
        :, None
    ]
    deviation = x3[share:] - teacher.astype(F32)
    loss_part = jnp.sum(valid_own * deviation * deviation)
    g3 = jnp.concatenate(
        [
            cot_prompt.astype(F32),
            cot_cont.astype(F32) + 2.0 * valid_own * deviation / token_count,
        ]
    )
    y_all = x3.astype(BF)

    g3_low = g3.astype(BF)
    d_hidden = mm(g3_low, wd, NT).astype(BF).astype(F32)
    d_gate, d_upper = gelu_pull(d_hidden)
    d_gate = d_gate.astype(BF)
    d_upper = d_upper.astype(BF)
    ffn_grads = [
        mm(d_gate, n3, TN).astype(BF),
        mm(d_upper, n3, TN).astype(BF),
        mm(hidden, g3_low, TN).astype(BF),
    ]
    d_n3 = mm(d_gate, wg_t) + mm(d_upper, wu_t)
    back3, gain_ffn_part = norm_back(x2, gain_ffn, d_n3)
    g2 = g3 + back3

    g2_low = g2.astype(BF)
    d_mixed_c = mm(g2_low, co_full, NT).astype(BF)
    d_query_c, d_key_c, d_value_c = pl.pallas_call(
        cross_back,
        out_shape=shaped(
            ((own_count, pairs * TILE), BF),
            ((2 * ENC_LEN, pairs * TILE), BF),
            ((2 * ENC_LEN, pairs * TILE), BF),
        ),
        grid_spec=pltpu.PrefetchScalarGridSpec(
            num_scalar_prefetch=1,
            grid=(pairs,),
            in_specs=[
                columns(own_count), columns(2 * ENC_LEN), columns(2 * ENC_LEN),
                columns(own_count), columns(own_count),
            ],
            out_specs=[columns(own_count), columns(2 * ENC_LEN), columns(2 * ENC_LEN)],
            scratch_shapes=[pltpu.VMEM((2 * ENC_LEN, TILE), F32)] * 2,
        ),
        compiler_params=pltpu.CompilerParams(dimension_semantics=("arbitrary",)),
        cost_estimate=cost(cross_cells * 256 * 2 * 5, cross_cells, [query_c, key_c, value_c]),
        name="cross_back",
    )(far_here, query_c, key_c, value_c, d_mixed_c, lse_cross)
    d_n2 = mm(d_query_c, cq_t)
    back2, gain_cross_part = norm_back(x1, gain_cross, d_n2)
    g1 = g2 + back2
    g1_low = g1.astype(BF)

    attn_grads = [
        mm(mixed_self, g1_low, TN).astype(BF),
        mm(d_query_c, n2, TN).astype(BF),
        mm(d_key_c, enc_pair, TN).astype(BF),
        mm(d_value_c, enc_pair, TN).astype(BF),
        mm(mixed_cross, g2_low, TN).astype(BF),
    ]
    d_mixed_s = jnp.einsum("nd,zcd->znc", g1_low, wo_all, preferred_element_type=F32).astype(BF)
    enc_part = (mm(d_key_c, ck_t) + mm(d_value_c, cv_t)).astype(BF)

    small = jnp.zeros((8, LINE), F32)
    small = small.at[1, :width].set(gain_cross_part).at[2, :width].set(gain_ffn_part)
    small = small.at[3, 0].set(loss_part)
    unit = (stream * norm_scale(stream)).astype(BF)
    totals, enc_sum, d_n1, grouped, small = reduce_all(
        hot,
        [line, ok_cols, query_s, key_s, value_s, key_t, key_far, value_far, key_far.T,
         lse_prompt, lse_cont],
        [n1, unit, w_q, w_k, w_v],
        small,
        d_mixed_s,
        enc_part.reshape(2 * ranks, ENC_LEN // ranks, width),
        [a.reshape(ranks, hidden_here, width) for a in ffn_grads]
        + [a.reshape(ranks, cols, width) for a in attn_grads],
        bits,
        heads,
        4,
    )
    totals = [total.astype(F32) for total in totals]
    grad_enc = enc_sum.reshape(ENC_LEN, width).astype(F32)
    grad_table = jnp.dot(
        grouped[4 : 4 + heads, :DIST], bucket_hot, precision=lax.Precision.HIGHEST
    ).T
    back1, ignored = norm_back(x_own, gain_self, d_n1)
    grad_x = g1 + back1
    return (
        y_all[:share],
        y_all[share:],
        grad_x[:share],
        grad_x[share:],
        grad_enc,
        small[0, :width],
        small[1, :width],
        small[2, :width],
        grad_table,
        totals[8].T,
        totals[9].T,
        totals[10].T,
        totals[3],
        totals[4].T,
        totals[5].T,
        totals[6].T,
        totals[7],
        totals[0].T,
        totals[1].T,
        totals[2],
        small[3, 0] / token_count,
    )


def solution(mesh):
    rows = P("dp", None)
    both = P(("dp", "tensor"), None)
    columns = P(None, "tensor")
    shards = P("tensor", None)
    return jax.shard_map(
        on_device,
        mesh=mesh,
        in_specs=(
            (rows,) * 3 + (both,) * 3 + (P("dp"),) * 2 + (P(),) * 4 + (columns,) * 4
            + (shards,) + (columns,) * 3 + (shards,) + (columns,) * 2 + (shards,)
        ),
        out_specs=(
            (both,) * 4 + (rows,) + (P(),) * 3 + (columns,) * 4 + (shards,) + (columns,) * 3
            + (shards,) + (columns,) * 2 + (shards, P())
        ),
        check_vma=False,
    )
```

```python
import functools

import jax
import jax.numpy as jnp
from jax import lax
from jax.experimental import pallas as pl
from jax.experimental.pallas import tpu as pltpu
from jax.sharding import PartitionSpec as P

HEAD = 64
PROMPT = 1024
CONT_LEN = 128
ENC_LEN = 512
TILE = 128
DIST = PROMPT + CONT_LEN
LINE = DIST + 2 * TILE
SLAB = DIST + TILE

norm_eps = 1e-06
masked_value = -1e30
BF = jnp.bfloat16
F32 = jnp.float32
NT = (((1,), (1,)), ((), ()))
TN = (((0,), (0,)), ((), ()))
NN = (((1,), (0,)), ((), ()))


def mm(left, right, dims=NN):
    return lax.dot_general(left, right, dims, preferred_element_type=F32)


def from_ahead(block, step):
    count = lax.axis_size("tensor")
    return lax.ppermute(block, "tensor", [((i + step) % count, i) for i in range(count)])


def to_ahead(block, step):
    count = lax.axis_size("tensor")
    return lax.ppermute(block, "tensor", [(i, (i + step) % count) for i in range(count)])


def flip_bit(block, bit, axis="dp"):
    count = lax.axis_size(axis)
    return lax.ppermute(block, axis, [(i, i ^ (1 << bit)) for i in range(count)])


def norm_scale(values):
    return lax.rsqrt(jnp.mean(values * values, axis=-1, keepdims=True) + norm_eps)


def rms_norm(values, weight):
    return values * norm_scale(values) * weight


def norm_back(values, weight, grad):
    scale = norm_scale(values)
    unit = values * scale
    weighted = grad * weight
    inner = jnp.mean(weighted * unit, axis=-1, keepdims=True)
    return (scale * (weighted - unit * inner), jnp.sum(grad * unit, axis=0))


def make_slab(line):
    wide = jnp.broadcast_to(line, (TILE, LINE))
    return pltpu.roll(wide, LINE - (TILE - 1), 1, stride=1, stride_axis=0)[:, :SLAB]


def head_mask(head, width, dtype):
    lane = lax.broadcasted_iota(jnp.int32, (1, width), 1)
    return (lane // HEAD == head).astype(dtype)


def cont_rows(slot):
    return pl.ds(slot * CONT_LEN, CONT_LEN)


def late_rows(slot):
    return pl.ds(PROMPT + slot * CONT_LEN, CONT_LEN)


def row_of(lse, head):
    width = lse.shape[1]
    lane = lax.broadcasted_iota(jnp.int32, (1, width), 1)
    column = jnp.sum(jnp.where(lane == head * HEAD, lse, 0.0), axis=-1, keepdims=True)
    return jnp.broadcast_to(column, (lse.shape[0], TILE)).T[0:1, :]


def fold_slab(block):
    rows = TILE
    block = jnp.concatenate([block, jnp.zeros((TILE, LINE - SLAB), F32)], axis=1)
    while rows > 8:
        rows //= 2
        block = pltpu.roll(block[:rows], rows, 1) + block[rows:]
    line = jnp.zeros((1, LINE), F32)
    for r in range(rows):
        line = line + pltpu.roll(block, rows - 1 - r, 1)[r : r + 1]
    return line


def cross_fwd(far_ref, q_ref, k_ref, v_ref, o_ref, lse_ref):
    rows = q_ref.shape[0] - CONT_LEN
    far = pl.ds(pl.multiple_of(far_ref[0] * ENC_LEN, ENC_LEN), ENC_LEN)
    for part, keys in ((pl.ds(0, rows), pl.ds(0, ENC_LEN)), (pl.ds(rows, CONT_LEN), far)):
        q = q_ref[part, :]
        k = k_ref[keys, :]
        v = v_ref[keys, :]
        o = 0.0
        lse = 0.0
        for head in range(2):
            mask = head_mask(head, TILE, BF)
            s = mm(q * mask, k, NT)
            top = jnp.max(s, axis=-1, keepdims=True)
            e = jnp.exp(s - top)
            total = jnp.sum(e, axis=-1, keepdims=True)
            o = o + mm(e.astype(BF), v * mask) / total
            lse = lse + (top + jnp.log(total)) * head_mask(head, TILE, F32)
        o_ref[part, :] = o.astype(BF)
        lse_ref[part, :] = lse


def cross_back(far_ref, q_ref, k_ref, v_ref, do_ref, lse_ref, dq_ref, dk_ref, dv_ref, dk, dv):
    rows = q_ref.shape[0] - CONT_LEN
    far = pl.ds(pl.multiple_of(far_ref[0] * ENC_LEN, ENC_LEN), ENC_LEN)
    dk[ENC_LEN : 2 * ENC_LEN, :] = jnp.zeros((ENC_LEN, TILE), F32)
    dv[ENC_LEN : 2 * ENC_LEN, :] = jnp.zeros((ENC_LEN, TILE), F32)
    for index, (part, keys) in enumerate(
        ((pl.ds(0, rows), pl.ds(0, ENC_LEN)), (pl.ds(rows, CONT_LEN), far))
    ):
        q = q_ref[part, :]
        k = k_ref[keys, :]
        kt = k.T
        v = v_ref[keys, :]
        do = do_ref[part, :]
        lse = lse_ref[part, :].T
        gk, gv = (0.0, 0.0)
        dq = []
        for head in range(2):
            mask = head_mask(head, TILE, BF)
            qm = q * mask
            dom = do * mask
            s = mm(k, qm, NT)
            p = jnp.exp(s - lse[HEAD * head : HEAD * head + 1, :])
            dp = mm(v, dom, NT)
            centre = jnp.sum(p * dp, axis=0, keepdims=True)
            low = (p * (dp - centre)).astype(BF)
            gv = gv + mm(p.astype(BF), dom)
            gk = gk + mm(low, qm)
            dq.append(mm(kt[HEAD * head : HEAD * (head + 1), :], low))
        dq_ref[part, :] = (jnp.concatenate(dq, axis=0).T * HEAD ** (-0.5)).astype(BF)
        if index == 0:
            dk[0:ENC_LEN, :] = gk
            dv[0:ENC_LEN, :] = gv
        else:
            dk[keys, :] = dk[keys, :] + gk
            dv[keys, :] = dv[keys, :] + gv
    dk_ref[...] = dk[...].astype(BF)
    dv_ref[...] = dv[...].astype(BF)


def whole(shape):
    return pl.BlockSpec(shape, lambda *_: (0,) * len(shape))


def by_head(shape):
    return pl.BlockSpec((1,) + shape[1:], lambda head, *_: (head,) + (0,) * (len(shape) - 1))


def cost(flops, transcendentals, arrays):
    return pl.CostEstimate(
        flops=int(flops),
        transcendentals=int(transcendentals),
        bytes_accessed=int(sum(a.size * a.dtype.itemsize for a in arrays)),
    )


def shaped(*pairs):
    return [jax.ShapeDtypeStruct(shape, dtype) for shape, dtype in pairs]


MESH = pl.DeviceIdType.MESH


class Links:
    def __init__(self, sends, receives, local, bits):
        self.sends, self.receives, self.local_sems = sends, receives, local
        self.used = 0
        self.used_local = 0
        self.bits = bits
        self.data = lax.axis_index("dp")
        self.tensor = lax.axis_index("tensor")
        self.ranks = lax.axis_size("tensor")

    def bit(self, index):
        return self.data // (1 << index) % 2

    def partner(self, index):
        return (self.data + (1 << index) * (1 - 2 * self.bit(index)), self.tensor)

    def ahead(self, step):
        return (self.data, (self.tensor + step) % self.ranks)

    def across(self, index):
        here = self.tensor // (1 << index) % 2
        return (self.data, self.tensor + (1 << index) * (1 - 2 * here))

    def barrier(self):
        sem = pltpu.get_barrier_semaphore()
        others = [self.partner(index) for index in range(self.bits)]
        others += [self.ahead(step) for step in range(1, self.ranks)]
        for other in others:
            pl.semaphore_signal(sem, inc=1, device_id=other, device_id_type=MESH)
        pl.semaphore_wait(sem, len(others))

    def send(self, source, target, device):
        copy = pltpu.make_async_remote_copy(
            src_ref=source,
            dst_ref=target,
            send_sem=self.sends.at[self.used],
            recv_sem=self.receives.at[self.used],
            device_id=device,
            device_id_type=MESH,
        )
        self.used += 1
        copy.start()
        return copy

    def local(self, source, target):
        copy = pltpu.make_async_copy(source, target, self.local_sems.at[self.used_local])
        self.used_local += 1
        copy.start()
        return copy


def span(start, size, step):
    return pl.ds(pl.multiple_of(start, step), size)


def bit_order(place):
    return (1, 2) if place % 2 == 0 else (2, 1)


def split_chunks(sizes, unit):
    chunks = []
    for index, rows in enumerate(sizes):
        step = rows
        while step > unit:
            step //= 2
        chunks += [(index, start, step) for start in range(0, rows, step)]
    return chunks


def gather_stream(links, own, full, stage, first, rows, place):
    one, two = bit_order(place)
    width = own.shape[1]
    half = width // 2
    cols = span(links.bit(0) * half, half, 128)
    base = first + links.bit(one) * (rows // 2)
    quarter = span(base + links.bit(two) * (rows // 4), rows // 4, 16)
    mine = links.local(own.at[pl.ds(first, rows), :], stage)
    ranks = links.ranks
    copies = [links.send(own.at[quarter, cols], full.at[2, quarter, cols], links.across(1))]
    yield
    mine.wait()
    home = links.local(stage, full.at[0, pl.ds(first, rows), :])
    copies[0].wait()
    near = (links.tensor - flip_rank(links.tensor, (1,)) + ranks) % ranks
    copies = [
        links.send(own.at[quarter, cols], full.at[near, quarter, cols], links.across(0)),
        links.send(
            full.at[2, quarter, cols], full.at[(near + 2) % ranks, quarter, cols], links.across(0)
        ),
    ]
    yield
    for copy in copies:
        copy.wait()
    others = pl.ds(1, ranks - 1)
    part = full.at[others, quarter, cols]
    copy = links.send(part, part, links.partner(two))
    yield
    copy.wait()
    part = full.at[others, span(base, rows // 2, 16), cols]
    copy = links.send(part, part, links.partner(one))
    yield
    copy.wait()
    part = full.at[others, pl.ds(first, rows), cols]
    copy = links.send(part, part, links.partner(0))
    yield
    copy.wait()
    home.wait()


def count_stream(links, count, held, came, final):
    held[0] = count[...]
    for index in range(links.bits):
        copy = links.send(held.at[index], came.at[index], links.partner(index))
        yield
        copy.wait()
        value = held[index] + came[index]
        held[index + 1] = value
    final[...] = value


def attend(ins, far_refs, lent, work, heads):
    line_ref, ok_ref, q_ref, k_ref, v_ref = ins
    o_ref, o_late, lse_ref, lse_late, slab = work
    width = q_ref.shape[1]
    block = 2 * TILE
    for ref in (o_ref, o_late, lse_ref, lse_late):
        ref[...] = jnp.zeros_like(ref)
    for head in range(heads):
        slab[...] = make_slab(line_ref[head])
        mask = head_mask(head, width, BF)
        mask_f = head_mask(head, width, F32)
        for idx in range(PROMPT // block):
            keys = block * (idx + 1)
            rows = pl.ds(idx * block, block)
            s = mm(q_ref[rows, :] * mask, k_ref[0:keys, :], NT)
            start = PROMPT - block * idx
            s = s + jnp.concatenate(
                [slab[:, start : start + keys], slab[:, start - TILE : start - TILE + keys]],
                axis=0,
            )
            top = jnp.max(s, axis=-1, keepdims=True)
            e = jnp.exp(s - top)
            total = jnp.sum(e, axis=-1, keepdims=True)
            o = mm(e.astype(BF), v_ref[0:keys, :] * mask) / total
            o_ref[rows, :] = o_ref[rows, :] + o.astype(BF)
            lse_ref[rows, :] = lse_ref[rows, :] + (top + jnp.log(total)) * mask_f
            yield
        if head == 0:
            for copy in lent:
                copy.wait()
        for pair in range(2):
            keys_ref, values_ref = (k_ref, v_ref) if pair == 0 else far_refs
            slots = [2 * pair, 2 * pair + 1]
            qs = [q_ref[late_rows(slot), :] * mask for slot in slots]
            s = mm(jnp.concatenate(qs, axis=0), keys_ref[0:PROMPT, :], NT)
            s = s + jnp.concatenate([slab[:, 0:PROMPT], slab[:, 0:PROMPT]], axis=0)
            own = jnp.concatenate(
                [
                    mm(q, k_ref[late_rows(slot), :], NT)
                    + slab[:, PROMPT:DIST]
                    + ok_ref[slot][0:1, :]
                    for q, slot in zip(qs, slots)
                ],
                axis=0,
            )
            top = jnp.maximum(
                jnp.max(s, axis=-1, keepdims=True), jnp.max(own, axis=-1, keepdims=True)
            )
            e = jnp.exp(s - top)
            e_own = jnp.exp(own - top)
            total = jnp.sum(e, axis=-1, keepdims=True) + jnp.sum(e_own, axis=-1, keepdims=True)
            o = mm(e.astype(BF), values_ref[0:PROMPT, :] * mask)
            low = e_own.astype(BF)
            o_own = [
                mm(low[CONT_LEN * i : CONT_LEN * (i + 1), :], v_ref[late_rows(slot), :] * mask)
                for i, slot in enumerate(slots)
            ]
            o = (o + jnp.concatenate(o_own, axis=0)) / total
            here = pl.ds(2 * pair * CONT_LEN, 2 * CONT_LEN)
            o_late[here, :] = o_late[here, :] + o.astype(BF)
            lse_late[here, :] = lse_late[here, :] + (top + jnp.log(total)) * mask_f
            yield


def gather_kernel(count, bits, chunks, heads, pace, *refs):
    refs = list(refs)

    def take(number):
        taken, refs[:number] = refs[:number], []
        return taken

    (hot_ref,) = take(1)
    ins = take(5)
    count_ref, enc_in = take(2)
    own = take(count)
    full = take(count)
    k_far, v_far, lse_ref, lse_late, mixed, enc_far, count_out = take(7)
    o_ref, o_late, slab, leave, arrive, held, came = take(7)
    stages, (sends, receives, local) = refs[:-3], refs[-3:]
    links = Links(sends, receives, local, bits)
    links.barrier()
    ranks = links.ranks
    streams = [
        gather_stream(links, own[index], full[index], stages[place], first, rows, place)
        for place, (index, first, rows) in enumerate(chunks)
    ]
    prompt_rows = pl.ds(0, PROMPT)
    lent = [
        links.send(ins[3].at[prompt_rows, :], k_far, links.partner(0)),
        links.send(ins[4].at[prompt_rows, :], v_far, links.partner(0)),
    ]
    swap = links.send(enc_in, enc_far, links.partner(0))
    counter = count_stream(links, count_ref, held, came, count_out)
    pairs = pair_steps(streams, 5)

    def steps():
        for ignored in pairs:
            next(counter, None)
            yield

    comm = steps()
    next(comm)
    work = (o_ref, o_late, lse_ref, lse_late, slab)
    for number, ignored in enumerate(attend(ins, (k_far, v_far), lent, work, heads)):
        if number % pace == pace - 1:
            next(comm)
    share = PROMPT // ranks
    conts = hot_ref.shape[0]
    moved = []
    for step in (2, 1, 3, 0):
        rank = (links.tensor + step) % ranks
        target = leave if step else arrive
        target[step, pl.ds(0, share), :] = o_ref[span(rank * share, share, 16), :]
        late = 0.0
        for i in range(conts):
            late = late + o_late[cont_rows(i), :].astype(F32) * hot_ref[rank, i][0:1, 0:1]
        target[step, pl.ds(share, CONT_LEN), :] = late.astype(BF)
        if step:
            moved.append(
                links.send(leave.at[step], arrive.at[ranks - step], links.ahead(step))
            )
    for ignored in comm:
        pass
    for copy in moved:
        copy.wait()
    cols = o_ref.shape[1]
    for step in range(ranks):
        mixed[:, step * cols : (step + 1) * cols] = arrive[step]
    swap.wait()
    for ignored in counter:
        pass


def gather_all(hot, ins, count, enc, own, bits, heads, pace):
    ranks = lax.axis_size("tensor")
    chunks = split_chunks([a.shape[0] for a in own], 200)
    any_space = pl.BlockSpec(memory_space=pl.ANY)
    vmem = pl.BlockSpec(memory_space=pltpu.VMEM)
    cols = heads * HEAD
    late = hot.shape[0] * CONT_LEN
    rows_own = PROMPT // ranks + CONT_LEN
    copies = len(chunks) * 6 + ranks + 2 + bits
    out = pl.pallas_call(
        functools.partial(gather_kernel, len(own), bits, chunks, heads, pace),
        out_shape=[jax.ShapeDtypeStruct((ranks,) + a.shape, a.dtype) for a in own]
        + shaped(
            ((PROMPT, cols), BF),
            ((PROMPT, cols), BF),
            ((PROMPT, cols), F32),
            ((late, cols), F32),
            ((rows_own, ranks * cols), BF),
            (enc.shape, BF),
            (count.shape, F32),
        ),
        in_specs=[vmem] * (2 + len(ins)) + [any_space] * (1 + len(own)),
        out_specs=[any_space] * len(own) + [vmem] * 5 + [any_space, vmem],
        scratch_shapes=[
            pltpu.VMEM((PROMPT, cols), BF),
            pltpu.VMEM((late, cols), BF),
            pltpu.VMEM((TILE, SLAB), F32),
            pltpu.VMEM((ranks, rows_own, cols), BF),
            pltpu.VMEM((ranks, rows_own, cols), BF),
            pltpu.VMEM((bits + 1,) + count.shape, F32),
            pltpu.VMEM((bits,) + count.shape, F32),
        ]
        + [pltpu.VMEM((rows, own[0].shape[1]), BF) for _, _, rows in chunks]
        + [
            pltpu.SemaphoreType.DMA((copies,)),
            pltpu.SemaphoreType.DMA((copies,)),
            pltpu.SemaphoreType.DMA((2 * len(chunks),)),
        ],
        compiler_params=pltpu.CompilerParams(
            collective_id=1, has_side_effects=True, vmem_limit_bytes=60 * 2**20
        ),
        name="gather_all",
    )(hot, *ins, count, enc, *own)
    return out[: len(own)], out[len(own) :]


CORE_ROOMS = 8
DOORS = 2


class Exits:
    def __init__(self, links, tall, wide):
        self.links = links
        self.rooms = (wide, tall)
        self.copies = ([None] * DOORS, [None] * DOORS)
        self.used = [0, 0]

    def leave(self, total, first, rows, out, turned):
        door = self.used[turned] % DOORS
        self.used[turned] += 1
        if self.copies[turned][door] is not None:
            self.copies[turned][door].wait()
        value = total[pl.ds(first, rows), :].astype(F32)
        if turned:
            room = self.rooms[1].at[door, :, pl.ds(0, rows)]
            target = out.at[:, pl.ds(first, rows)]
            value = value.T
        else:
            room = self.rooms[0].at[door, pl.ds(0, rows), :]
            target = out.at[pl.ds(first, rows), :]
        room[...] = value
        self.copies[turned][door] = self.links.local(room, target)

    def close(self):
        for copies in self.copies:
            for copy in copies:
                if copy is not None:
                    copy.wait()


def flip_rank(rank, bits):
    for bit in bits:
        rank = rank + bit * (1 - 2 * (rank // bit % 2))
    return rank


def pair_steps(streams, stages):
    pairs = [streams[i : i + 2] for i in range(0, len(streams), 2)]
    for step in range(len(pairs) + stages):
        for index in reversed(range(len(pairs))):
            if 0 <= step - index <= stages:
                for stream in pairs[index]:
                    next(stream, None)
        yield


def reduce_stream(
    links, grad, total, core_room, room, first, rows, place, slabs, exits, out, turned
):
    mine, from_one, from_two, from_far, from_more = room
    from_core = core_room.at[pl.ds(0, slabs), pl.ds(0, rows), :]
    one, two = bit_order(place)
    half = grad.shape[2] // 2
    whole_rows = pl.ds(first, rows)
    here = span(links.bit(0) * half, half, 128)
    there = span((1 - links.bit(0)) * half, half, 128)
    kept = links.local(grad.at[:, whole_rows, here], mine)
    copy = links.send(grad.at[:, whole_rows, there], from_core, links.partner(0))
    yield
    kept.wait()
    copy.wait()
    mine[...] = mine[...] + from_core[...]
    base = links.bit(one) * (rows // 2)
    given = (1 - links.bit(one)) * (rows // 2)
    copy = links.send(
        mine.at[:, span(given, rows // 2, 16), :], from_one, links.partner(one)
    )
    yield
    copy.wait()
    keep = span(base, rows // 2, 16)
    mine[:, keep, :] = mine[:, keep, :] + from_one[...]
    given = base + (1 - links.bit(two)) * (rows // 4)
    base_two = base + links.bit(two) * (rows // 4)
    copy = links.send(
        mine.at[:, span(given, rows // 4, 16), :], from_two, links.partner(two)
    )
    yield
    copy.wait()
    keep = span(base_two, rows // 4, 16)
    if slabs > 1:
        mine[:, keep, :] = mine[:, keep, :] + from_two[...]
        slab = [
            (flip_rank(links.tensor, flips) - links.tensor + slabs) % slabs
            for flips in ((), (1,), (2,), (1, 2))
        ]
        copies = [
            links.send(mine.at[slab[1], keep, :], from_far.at[0], links.across(0)),
            links.send(mine.at[slab[3], keep, :], from_far.at[1], links.across(0)),
        ]
        yield
        for copy in copies:
            copy.wait()
        mine[slab[2], keep, :] = mine[slab[2], keep, :] + from_far[1]
        copy = links.send(mine.at[slab[2], keep, :], from_far.at[2], links.across(1))
        yield
        copy.wait()
        value = mine[0, keep, :].astype(F32) + from_far[0].astype(F32)
        value = (value + from_far[2].astype(F32)).astype(BF)
    else:
        value = mine[0, keep, :] + from_two[0]
    quarter = span(first + base_two, rows // 4, 16)
    for index in range(3, links.bits):
        total[quarter, here] = value
        copy = links.send(
            total.at[quarter, here], from_more.at[index - 3], links.partner(index)
        )
        copy.wait()
        value = value + from_more[index - 3]
    total[quarter, here] = value
    copy = links.send(total.at[quarter, here], total.at[quarter, here], links.partner(two))
    yield
    copy.wait()
    part = total.at[span(first + base, rows // 2, 16), here]
    copy = links.send(part, part, links.partner(one))
    yield
    copy.wait()
    part = total.at[whole_rows, here]
    copy = links.send(part, part, links.partner(0))
    yield
    copy.wait()
    exits.leave(total, first, rows, out, turned)


def small_stream(links, held, came, grouped, final):
    tensor_bits = links.ranks.bit_length() - 1
    for index in range(links.bits + tensor_bits):
        device = links.partner(index) if index < links.bits else links.across(index - links.bits)
        copy = links.send(held.at[index], came.at[index], device)
        yield
        copy.wait()
        value = held[index] + came[index]
        held[index + 1] = value
        if index == links.bits - 1:
            grouped[...] = value
    final[...] = value


def rows_stream(links, parts, came, out, rows):
    copy = links.send(
        parts.at[pl.ds(2, 2), rows, :], came.at[pl.ds(0, 2), rows, :], links.across(0)
    )
    yield
    copy.wait()
    parts[1, rows, :] = parts[1, rows, :] + came[1, rows, :]
    copy = links.send(parts.at[1, rows, :], came.at[2, rows, :], links.across(1))
    yield
    copy.wait()
    out[rows, :] = (
        parts[0, rows, :].astype(F32) + came[0, rows, :].astype(F32) + came[2, rows, :].astype(F32)
    )


def rows_streams(links, parts, came, out, pieces):
    size = out.shape[0] // pieces
    active = []
    for piece in range(pieces + 2):
        if piece < pieces:
            active.append(rows_stream(links, parts, came, out, pl.ds(piece * size, size)))
        for stream in reversed(active):
            next(stream, None)
        yield


def encoder_stream(links, enc, from_core, total, came, final):
    count = from_core.shape[0]
    here = [flip_rank(links.tensor, flips) for flips in ((), (1,), (2,), (1, 2))]
    kept = links.local(enc.at[pl.ds(0, count)], total)
    copy = links.send(enc.at[pl.ds(count, count)], from_core, links.partner(0))
    yield
    kept.wait()
    copy.wait()
    total[...] = total[...] + from_core[...]
    copies = [
        links.send(total.at[here[1]], came.at[0], links.across(0)),
        links.send(total.at[here[3]], came.at[1], links.across(0)),
    ]
    yield
    for copy in copies:
        copy.wait()
    total[here[2]] = total[here[2]] + came[1]
    copy = links.send(total.at[here[2]], came.at[2], links.across(1))
    yield
    copy.wait()
    value = total[here[0]].astype(F32) + came[0].astype(F32) + came[2].astype(F32)
    final[here[0]] = value.astype(BF)
    copies = [links.send(final.at[here[0]], final.at[here[0]], links.across(1))]
    yield
    copies[0].wait()
    copies = [
        links.send(final.at[place], final.at[place], links.across(0))
        for place in (here[0], here[2])
    ]
    yield
    for copy in copies:
        copy.wait()


def attend_back(ins, work, heads):
    line_ref, ok_ref, q_ref, k_ref, v_ref, kt_ref, kf_ref, vf_ref, lse_ref, late_ref = ins
    do_ref, do_late, ktf_ref, slab, gslab, dqt, dqc, dk, dv, dkc, dvc, dkf, dvf, held = work
    width = q_ref.shape[1]
    block = 2 * TILE
    for ref in (dk, dv, dkf, dvf, dkc, dvc):
        ref[...] = jnp.zeros_like(ref)
    for head in range(heads):
        slab[...] = make_slab(line_ref[head]).T
        gslab[...] = jnp.zeros_like(gslab)
        mask = head_mask(head, width, BF)
        mine = pl.ds(head * HEAD, HEAD)
        for pair in range(2):
            keys_ref, kt, values_ref = (
                (k_ref, kt_ref, v_ref) if pair == 0 else (kf_ref, ktf_ref, vf_ref)
            )
            gk, gv = (dk, dv) if pair == 0 else (dkf, dvf)
            slots = [2 * pair, 2 * pair + 1]
            qs = [q_ref[late_rows(slot), :] * mask for slot in slots]
            dos = [do_late[slot] * mask for slot in slots]
            q = jnp.concatenate(qs, axis=0)
            do = jnp.concatenate(dos, axis=0)
            lse = row_of(
                jnp.concatenate([late_ref[cont_rows(slot), :] for slot in slots], axis=0), head
            )
            s = mm(keys_ref[0:PROMPT, :], q, NT)
            s = s + jnp.concatenate([slab[0:PROMPT, :], slab[0:PROMPT, :]], axis=1)
            keys_own = [k_ref[late_rows(slot), :] for slot in slots]
            own = jnp.concatenate(
                [
                    mm(keys, qc, NT) + slab[PROMPT:DIST, :] + ok_ref[slot]
                    for keys, qc, slot in zip(keys_own, qs, slots)
                ],
                axis=1,
            )
            p = jnp.exp(s - lse)
            p_own = jnp.exp(own - lse)
            dp = mm(values_ref[0:PROMPT, :], do, NT)
            dp_own = jnp.concatenate(
                [mm(v_ref[late_rows(slot), :], doc, NT) for doc, slot in zip(dos, slots)], axis=1
            )
            centre = jnp.sum(p * dp, axis=0, keepdims=True) + jnp.sum(
                p_own * dp_own, axis=0, keepdims=True
            )
            ds = p * (dp - centre)
            ds_own = p_own * (dp_own - centre)
            low = ds.astype(BF)
            low_own = ds_own.astype(BF)
            p_low = p_own.astype(BF)
            gv[...] = gv[...] + mm(p.astype(BF), do)
            gk[...] = gk[...] + mm(low, q)
            dq = mm(kt[mine, 0:PROMPT], low)
            for i in range(2):
                part = slice(CONT_LEN * i, CONT_LEN * (i + 1))
                spot = 2 * pair + i
                here = pl.ds(spot * CONT_LEN, CONT_LEN)
                dvc[here, :] = dvc[here, :] + mm(p_low[:, part], dos[i])
                dkc[here, :] = dkc[here, :] + mm(low_own[:, part], qs[i])
                head_keys = keys_own[i].T[head * HEAD : (head + 1) * HEAD, :]
                dqc[spot, mine, :] = dq[:, part] + mm(head_keys, low_own[:, part])
                gslab[0:PROMPT, :] = gslab[0:PROMPT, :] + ds[:, part]
                gslab[PROMPT:DIST, :] = gslab[PROMPT:DIST, :] + ds_own[:, part]
            yield
        for idx in range(PROMPT // block):
            keys = block * (idx + 1)
            rows = pl.ds(idx * block, block)
            q = q_ref[rows, :] * mask
            do = do_ref[idx, pl.ds(0, block), :] * mask
            s = mm(k_ref[0:keys, :], q, NT)
            start = PROMPT - block * idx
            s = s + jnp.concatenate(
                [slab[start : start + keys, :], slab[start - TILE : start - TILE + keys, :]],
                axis=1,
            )
            p = jnp.exp(s - row_of(lse_ref[rows, :], head))
            dp = mm(v_ref[0:keys, :], do, NT)
            centre = jnp.sum(p * dp, axis=0, keepdims=True)
            ds = p * (dp - centre)
            low = ds.astype(BF)
            dv[0:keys, :] = dv[0:keys, :] + mm(p.astype(BF), do)
            dk[0:keys, :] = dk[0:keys, :] + mm(low, q)
            dqt[mine, rows] = mm(kt_ref[mine, 0:keys], low)
            gslab[start : start + keys, :] = gslab[start : start + keys, :] + ds[:, 0:TILE]
            gslab[start - TILE : start - TILE + keys, :] = (
                gslab[start - TILE : start - TILE + keys, :] + ds[:, TILE:block]
            )
            yield
        held[0, pl.ds(4 + head, 1), :] = fold_slab(gslab[...].T)


def reduce_kernel(count, bits, chunks, heads, pace, turned, *refs):
    refs = list(refs)

    def take(number):
        taken, refs[:number] = refs[:number], []
        return taken

    (hot_ref,) = take(1)
    ins = take(10)
    n1_ref, unit_ref, wq_ref, wk_ref, wv_ref, small_ref, do_in, enc_in = take(8)
    grads = take(count)
    outs = take(count + 3)
    enc_final, out, grouped, final = take(4)
    do_ref, do_late, ktf, slab, gslab, dqt, dqc, dk, dv, dkc, dvc, dkf, dvf = take(13)
    lent_out, lent_in, dq_all, dk_all, dv_all, parts, came_rows = take(7)
    grads = grads + take(3)
    held, came, enc_core, enc_total, enc_came = take(5)
    totals = take(count + 3)
    tall, wide = take(2)
    core_rooms = take(CORE_ROOMS)
    sends, receives, local = refs[-3:]
    rooms = [refs[5 * i : 5 * i + 5] for i in range(len(chunks))]
    links = Links(sends, receives, local, bits)
    links.barrier()
    ranks = links.ranks
    width = n1_ref.shape[1]
    share = PROMPT // ranks
    own_rows, cols = do_ref.shape[1:]
    moved = []
    for step in (2, 1, 3):
        room = lent_out.at[step // 2, pl.ds(step % 2 * (PROMPT // 2), own_rows), :]
        room[...] = do_in[:, step * cols : (step + 1) * cols]
        moved.append(links.send(room, do_ref.at[links.tensor], links.ahead(step)))
    do_ref[links.tensor] = do_in[:, 0:cols]
    exits = Exits(links, tall, wide)
    streams = [
        reduce_stream(
            links, grads[index], totals[index], core_rooms[place % CORE_ROOMS], rooms[place], first,
            rows, place, grads[index].shape[0], exits, outs[index], turned[index],
        )
        for place, (index, first, rows) in enumerate(chunks)
    ]
    encoder = encoder_stream(links, enc_in, enc_core, enc_total, enc_came, enc_final)
    pairs = pair_steps(streams, 8)

    def steps():
        for ignored in pairs:
            next(encoder, None)
            yield

    comm = steps()
    next(comm)
    next(comm)
    next(comm)
    held[0] = small_ref[...]
    ktf[...] = ins[6][...].T
    for copy in moved:
        copy.wait()
    conts = dqc.shape[0]
    for i in range(conts):
        value = 0.0
        for cont in range(conts):
            late = do_ref[cont, pl.ds(share, CONT_LEN), :].astype(F32)
            value = value + late * hot_ref[cont, i][0:1, 0:1]
        do_late[i] = value.astype(BF)
    work = (do_ref, do_late, ktf, slab, gslab, dqt, dqc, dk, dv, dkc, dvc, dkf, dvf, held)
    for number, ignored in enumerate(attend_back(ins, work, heads)):
        if number % pace == pace - 1:
            next(comm)

    lent_out[0] = dkf[...].astype(BF)
    lent_out[1] = dvf[...].astype(BF)
    lent = links.send(lent_out, lent_in, links.partner(0))
    dq_all[0:PROMPT, :] = (dqt[...].T * HEAD ** (-0.5)).astype(BF)
    for i in range(conts):
        here = late_rows(i)
        spot = cont_rows(i)
        dq_all[here, :] = (dqc[i].T * HEAD ** (-0.5)).astype(BF)
        dk_all[here, :] = dkc[spot, :].astype(BF)
        dv_all[here, :] = dvc[spot, :].astype(BF)
    lent.wait()
    dk_all[0:PROMPT, :] = (dk[...] + lent_in[0].astype(F32)).astype(BF)
    dv_all[0:PROMPT, :] = (dv[...] + lent_in[1].astype(F32)).astype(BF)
    gain = jnp.zeros((1, width), F32)

    def input_grad(rows):
        value = (
            mm(dq_all[rows, :], wq_ref[...])
            + mm(dk_all[rows, :], wk_ref[...])
            + mm(dv_all[rows, :], wv_ref[...])
        )
        return value, jnp.sum(value * unit_ref[rows, :].astype(F32), axis=0, keepdims=True)

    late = []
    for i in range(conts):
        value, term = input_grad(late_rows(i))
        late.append(value)
        gain = gain + term
    for place, flips in ((2, (1,)), (3, (1, 2)), (1, (2,)), (0, ())):
        rank = flip_rank(links.tensor, flips)
        value, term = input_grad(span(rank * share, share, 16))
        gain = gain + term
        parts[place, pl.ds(0, share), :] = value.astype(BF)
        total = 0.0
        for i in range(conts):
            total = total + late[i] * hot_ref[rank, i][0:1, 0:1]
        parts[place, pl.ds(share, CONT_LEN), :] = total.astype(BF)
    held[0, 0:1, 0:width] = gain
    extras = [
        rows_streams(links, parts, came_rows, out, 12),
        small_stream(links, held, came, grouped, final),
    ]
    for stream in extras:
        next(stream)
    for index, whole_ref in enumerate((dq_all, dk_all, dv_all)):
        grads[count + index][0] = mm(whole_ref[...], n1_ref[...], TN).astype(BF)
    for ignored in comm:
        for stream in extras:
            next(stream, None)
    for stream in extras:
        for ignored in stream:
            pass
    exits.close()


def reduce_all(hot, ins, mats, small, do_in, enc, grads, turned, bits, heads, pace):
    ranks = lax.axis_size("tensor")
    width = mats[0].shape[1]
    cols = heads * HEAD
    half = width // 2
    chunks = split_chunks([a.shape[1] for a in grads], 200)
    chunks += [(len(grads) + i, 0, cols) for i in range(3)]
    more = max(bits - 3, 1)
    conts = hot.shape[0]
    late = conts * CONT_LEN
    own = PROMPT // ranks + CONT_LEN
    rooms = []
    for index, _, rows in chunks:
        slabs = grads[index].shape[0] if index < len(grads) else 1
        rooms += [
            pltpu.VMEM((slabs, rows, half), BF),
            pltpu.VMEM((slabs, rows // 2, half), BF),
            pltpu.VMEM((slabs, rows // 4, half), BF),
            pltpu.VMEM((3, rows // 4, half), BF),
            pltpu.VMEM((more, rows // 4, half), BF),
        ]
    small_steps = bits + ranks.bit_length() - 1
    copies = len(chunks) * (9 + bits - 3) + small_steps + ranks + 32
    enc_block = (enc.shape[1], width)
    heights = [a.shape[1] for a in grads] + [cols] * 3
    tallest = max(c[2] for c in chunks)
    turning = max(c[2] for c in chunks if turned[c[0]])
    any_space = pl.BlockSpec(memory_space=pl.ANY)
    vmem = pl.BlockSpec(memory_space=pltpu.VMEM)
    out = pl.pallas_call(
        functools.partial(reduce_kernel, len(grads), bits, chunks, heads, pace, turned),
        out_shape=shaped(
            *[
                ((width, rows) if turn else (rows, width), F32)
                for rows, turn in zip(heights, turned)
            ],
            ((ranks,) + enc_block, BF),
            ((own, width), F32),
            (small.shape, F32),
            (small.shape, F32),
        ),
        in_specs=[vmem] * (len(ins) + len(mats) + 3)
        + [any_space] * (1 + len(grads)),
        out_specs=[any_space] * (len(grads) + 3) + [vmem] * 4,
        scratch_shapes=[
            pltpu.VMEM((ranks, own, cols), BF),
            pltpu.VMEM((conts, CONT_LEN, cols), BF),
            pltpu.VMEM((cols, PROMPT), BF),
            pltpu.VMEM((SLAB, TILE), F32),
            pltpu.VMEM((SLAB, TILE), F32),
            pltpu.VMEM((cols, PROMPT), F32),
            pltpu.VMEM((conts, cols, CONT_LEN), F32),
            pltpu.VMEM((PROMPT, cols), F32),
            pltpu.VMEM((PROMPT, cols), F32),
            pltpu.VMEM((late, cols), F32),
            pltpu.VMEM((late, cols), F32),
            pltpu.VMEM((PROMPT, cols), F32),
            pltpu.VMEM((PROMPT, cols), F32),
            pltpu.VMEM((2, PROMPT, cols), BF),
            pltpu.VMEM((2, PROMPT, cols), BF),
            pltpu.VMEM((PROMPT + late, cols), BF),
            pltpu.VMEM((PROMPT + late, cols), BF),
            pltpu.VMEM((PROMPT + late, cols), BF),
            pltpu.VMEM((ranks, own, width), BF),
            pltpu.VMEM((ranks - 1, own, width), BF),
            pltpu.VMEM((1, cols, width), BF),
            pltpu.VMEM((1, cols, width), BF),
            pltpu.VMEM((1, cols, width), BF),
            pltpu.VMEM((small_steps + 1,) + small.shape, F32),
            pltpu.VMEM((small_steps,) + small.shape, F32),
            pltpu.VMEM((ranks,) + enc_block, BF),
            pltpu.VMEM((ranks,) + enc_block, BF),
            pltpu.VMEM((ranks - 1,) + enc_block, BF),
        ]
        + [pltpu.VMEM((rows, width), BF) for rows in heights]
        + [pltpu.VMEM((DOORS, width, turning), F32), pltpu.VMEM((DOORS, tallest, width), F32)]
        + [pltpu.VMEM((ranks, tallest, half), BF)] * CORE_ROOMS
        + rooms
        + [
            pltpu.SemaphoreType.DMA((copies,)),
            pltpu.SemaphoreType.DMA((copies,)),
            pltpu.SemaphoreType.DMA((2 * len(chunks) + 2,)),
        ],
        compiler_params=pltpu.CompilerParams(
            collective_id=2, has_side_effects=True, vmem_limit_bytes=67043328
        ),
        name="reduce_all",
    )(hot, *ins, *mats, small, do_in, enc, *grads)
    return out[: len(grads) + 3], out[-4], out[-3], out[-2], out[-1]


def run_heads(kernel, heads, scalars, lines, arrays, outs, scratch, out_heads, cells, name):
    in_specs = [by_head(a.shape) for a in lines] + [whole(a.shape) for a in arrays]
    out_specs = [
        by_head(o.shape) if i in out_heads else whole(o.shape) for i, o in enumerate(outs)
    ]
    return pl.pallas_call(
        kernel,
        out_shape=outs,
        grid_spec=pltpu.PrefetchScalarGridSpec(
            num_scalar_prefetch=len(scalars),
            grid=(heads,),
            in_specs=in_specs,
            out_specs=out_specs,
            scratch_shapes=scratch,
        ),
        compiler_params=pltpu.CompilerParams(dimension_semantics=("arbitrary",)),
        cost_estimate=cost(
            cells * heads * 256 * 2 * (2 if not out_heads else 5), cells * heads,
            list(lines) + list(arrays) + list(outs),
        ),
        name=name,
    )(*scalars, *lines, *arrays)


def on_device(
    x_prompt,
    x_cont,
    enc_out,
    cot_prompt,
    cot_cont,
    teacher,
    valid,
    prompt_of,
    buckets,
    gain_self,
    gain_cross,
    gain_ffn,
    rel_table,
    w_q,
    w_k,
    w_v,
    w_o,
    c_q,
    c_k,
    c_v,
    c_o,
    w_gate,
    w_up,
    w_down,
):
    width = x_prompt.shape[1]
    cont_count = prompt_of.shape[0]
    heads = w_q.shape[1] // HEAD
    cols = heads * HEAD
    hidden_here = w_gate.shape[1]
    ranks = lax.axis_size("tensor")
    data_size = lax.axis_size("dp")
    share = PROMPT // ranks
    tensor_rank = lax.axis_index("tensor")
    data_rank = lax.axis_index("dp")
    factor = HEAD ** (-0.5)
    bits = data_size.bit_length() - 1

    far = (prompt_of != data_rank).astype(jnp.int32)
    index = jnp.arange(cont_count, dtype=jnp.int32)
    before = index[None, :] < index[:, None]
    near_rank = jnp.sum(jnp.where(before, 1 - far[None, :], 0), axis=1)
    far_rank = jnp.sum(jnp.where(before, far[None, :], 0), axis=1)
    spot = jnp.where(far == 0, near_rank, cont_count // 2 + far_rank)
    slots = jnp.sum(jnp.where(spot[None, :] == index[:, None], index[None, :], 0), axis=1)
    hot = jnp.broadcast_to(
        (spot[:, None] == index[None, :]).astype(F32)[:, :, None, None],
        (cont_count, cont_count, 8, 128),
    )

    def by_place(rows):
        return jnp.concatenate(
            [
                lax.dynamic_slice_in_dim(rows, slots[i] * CONT_LEN, CONT_LEN, 0)
                for i in range(cont_count)
            ]
        )

    far_here = lax.dynamic_slice_in_dim(far, tensor_rank, 1, 0)

    def own_rows(prompt_rows, conts):
        return jnp.concatenate(
            [
                lax.dynamic_slice_in_dim(prompt_rows, tensor_rank * share, share, 0),
                lax.dynamic_slice_in_dim(conts, tensor_rank * CONT_LEN, CONT_LEN, 0),
            ]
        )

    count = jnp.broadcast_to(jnp.sum(valid.astype(F32)), (8, 128))

    bucket_hot = (buckets[::-1][:, None] == jnp.arange(rel_table.shape[0])[None, :]).astype(F32)
    table = jnp.dot(bucket_hot, rel_table, precision=lax.Precision.HIGHEST).T
    line = jnp.concatenate(
        [table, jnp.full((heads, LINE - DIST), masked_value, F32)], axis=1
    ).reshape(heads, 1, LINE)
    ok = jnp.where(by_place(valid) > 0, 0.0, masked_value).astype(F32)
    ok_rows = jnp.broadcast_to(ok.reshape(cont_count, 1, CONT_LEN), (cont_count, 8, CONT_LEN))
    ok_cols = jnp.broadcast_to(
        ok.reshape(cont_count, CONT_LEN, 1), (cont_count, CONT_LEN, CONT_LEN)
    )

    stream = jnp.concatenate([x_prompt, by_place(x_cont)]).astype(F32)
    n1 = rms_norm(stream, gain_self).astype(BF)
    key_s = mm(n1, w_k).astype(BF)
    value_s = mm(n1, w_v).astype(BF)
    query_s = (mm(n1, w_q).astype(F32) * factor).astype(BF)
    key_t = mm(w_k, n1, (((0,), (1,)), ((), ()))).astype(BF)
    weights, (key_far, value_far, lse_prompt, lse_cont, mixed_self, enc_far, count) = gather_all(
        hot,
        [line, ok_rows, query_s, key_s, value_s],
        count,
        enc_out,
        [w_o, c_q.T, c_k.T, c_v.T, c_o, w_gate.T, w_up.T, w_down],
        bits,
        heads,
        2,
    )
    wo_all, cq_all, ck_all, cv_all, co_all, wg_all, wu_all, wd_all = weights
    token_count = count[0, 0]

    wo_full, cq_t, ck_t, cv_t, co_full = (
        a.reshape(ranks * cols, width) for a in (wo_all, cq_all, ck_all, cv_all, co_all)
    )
    x_own = own_rows(x_prompt, x_cont).astype(F32)
    x1 = x_own + mm(mixed_self, wo_full)
    n2 = rms_norm(x1, gain_cross).astype(BF)
    query_c = (mm(n2, cq_t, NT) * factor).astype(BF)
    enc_pair = jnp.concatenate([enc_out, enc_far])
    key_c = mm(enc_pair, ck_t, NT).astype(BF)
    value_c = mm(enc_pair, cv_t, NT).astype(BF)
    own_count = query_c.shape[0]
    pairs = query_c.shape[1] // TILE

    def columns(rows):
        return pl.BlockSpec((rows, TILE), lambda i, *_: (0, i))

    cross_cells = own_count * ENC_LEN * pairs * 2
    mixed_cross, lse_cross = pl.pallas_call(
        cross_fwd,
        out_shape=shaped(((own_count, pairs * TILE), BF), ((own_count, pairs * TILE), F32)),
        grid_spec=pltpu.PrefetchScalarGridSpec(
            num_scalar_prefetch=1,
            grid=(pairs,),
            in_specs=[columns(own_count), columns(2 * ENC_LEN), columns(2 * ENC_LEN)],
            out_specs=[columns(own_count), columns(own_count)],
        ),
        compiler_params=pltpu.CompilerParams(dimension_semantics=("arbitrary",)),
        cost_estimate=cost(cross_cells * 256 * 2 * 2, cross_cells, [query_c, key_c, value_c]),
        name="cross_fwd",
    )(far_here, query_c, key_c, value_c)
    x2 = x1 + mm(mixed_cross, co_full)
    n3 = rms_norm(x2, gain_ffn).astype(BF)
    wg_t, wu_t, wd = (a.reshape(ranks * hidden_here, width) for a in (wg_all, wu_all, wd_all))
    gate_pre = mm(n3, wg_t, NT)
    upper = mm(n3, wu_t, NT)
    hidden, gelu_pull = jax.vjp(
        lambda first_in, second_in: jax.nn.gelu(first_in, approximate=True) * second_in,
        gate_pre,
        upper,
    )
    hidden = hidden.astype(BF)
    x3 = x2 + mm(hidden, wd)
    valid_own = lax.dynamic_slice_in_dim(valid, tensor_rank * CONT_LEN, CONT_LEN, 0).astype(F32)[
        :, None
    ]
    deviation = x3[share:] - teacher.astype(F32)
    loss_part = jnp.sum(valid_own * deviation * deviation)
    g3 = jnp.concatenate(
        [
            cot_prompt.astype(F32),
            cot_cont.astype(F32) + 2.0 * valid_own * deviation / token_count,
        ]
    )
    y_all = x3.astype(BF)

    g3_low = g3.astype(BF)
    d_hidden = mm(g3_low, wd, NT).astype(BF).astype(F32)
    d_gate, d_upper = gelu_pull(d_hidden)
    d_gate = d_gate.astype(BF)
    d_upper = d_upper.astype(BF)
    ffn_grads = [
        mm(d_gate, n3, TN).astype(BF),
        mm(d_upper, n3, TN).astype(BF),
        mm(hidden, g3_low, TN).astype(BF),
    ]
    d_n3 = mm(d_gate, wg_t) + mm(d_upper, wu_t)
    back3, gain_ffn_part = norm_back(x2, gain_ffn, d_n3)
    g2 = g3 + back3

    g2_low = g2.astype(BF)
    d_mixed_c = mm(g2_low, co_full, NT).astype(BF)
    d_query_c, d_key_c, d_value_c = pl.pallas_call(
        cross_back,
        out_shape=shaped(
            ((own_count, pairs * TILE), BF),
            ((2 * ENC_LEN, pairs * TILE), BF),
            ((2 * ENC_LEN, pairs * TILE), BF),
        ),
        grid_spec=pltpu.PrefetchScalarGridSpec(
            num_scalar_prefetch=1,
            grid=(pairs,),
            in_specs=[
                columns(own_count), columns(2 * ENC_LEN), columns(2 * ENC_LEN),
                columns(own_count), columns(own_count),
            ],
            out_specs=[columns(own_count), columns(2 * ENC_LEN), columns(2 * ENC_LEN)],
            scratch_shapes=[pltpu.VMEM((2 * ENC_LEN, TILE), F32)] * 2,
        ),
        compiler_params=pltpu.CompilerParams(dimension_semantics=("arbitrary",)),
        cost_estimate=cost(cross_cells * 256 * 2 * 5, cross_cells, [query_c, key_c, value_c]),
        name="cross_back",
    )(far_here, query_c, key_c, value_c, d_mixed_c, lse_cross)
    d_n2 = mm(d_query_c, cq_t)
    back2, gain_cross_part = norm_back(x1, gain_cross, d_n2)
    g1 = g2 + back2
    g1_low = g1.astype(BF)

    attn_grads = [
        mm(mixed_self, g1_low, TN).astype(BF),
        mm(d_query_c, n2, TN).astype(BF),
        mm(d_key_c, enc_pair, TN).astype(BF),
        mm(d_value_c, enc_pair, TN).astype(BF),
        mm(mixed_cross, g2_low, TN).astype(BF),
    ]
    d_mixed_s = mm(g1_low, wo_full, NT).astype(BF)
    enc_part = (mm(d_key_c, ck_t) + mm(d_value_c, cv_t)).astype(BF)

    small = jnp.zeros((8, LINE), F32)
    small = small.at[1, :width].set(gain_cross_part).at[2, :width].set(gain_ffn_part)
    small = small.at[3, 0].set(loss_part)
    unit = (stream * norm_scale(stream)).astype(BF)
    totals, enc_sum, d_n1, grouped, small = reduce_all(
        hot,
        [line, ok_cols, query_s, key_s, value_s, key_t, key_far, value_far,
         lse_prompt, lse_cont],
        [n1, unit, w_q.T, w_k.T, w_v.T],
        small,
        d_mixed_s,
        enc_part.reshape(2 * ranks, ENC_LEN // ranks, width),
        [a.reshape(ranks, hidden_here, width) for a in ffn_grads]
        + [a.reshape(ranks, cols, width) for a in attn_grads],
        (True, True) + (False,) * 9,
        bits,
        heads,
        9,
    )
    grad_enc = enc_sum.reshape(ENC_LEN, width).astype(F32)
    grad_table = jnp.dot(
        grouped[4 : 4 + heads, :DIST], bucket_hot, precision=lax.Precision.HIGHEST
    ).T
    back1, ignored = norm_back(x_own, gain_self, d_n1)
    grad_x = g1 + back1
    return (
        y_all[:share],
        y_all[share:],
        grad_x[:share],
        grad_x[share:],
        grad_enc,
        small[0, :width],
        small[1, :width],
        small[2, :width],
        grad_table,
        totals[8].T,
        totals[9].T,
        totals[10].T,
        totals[3],
        totals[4].T,
        totals[5].T,
        totals[6].T,
        totals[7],
        totals[0],
        totals[1],
        totals[2],
        small[3, 0] / token_count,
    )


def solution(mesh):
    rows = P("dp", None)
    both = P(("dp", "tensor"), None)
    columns = P(None, "tensor")
    shards = P("tensor", None)
    return jax.shard_map(
        on_device,
        mesh=mesh,
        in_specs=(
            (rows,) * 3 + (both,) * 3 + (P("dp"),) * 2 + (P(),) * 4 + (columns,) * 4
            + (shards,) + (columns,) * 3 + (shards,) + (columns,) * 2 + (shards,)
        ),
        out_specs=(
            (both,) * 4 + (rows,) + (P(),) * 3 + (columns,) * 4 + (shards,) + (columns,) * 3
            + (shards,) + (columns,) * 2 + (shards, P())
        ),
        check_vma=False,
    )
```
